32 devices in a mesh: dp: 4 (over z), seqhi: 2 (over x), seqlo: 4 (over y, core).
Axes of the slice: x: 2, y: 2, z: 4, core: 2. Of those that a mesh axis runs over, the one named last changes fastest.
Arguments:
- queries: bfloat16 [4, 2048, 384], P('dp', ('seqhi', 'seqlo')), may hold values from -2 to 2
- key_rows: bfloat16 [4, 2048, 384], P('dp', ('seqhi', 'seqlo')), may hold values from -2 to 2
- value_rows: bfloat16 [4, 2048, 384], P('dp', ('seqhi', 'seqlo')), may hold values from -3 to 3
- head_scale: float32 [6], replicated, may hold values from 0.15 to 1
- out_weight: bfloat16 [384, 384], replicated, may hold values from -0.3125 to 0.3125
- cotangent: bfloat16 [4, 2048, 384], P('dp', ('seqhi', 'seqlo')), may hold values from -6 to 6
Outputs:
- queries_gradient: bfloat16 [4, 2048, 384], P('dp', ('seqhi', 'seqlo'))
- keys_gradient: bfloat16 [4, 2048, 384], P('dp', ('seqhi', 'seqlo'))
- values_gradient: bfloat16 [4, 2048, 384], P('dp', ('seqhi', 'seqlo'))
- weight_gradient: float32 [384, 384], P('dp')
The draws below stay inside these ranges and needn't reach their ends.
All inputs are finite; a program needn't handle non-finite values.
Results may differ from the reference program's by a relative error of at most 0.025.
Values may be sent and summed in bfloat16 or wider, within the bound.
No kernel may reach another device: no remote copies, remote signals or barrier semaphores. Data moves between devices by JAX's collectives and lax.ppermute only.
A program may use at most 64 MiB of HBM per device.

```python
import math
import jax
import jax.numpy as jnp
from jax import lax

HEADS = 6
HEAD_DIM = 64
BLOCK = 128
D = 384
TOKENS = 2048
SEQS = 4
N_SEQHI = 2
N_SEQLO = 4


def smooth_part(key, salt):
    base_key = jax.random.fold_in(key, salt)
    array_shape = (SEQS, 1, HEADS * HEAD_DIM)
    low_log = math.log(4.0 * BLOCK)
    high_log = math.log(2.0 * TOKENS)
    position = jnp.arange(TOKENS, dtype=jnp.float32)[None, :, None]
    summed = jnp.zeros((SEQS, TOKENS, HEADS * HEAD_DIM), jnp.float32)
    for component in range(2):
        period = jnp.exp(jax.random.uniform(jax.random.fold_in(base_key, 2 * component), array_shape, jnp.float32, low_log, high_log))
        phase = jax.random.uniform(jax.random.fold_in(base_key, 2 * component + 1), array_shape, jnp.float32, -math.pi, math.pi)
        summed = summed + 0.5 * jnp.sin(2.0 * math.pi * position / period + phase)
    return summed


def rough_part(key, salt):
    noise_values = jax.random.uniform(jax.random.fold_in(key, salt), (SEQS, TOKENS, HEADS * HEAD_DIM), jnp.float32, -1.0, 1.0)
    return noise_values


def draw_queries(key, part):
    return (0.6 * rough_part(key, 1) + 1.4 * smooth_part(key, 7)).astype(jnp.bfloat16)


def draw_key_rows(key, part):
    return (0.6 * rough_part(key, 2) + 1.4 * smooth_part(key, 7)).astype(jnp.bfloat16)


def draw_value_rows(key, part):
    return (1.5 * rough_part(key, 3) + 1.5 * smooth_part(key, 9)).astype(jnp.bfloat16)


def raised(result, key, source, target, parts, factor):
    owner, partner = [(jnp.arange(result.shape[dim]) // (result.shape[dim] // parts)).reshape([-1 if axis == dim else 1 for axis in range(result.ndim)]) for dim in (source, target)]
    chosen = jax.random.permutation(key, parts)[partner]
    strong = (owner == chosen) | (owner == (partner + parts // 2) % parts)
    return jnp.where(strong, factor * result, result)


def levels(stream_key, dims, pieces, smallest, largest):
    def one(dim, shards_of):
        heights = jax.random.uniform(jax.random.fold_in(jax.random.fold_in(stream_key, 6), dim), (shards_of,), jnp.float32, smallest / len(pieces), largest / len(pieces))
        return jnp.repeat(jnp.exp(heights), dims[dim] // shards_of).reshape((-1,) + (1,) * (len(dims) - dim - 1))

    level = one(*pieces[0])
    for cut in pieces[1:]:
        level = level * one(*cut)
    return level


def normal_values(key, dims, scale, most, pieces=(), held_as=jnp.bfloat16):
    gain = levels(key, dims, pieces, -0.22, 0.18) if pieces else 1.0
    drawn = jax.random.normal(key, dims, jnp.float32) * scale * gain
    return jnp.minimum(jnp.maximum(drawn, -most), most).astype(held_as)


def gaussian_with(stream_key, dims, width, bound, shards, heavy, kind=jnp.bfloat16):
    drawn = width * jax.random.normal(stream_key, dims, jnp.float32)
    if shards:
        drawn = drawn * levels(stream_key, dims, shards, -0.22, 0.18)
    return jnp.clip(raised(drawn, jax.random.fold_in(stream_key, 3), *heavy), -bound, bound).astype(kind)


def setup_inputs(seed: int = 0) -> dict:
    seeds = jax.random.split(jax.random.key(seed), 7)
    return {
        "queries": draw_queries(jax.random.fold_in(seeds[6], 71), 0),
        "key_rows": draw_key_rows(jax.random.fold_in(seeds[6], 71), 0),
        "value_rows": draw_value_rows(jax.random.fold_in(seeds[6], 71), 0),
        "head_scale": jnp.clip(jnp.exp(jax.random.uniform(seeds[3], (HEADS,), jnp.float32, math.log(0.15), math.log(1.0))), 0.15, 1.0),
        "out_weight": normal_values(seeds[4], (D, D), D ** -0.5, 0.3125),
        "cotangent": gaussian_with(seeds[5], (SEQS, TOKENS, D), 1.0, 6.0, ((0, 4), (1, 8)), (1, 2, 8, 2.0)),
    }


def split_heads(matrix, head_count):
    return matrix.reshape(matrix.shape[0], head_count, matrix.shape[1] // head_count)

def pair_mean(matrix):
    paired = matrix.astype(jnp.float32).reshape(matrix.shape[0] // 2, 2, matrix.shape[1])
    return (0.5 * (paired[:, 0] + paired[:, 1])).astype(jnp.bfloat16)

def pair_total(matrix):
    paired = matrix.astype(jnp.float32).reshape(matrix.shape[0] // 2, 2, matrix.shape[1])
    return (paired[:, 0] + paired[:, 1]).astype(jnp.bfloat16)

def spread_rows(matrix, factor):
    widened = jnp.broadcast_to(matrix[:, None], (matrix.shape[0], factor) + matrix.shape[1:])
    return widened.reshape((matrix.shape[0] * factor,) + matrix.shape[1:])

def group_sum(matrix, factor):
    return lax.optimization_barrier(jnp.sum(matrix.reshape((matrix.shape[0] // factor, factor) + matrix.shape[1:]), axis=1))

def score_terms(queries, key_block, scales):
    head_count = scales.shape[0]
    factor = scales / jnp.sqrt(jnp.float32(queries.shape[1] // head_count))
    logits = jnp.einsum('rhe,che->hrc', split_heads(queries, head_count).astype(jnp.float32), split_heads(key_block, head_count).astype(jnp.float32))
    return (jnp.exp(logits * factor[:, None, None]), factor)

def attend(queries, key_block, value_block, scales, multiplicity):
    head_count = scales.shape[0]
    weights, factor = score_terms(queries, key_block, scales)
    probabilities = weights.astype(jnp.bfloat16)
    numerator = jnp.einsum('hrc,che->rhe', probabilities.astype(jnp.float32), split_heads(value_block, head_count).astype(jnp.float32))
    numerator = numerator.reshape(queries.shape[0], queries.shape[1])
    denominator = multiplicity * lax.optimization_barrier(jnp.sum(weights, axis=2)).T
    return (numerator, denominator)

def attend_back(queries, key_block, value_block, scales, multiplicity, numer_grad, denom_grad):
    head_count = scales.shape[0]
    weights, factor = score_terms(queries, key_block, scales)
    probabilities = weights.astype(jnp.bfloat16).astype(jnp.float32)
    grad_heads = split_heads(numer_grad, head_count).astype(jnp.float32)
    prob_grad = jnp.einsum('rhe,che->hrc', grad_heads, split_heads(value_block, head_count).astype(jnp.float32))
    logit_grad = (weights * (prob_grad + multiplicity * denom_grad.T[:, :, None]) * factor[:, None, None]).astype(jnp.bfloat16).astype(jnp.float32)
    query_piece = jnp.einsum('hrc,che->rhe', logit_grad, split_heads(key_block, head_count).astype(jnp.float32)).reshape(queries.shape)
    key_piece = jnp.einsum('hrc,rhe->che', logit_grad, split_heads(queries, head_count).astype(jnp.float32)).reshape(key_block.shape)
    value_piece = jnp.einsum('hrc,rhe->che', probabilities, grad_heads).reshape(value_block.shape)
    return (query_piece, key_piece, value_piece)

def flip_blocks(matrix):
    return matrix.reshape((matrix.shape[0] // 2, 2) + matrix.shape[1:])[:, ::-1].reshape(matrix.shape)

def cut_rows(matrix, size):
    return matrix.reshape((matrix.shape[0] // size, size) + matrix.shape[1:])

def one_sequence(triple_in):
    queries, key_rows, value_rows, cotangent, head_scale, out_weight = triple_in
    tokens, feature_width = queries.shape
    head_count = head_scale.shape[0]
    regions = N_SEQHI * N_SEQLO
    per_region = tokens // regions
    top_level = regions.bit_length() - 1
    first_pass = lax.map(lambda triple: attend(triple[0], triple[1], triple[2], head_scale, 1.0), (cut_rows(queries, per_region), cut_rows(key_rows, per_region), cut_rows(value_rows, per_region)))
    numerator = first_pass[0].reshape(tokens, feature_width)
    denominator = first_pass[1].reshape(tokens, head_count)
    level_queries = [queries]
    level_keys = [key_rows]
    level_values = [value_rows]
    for height in range(1, top_level + 1):
        level_queries.append(pair_mean(level_queries[-1]))
        level_keys.append(pair_mean(level_keys[-1]))
        level_values.append(pair_total(level_values[-1]))
        factor = 2 ** height
        level_pass = lax.map(lambda triple: attend(triple[0], triple[1], triple[2], head_scale, float(factor)), (cut_rows(level_queries[height], BLOCK), flip_blocks(cut_rows(level_keys[height], BLOCK)), flip_blocks(cut_rows(level_values[height], BLOCK))))
        numerator = numerator + spread_rows(level_pass[0].reshape(-1, feature_width), factor)
        denominator = denominator + spread_rows(level_pass[1].reshape(-1, head_count), factor)
    attended_heads = split_heads(numerator, head_count) / denominator[:, :, None]
    attended = attended_heads.reshape(tokens, feature_width).astype(jnp.bfloat16)
    weight_term = jnp.dot(attended.T, cotangent, preferred_element_type=jnp.float32)
    backward = jnp.dot(cotangent, out_weight.T, preferred_element_type=jnp.float32).astype(jnp.bfloat16)
    back_heads = split_heads(backward, head_count).astype(jnp.float32)
    numer_grad = (back_heads / denominator[:, :, None]).reshape(tokens, feature_width)
    denom_grad = -lax.optimization_barrier(jnp.sum(back_heads * attended_heads, axis=2)) / denominator
    base_pass = lax.map(lambda sextet: attend_back(sextet[0], sextet[1], sextet[2], head_scale, 1.0, sextet[3], sextet[4]), (cut_rows(queries, per_region), cut_rows(key_rows, per_region), cut_rows(value_rows, per_region), cut_rows(numer_grad.astype(jnp.bfloat16), per_region), cut_rows(denom_grad, per_region)))
    query_grads = [base_pass[0].reshape(tokens, feature_width)]
    key_grads = [base_pass[1].reshape(tokens, feature_width)]
    value_grads = [base_pass[2].reshape(tokens, feature_width)]
    for height in range(1, top_level + 1):
        factor = 2 ** height
        coarse_numer = group_sum(numer_grad, factor).astype(jnp.bfloat16)
        coarse_denom = group_sum(denom_grad, factor)
        level_pass = lax.map(lambda sextet: attend_back(sextet[0], sextet[1], sextet[2], head_scale, float(factor), sextet[3], sextet[4]), (cut_rows(level_queries[height], BLOCK), flip_blocks(cut_rows(level_keys[height], BLOCK)), flip_blocks(cut_rows(level_values[height], BLOCK)), cut_rows(coarse_numer, BLOCK), cut_rows(coarse_denom, BLOCK)))
        query_grads.append(level_pass[0].reshape(-1, feature_width))
        key_grads.append(flip_blocks(level_pass[1]).reshape(-1, feature_width))
        value_grads.append(flip_blocks(level_pass[2]).reshape(-1, feature_width))
    chain_query = query_grads[top_level]
    chain_key = key_grads[top_level]
    chain_value = value_grads[top_level]
    for height in range(top_level - 1, -1, -1):
        chain_query = query_grads[height] + spread_rows(0.5 * chain_query, 2)
        chain_key = key_grads[height] + spread_rows(0.5 * chain_key, 2)
        chain_value = value_grads[height] + spread_rows(chain_value, 2)
    return (chain_query.astype(jnp.bfloat16), chain_key.astype(jnp.bfloat16), chain_value.astype(jnp.bfloat16), weight_term)

def reference(queries, key_rows, value_rows, head_scale, out_weight, cotangent):
    sequences = queries.shape[0]
    scales_all = jnp.broadcast_to(head_scale[None], (sequences,) + head_scale.shape)
    weights_all = jnp.broadcast_to(out_weight[None], (sequences,) + out_weight.shape)
    results = lax.map(one_sequence, (queries, key_rows, value_rows, cotangent, scales_all, weights_all))
    return (results[0], results[1], results[2], lax.optimization_barrier(jnp.sum(results[3], axis=0)))
```

```python
import functools
import math

import jax
import jax.numpy as jnp
from jax import lax
from jax.experimental import pallas as pl
from jax.experimental.pallas import tpu as pltpu
from jax.sharding import PartitionSpec as P

BF = jnp.bfloat16
F32 = jnp.float32
SEQ = ("seqhi", "seqlo")
LANES = 128
HALF = 64
LOG2E = math.log2(math.e)
NN = (((1,), (0,)), ((), ()))
NT = (((1,), (1,)), ((), ()))
TN = (((0,), (0,)), ((), ()))


def dot(left, right, dims=NN):
    return lax.dot_general(left, right, dims, preferred_element_type=F32)


def iota(shape, dim):
    return lax.broadcasted_iota(jnp.int32, shape, dim)


def order_matrix(rows, top, inverse=False):
    source = iota((rows, rows), 0 if inverse else 1)
    place = source >> top
    for bit in range(top):
        place = place + ((source >> bit) & 1) * (rows >> (bit + 1))
    return jnp.where(place == iota((rows, rows), 1 if inverse else 0), 1.0, 0.0).astype(BF)


def side_masks():
    lane = iota((1, LANES), 1)
    low = jnp.where(lane < HALF, 1.0, 0.0)
    return low.astype(BF), (1.0 - low).astype(BF)


def side_factor(scale_ref, pair):
    lane = iota((1, LANES), 1)
    return jnp.where(lane < HALF, scale_ref[2 * pair], scale_ref[2 * pair + 1]) * (HALF**-0.5)


def exponent(scale_ref, head):
    return scale_ref[head] * (HALF**-0.5 * LOG2E)


def stack(parts, axis):
    return parts[0] if len(parts) == 1 else jnp.concatenate(parts, axis=axis)


def doubled(value):
    return jnp.concatenate([value, value], axis=0)


def halves_sum(value):
    half = value.shape[0] // 2
    return value[:half] + value[half:]


def lane_pair(offset, pair):
    return slice(offset + LANES * pair, offset + LANES * (pair + 1))


def denom_slot(pair, side, amount, rows):
    lane = iota((1, LANES), 1)
    slot = lane - side * HALF
    hit = (slot == 16 * pair) | (slot == 16 * pair + 8)
    row = jnp.where(hit, float(amount), 0.0)
    return jnp.broadcast_to(row, (rows, LANES)).astype(BF)


def denom_lanes(denoms):
    lane = iota((1, LANES), 1)
    slot = (lane % HALF) // 8
    packed = jnp.zeros(denoms[0].shape, F32)
    for pair, value in enumerate(denoms):
        high = value.astype(BF).astype(F32)
        packed = jnp.where(slot == 2 * pair, high, packed)
        packed = jnp.where(slot == 2 * pair + 1, value - high, packed)
    return packed.astype(BF)


def pool_kernel(top, q_ref, k_ref, v_ref, *level_refs):
    rows, width = q_ref.shape
    order = order_matrix(rows, top)
    for which, ref in enumerate((q_ref, k_ref, v_ref)):
        current = dot(order, ref[...])
        columns = slice(which * width, (which + 1) * width)
        level_refs[0][:, columns] = current.astype(BF)
        for height in range(1, top + 1):
            total = halves_sum(current)
            rounded = (total if which == 2 else 0.5 * total).astype(BF)
            level_refs[height][:, columns] = rounded
            current = rounded.astype(F32)


def attend(scale_ref, pair, queries, keys, values, amount, low, high):
    weights = []
    for side, mask in enumerate((low, high)):
        logits = dot(queries * mask, keys, NT)
        weights.append(jnp.exp2(logits * exponent(scale_ref, 2 * pair + side)).astype(BF))
    count = jnp.full(values.shape, float(amount), BF)
    right = stack([stack([values * mask, count * mask], 1) for mask in (low, high)], 0)
    return dot(stack(weights, 1), right)


def base_kernel(top, scale_ref, x_ref, cot_ref, w_ref, numer_ref, denom_ref, cotp_ref, back_ref):
    rows, width = cot_ref.shape
    low, high = side_masks()
    for pair in range(width // LANES):
        q, k, v = (x_ref[:, lane_pair(width * which, pair)] for which in range(3))
        both = attend(scale_ref, pair, q, k, v, 1, low, high)
        numer_ref[:, lane_pair(0, pair)] = both[:, :LANES]
        denom_ref[:, lane_pair(0, pair)] = both[:, LANES:]
    cotan = dot(order_matrix(rows, top), cot_ref[...]).astype(BF)
    cotp_ref[...] = cotan
    back_ref[...] = dot(cotan, w_ref[...], NT).astype(BF)


def forward_kernel(top, counts, parts, scale_ref, place_ref, numer_ref, denom_ref, cotp_ref, back_ref, *refs):
    own, refs = refs[:top], refs[top:]
    siblings = []
    for count in counts:
        siblings.append(refs[:count])
        refs = refs[count:]
    grads, refs = refs[: top + 1], refs[top + 1 :]
    pieces, (weight_ref,) = refs[:parts], refs[parts:]
    width = numer_ref.shape[1]
    low, high = side_masks()
    lane = iota((LANES, LANES), 1)
    ones = jnp.where(lane // HALF == iota((LANES, LANES), 0) // HALF, 1.0, 0.0).astype(BF)
    adder = doubled(ones)
    grad_rows = []
    denom_rows = []
    attended = []
    for pair in range(width // LANES):
        total = None
        for height in range(top, 0, -1):
            keys, values = (
                stack([ref[:, lane_pair(width * which, pair)] for ref in siblings[height - 1]], 0)
                for which in (1, 2)
            )
            queries = own[height - 1][:, lane_pair(0, pair)]
            both = attend(scale_ref, pair, queries, keys, values, 2**height, low, high)
            total = both if total is None else both + doubled(total)
        total = doubled(total)
        numer = numer_ref[:, lane_pair(0, pair)] + total[:, :LANES]
        inverse = 1.0 / (denom_ref[:, lane_pair(0, pair)] + total[:, LANES:])
        ratio = numer * inverse
        attended.append(ratio.astype(BF))
        back = back_ref[:, lane_pair(0, pair)].astype(F32)
        product = back * ratio
        product_high = product.astype(BF)
        product_low = (product - product_high.astype(F32)).astype(BF)
        summed = dot(stack([product_high, product_low], 1), adder)
        grad_rows.append(back * inverse)
        denom_rows.append(-summed * inverse)
    weight_ref[...] = dot(stack(attended, 1), cotp_ref[...], TN)
    own_rows = width // parts
    for step in range(parts):
        start = lax.rem(place_ref[0] + step, parts) * own_rows
        piece = weight_ref[pl.ds(pl.multiple_of(start, 16), own_rows), :]
        pieces[step][...] = piece.astype(BF)
    for height in range(top + 1):
        if height:
            grad_rows = [halves_sum(value) for value in grad_rows]
            denom_rows = [halves_sum(value) for value in denom_rows]
        for pair, value in enumerate(grad_rows):
            grads[height][:, lane_pair(0, pair)] = value.astype(BF)
        grads[height][:, width:] = denom_lanes(denom_rows)


def slopes(scale_ref, pair, first, second, left, right, low, high):
    weights, slope = [], []
    for side, mask in enumerate((low, high)):
        logits = dot(first * mask, second, NT)
        weight = jnp.exp2(logits * exponent(scale_ref, 2 * pair + side))
        weights.append(weight.astype(BF))
        slope.append((weight * dot(left[side], right[side], NT)).astype(BF))
    return weights, slope


def masked_stack(value, low, high):
    return stack([value * low, value * high], 0)


def query_kernel(top, counts, scale_ref, x_ref, gh_ref, *refs):
    own, refs = refs[:top], refs[top:]
    own_grads, refs = refs[:top], refs[top:]
    siblings = []
    for count in counts:
        siblings.append(refs[:count])
        refs = refs[count:]
    out_ref, base_key_ref, base_value_ref = refs
    rows, width = out_ref.shape
    low, high = side_masks()
    results = []
    for pair in range(width // LANES):
        factor = side_factor(scale_ref, pair)
        total = None
        for height in range(top, -1, -1):
            if height:
                queries = own[height - 1][:, lane_pair(0, pair)]
                keys, values = (
                    stack([ref[:, lane_pair(width * which, pair)] for ref in siblings[height - 1]], 0)
                    for which in (1, 2)
                )
                grad_ref = own_grads[height - 1]
            else:
                queries, keys, values = (x_ref[:, lane_pair(width * which, pair)] for which in range(3))
                grad_ref = gh_ref
            grad = grad_ref[:, lane_pair(0, pair)]
            denom = grad_ref[:, width:]
            left = [stack([grad * mask, denom], 1) for mask in (low, high)]
            right = [
                stack([values, denom_slot(pair, side, 2**height, values.shape[0])], 1) for side in (0, 1)
            ]
            weights, slope = slopes(scale_ref, pair, queries, keys, left, right, low, high)
            piece = dot(stack(slope, 1), masked_stack(keys, low, high)) * factor
            total = piece if total is None else piece + 0.5 * doubled(total)
            if not height:
                key_piece = dot(stack(slope, 0), masked_stack(queries, low, high), TN)
                value_piece = dot(stack(weights, 0), masked_stack(grad, low, high), TN)
                base_key_ref[:, lane_pair(0, pair)] = key_piece * factor
                base_value_ref[:, lane_pair(0, pair)] = value_piece
        results.append(total.astype(BF))
    out_ref[...] = dot(order_matrix(rows, top, True), stack(results, 1)).astype(BF)


def key_kernel(top, counts, scale_ref, base_key_ref, base_value_ref, *refs):
    own, refs = refs[:top], refs[top:]
    siblings = []
    for count in counts:
        siblings.append(refs[:count])
        refs = refs[count:]
    sibling_grads = []
    for count in counts:
        sibling_grads.append(refs[:count])
        refs = refs[count:]
    key_out_ref, value_out_ref = refs
    rows, width = key_out_ref.shape
    low, high = side_masks()
    key_results, value_results = [], []
    for pair in range(width // LANES):
        factor = side_factor(scale_ref, pair)
        key_total = value_total = None
        for height in range(top, 0, -1):
            keys, values = (own[height - 1][:, lane_pair(width * which, pair)] for which in (1, 2))
            queries = stack([ref[:, lane_pair(0, pair)] for ref in siblings[height - 1]], 0)
            grad = stack([ref[:, lane_pair(0, pair)] for ref in sibling_grads[height - 1]], 0)
            denom = stack([ref[:, width:] for ref in sibling_grads[height - 1]], 0)
            left = [
                stack([values * mask, denom_slot(pair, side, 2**height, values.shape[0])], 1)
                for side, mask in enumerate((low, high))
            ]
            right = [stack([grad, denom], 1)] * 2
            weights, slope = slopes(scale_ref, pair, keys, queries, left, right, low, high)
            key_piece = dot(stack(slope, 1), masked_stack(queries, low, high)) * factor
            value_piece = dot(stack(weights, 1), masked_stack(grad, low, high))
            if key_total is not None:
                key_piece = key_piece + 0.5 * doubled(key_total)
                value_piece = value_piece + doubled(value_total)
            key_total, value_total = key_piece, value_piece
        key_total = base_key_ref[:, lane_pair(0, pair)] + 0.5 * doubled(key_total)
        value_total = base_value_ref[:, lane_pair(0, pair)] + doubled(value_total)
        key_results.append(key_total.astype(BF))
        value_results.append(value_total.astype(BF))
    back = order_matrix(rows, top, True)
    key_out_ref[...] = dot(back, stack(key_results, 1)).astype(BF)
    value_out_ref[...] = dot(back, stack(value_results, 1)).astype(BF)


VMEM = pl.BlockSpec(memory_space=pltpu.VMEM)
SMEM = pl.BlockSpec(memory_space=pltpu.SMEM)


def call(kernel, name, shapes, scalars, arrays, scratch=()):
    return pl.pallas_call(
        kernel,
        out_shape=[jax.ShapeDtypeStruct(shape, kind) for shape, kind in shapes],
        in_specs=[SMEM] * len(scalars) + [VMEM] * len(arrays),
        out_specs=[VMEM] * len(shapes),
        scratch_shapes=list(scratch),
        compiler_params=pltpu.CompilerParams(vmem_limit_bytes=48 * 2**20),
        name=name,
    )(*scalars, *arrays)


def traded(value, mask):
    return lax.ppermute(value, SEQ, [(source, source ^ mask) for source in range(lax.axis_size(SEQ))])


def from_siblings(levels, top):
    arrived = {}
    for offset in range(1, 2**top):
        height = offset.bit_length()
        if offset == 1:
            arrived[1] = traded(levels[1], 1)
        elif offset % 2 == 0:
            arrived[offset] = traded(levels[height], offset)
        else:
            arrived[offset] = traded(arrived[offset - 1], 1)
    grouped = []
    for height in range(1, top + 1):
        parts = [arrived[offset] for offset in range(2 ** (height - 1), 2**height)]
        if parts[0].shape[0] < 16:
            parts = [jnp.concatenate(parts, axis=0)]
        grouped.append(parts)
    return grouped


def flat(groups):
    return [part for group in groups for part in group]


def shards(queries, key_rows, value_rows, head_scale, out_weight, cotangent):
    rows, width = queries.shape[1:]
    top = lax.axis_size(SEQ).bit_length() - 1
    parts = lax.axis_size("dp")
    assert width == HALF * head_scale.shape[0] and width % LANES == 0 and width <= 4 * LANES
    whole = (rows, width)
    levels = call(
        functools.partial(pool_kernel, top),
        "pool",
        [((rows >> height, 3 * width), BF) for height in range(top + 1)],
        [],
        [queries[0], key_rows[0], value_rows[0]],
    )
    siblings = from_siblings(levels, top)
    counts = [len(group) for group in siblings]
    numer, denom, cotan, back = call(
        functools.partial(base_kernel, top),
        "base",
        [(whole, F32), (whole, F32), (whole, BF), (whole, BF)],
        [head_scale],
        [levels[0], cotangent[0], out_weight],
    )
    place = lax.axis_index("dp").astype(jnp.int32).reshape(1)
    outs = call(
        functools.partial(forward_kernel, top, counts, parts),
        "forward",
        [((rows >> height, width + LANES), BF) for height in range(top + 1)]
        + [((width // parts, width), BF)] * parts,
        [head_scale, place],
        [numer, denom, cotan, back, *levels[1:], *flat(siblings)],
        [pltpu.VMEM((width, width), F32)],
    )
    grads, pieces = outs[: top + 1], outs[top + 1 :]
    weight = pieces[0].astype(F32)
    for step in range(1, parts):
        weight = weight + lax.ppermute(
            pieces[step], "dp", [(source, (source + step) % parts) for source in range(parts)]
        ).astype(F32)
    weight = weight.astype(BF)
    sibling_grads = from_siblings(grads, top)
    query_grad, base_key, base_value = call(
        functools.partial(query_kernel, top, counts),
        "query",
        [(whole, BF), (whole, F32), (whole, F32)],
        [head_scale],
        [levels[0], grads[0], *levels[1:], *grads[1:], *flat(siblings)],
    )
    key_grad, value_grad = call(
        functools.partial(key_kernel, top, counts),
        "key",
        [(whole, BF), (whole, BF)],
        [head_scale],
        [base_key, base_value, *levels[1:], *flat(siblings), *flat(sibling_grads)],
    )
    bit = 1
    while bit < top:
        group = [weight]
        for mask in range(1, 2 ** min(2, top - bit)):
            group.append(traded(weight, mask << bit))
        last = bit + 2 >= top
        if last:
            group = group + [traded(value, 1) for value in group]
        weight = sum(value.astype(F32) for value in group)
        if not last:
            weight = weight.astype(BF)
        bit += 2
    if top < 2:
        weight = weight.astype(F32)
        if top == 1:
            weight = weight + traded(weight, 1)
    return query_grad[None], key_grad[None], value_grad[None], weight


def solution(mesh):
    spread = P("dp", SEQ, None)
    return jax.shard_map(
        shards,
        mesh=mesh,
        in_specs=(spread, spread, spread, P(), P(), spread),
        out_specs=(spread, spread, spread, P("dp", None)),
        check_vma=False,
    )
```

```python
import functools
import math

import jax
import jax.numpy as jnp
from jax import lax
from jax.experimental import pallas as pl
from jax.experimental.pallas import tpu as pltpu
from jax.sharding import PartitionSpec as P

BF = jnp.bfloat16
F32 = jnp.float32
SEQ = ("seqhi", "seqlo")
LANES = 128
HALF = 64
LOG2E = math.log2(math.e)
NN = (((1,), (0,)), ((), ()))
NT = (((1,), (1,)), ((), ()))
TN = (((0,), (0,)), ((), ()))


def dot(left, right, dims=NN):
    return lax.dot_general(left, right, dims, preferred_element_type=F32)


def iota(shape, dim):
    return lax.broadcasted_iota(jnp.int32, shape, dim)


def order_matrix(rows, top, inverse=False):
    source = iota((rows, rows), 0 if inverse else 1)
    place = source >> top
    for bit in range(top):
        place = place + ((source >> bit) & 1) * (rows >> (bit + 1))
    return jnp.where(place == iota((rows, rows), 1 if inverse else 0), 1.0, 0.0).astype(BF)


def side_masks():
    lane = iota((1, LANES), 1)
    low = jnp.where(lane < HALF, 1.0, 0.0)
    return low.astype(BF), (1.0 - low).astype(BF)


def factor_rows(heads):
    return -(-(heads + heads // 2) // 8) * 8


def fill_factors(scale_ref, factor_ref):
    heads = scale_ref.shape[0]
    lane = iota((1, LANES), 1)
    for head in range(heads):
        factor_ref[head : head + 1, :] = jnp.full((1, LANES), scale_ref[head] * (HALF**-0.5 * LOG2E), F32)
    for pair in range(heads // 2):
        both = jnp.where(lane < HALF, scale_ref[2 * pair], scale_ref[2 * pair + 1]) * (HALF**-0.5)
        factor_ref[heads + pair : heads + pair + 1, :] = both


def exponent(factor_ref, head, columns):
    return stack([factor_ref[head : head + 1, :]] * (columns // LANES), 1)


def side_factor(factor_ref, heads, pair):
    return factor_ref[heads + pair : heads + pair + 1, :]


def stack(parts, axis):
    return parts[0] if len(parts) == 1 else jnp.concatenate(parts, axis=axis)


def doubled(value):
    return jnp.concatenate([value, value], axis=0)


def halves_sum(value):
    half = value.shape[0] // 2
    return value[:half] + value[half:]


def lane_pair(offset, pair):
    return slice(offset + LANES * pair, offset + LANES * (pair + 1))


def denom_slot(pair, side, amount, rows):
    lane = iota((1, LANES), 1)
    slot = lane - side * HALF
    hit = (slot == 16 * pair) | (slot == 16 * pair + 8)
    row = jnp.where(hit, float(amount), 0.0)
    return jnp.broadcast_to(row, (rows, LANES)).astype(BF)


def denom_lanes(denoms):
    lane = iota((1, LANES), 1)
    slot = (lane % HALF) // 8
    packed = jnp.zeros(denoms[0].shape, F32)
    for pair, value in enumerate(denoms):
        high = value.astype(BF).astype(F32)
        packed = jnp.where(slot == 2 * pair, high, packed)
        packed = jnp.where(slot == 2 * pair + 1, value - high, packed)
    return packed.astype(BF)


class View:
    def __init__(self, array, start=0, rows=None):
        self.array = array
        self.start = start
        self.rows = array.shape[0] - start if rows is None else rows


VMEM = pl.BlockSpec(memory_space=pltpu.VMEM)
SMEM = pl.BlockSpec(memory_space=pltpu.SMEM)
HBM = pl.BlockSpec(memory_space=pltpu.HBM)


def call(kernel, name, shapes, arrays, views=(), scalars=(), flops=0, scratch=(), specs=None):
    unique, where = [], []
    for group in views:
        places = []
        for view in group:
            spot = next((at for at, array in enumerate(unique) if array is view.array), None)
            if spot is None:
                spot = len(unique)
                unique.append(view.array)
            places.append((spot, view.start, view.rows))
        where.append(places)

    def body(*refs):
        scalar_refs, refs = refs[: len(scalars)], refs[len(scalars) :]
        array_refs, refs = refs[: len(arrays)], refs[len(arrays) :]
        view_refs, refs = refs[: len(unique)], refs[len(unique) :]

        def load(group, columns):
            return stack(
                [view_refs[spot][start : start + rows, columns] for spot, start, rows in where[group]], 0
            )

        kernel(load, *scalar_refs, *array_refs, *refs)

    moved = sum(math.prod(shape) * jnp.dtype(kind).itemsize for shape, kind in shapes)
    return pl.pallas_call(
        body,
        out_shape=[jax.ShapeDtypeStruct(shape, kind) for shape, kind in shapes],
        in_specs=[SMEM] * len(scalars) + (specs or [VMEM] * len(arrays)) + [VMEM] * len(unique),
        out_specs=[VMEM] * len(shapes),
        scratch_shapes=list(scratch),
        compiler_params=pltpu.CompilerParams(vmem_limit_bytes=48 * 2**20),
        cost_estimate=pl.CostEstimate(flops=flops, transcendentals=0, bytes_accessed=moved),
        name=name,
    )(*scalars, *arrays, *unique)


def pool_kernel(top, places, load, q_hbm, k_hbm, v_hbm, scale_hbm, factor_ref, *refs):
    level_refs, (q_ref, k_ref, v_ref, scale_ref, sems) = refs[:-5], refs[-5:]
    copies = [
        pltpu.make_async_copy(source, target, sems.at[index])
        for index, (source, target) in enumerate(
            ((q_hbm, q_ref), (k_hbm, k_ref), (v_hbm, v_ref), (scale_hbm, scale_ref))
        )
    ]
    for copy in copies:
        copy.start()
    rows, width = q_ref.shape
    order = order_matrix(rows, top)
    for which, ref in enumerate((q_ref, k_ref, v_ref)):
        copies[which].wait()
        current = dot(order, ref[...])
        columns = slice(which * width, (which + 1) * width)
        level_refs[0][:, columns] = current.astype(BF)
        for height in range(1, top + 1):
            total = halves_sum(current)
            rounded = (total if which == 2 else 0.5 * total).astype(BF)
            target, start = places[height - 1]
            level_refs[target][start : start + rounded.shape[0], columns] = rounded
            current = rounded.astype(F32)
    copies[3].wait()
    fill_factors(scale_ref, factor_ref)


def attend(factor_ref, pair, queries, keys, values, amount, low, high):
    weights = []
    for side, mask in enumerate((low, high)):
        logits = dot(queries * mask, keys, NT)
        weights.append(jnp.exp2(logits * exponent(factor_ref, 2 * pair + side, keys.shape[0])).astype(BF))
    count = jnp.full(values.shape, float(amount), BF)
    right = stack([stack([values * mask, count * mask], 1) for mask in (low, high)], 0)
    return dot(stack(weights, 1), right)


def base_kernel(top, load, factor_ref, x_ref, cot_ref, w_ref, numer_ref, denom_ref, cotp_ref, back_ref):
    rows, width = cot_ref.shape
    low, high = side_masks()
    for pair in range(width // LANES):
        q, k, v = (x_ref[:, lane_pair(width * which, pair)] for which in range(3))
        both = attend(factor_ref, pair, q, k, v, 1, low, high)
        numer_ref[:, lane_pair(0, pair)] = both[:, :LANES]
        denom_ref[:, lane_pair(0, pair)] = both[:, LANES:]
    cotan = dot(order_matrix(rows, top), cot_ref[...]).astype(BF)
    cotp_ref[...] = cotan
    back_ref[...] = dot(cotan, w_ref[...], NT).astype(BF)


def packed_rows(own_rows, width):
    return own_rows * width // (width + LANES)


def pack(piece):
    own_rows, width = piece.shape
    rows = packed_rows(own_rows, width)
    tail = stack([piece[rows:, lane_pair(0, block)] for block in range(width // LANES)], 0)
    return stack([piece[:rows], tail], 1)


def unpack_into(packed, out_ref):
    own_rows, width = out_ref.shape
    rows = packed.shape[0]
    out_ref[:rows, :] = packed[:, :width]
    extra = own_rows - rows
    for block in range(width // LANES):
        out_ref[rows:, lane_pair(0, block)] = packed[block * extra : (block + 1) * extra, width:]


def forward_kernel(
    top, parts, packed, grad_places, piece_places,
    load, place_ref, factor_ref, numer_ref, denom_ref, cotp_ref, back_ref, *refs
):
    out_refs, weight_ref = refs[:-1], refs[-1]
    rows, width = numer_ref.shape
    low, high = side_masks()
    lane = iota((LANES, LANES), 1)
    ones = jnp.where(lane // HALF == iota((LANES, LANES), 0) // HALF, 1.0, 0.0).astype(BF)
    adder = doubled(ones)
    grad_rows = []
    denom_rows = []
    attended = []
    for pair in range(width // LANES):
        total = None
        for height in range(top, 0, -1):
            keys, values = (load(top + height - 1, lane_pair(width * which, pair)) for which in (1, 2))
            queries = load(height - 1, lane_pair(0, pair))
            both = attend(factor_ref, pair, queries, keys, values, 2**height, low, high)
            total = both if total is None else both + doubled(total)
        total = doubled(total)
        numer = numer_ref[:, lane_pair(0, pair)] + total[:, :LANES]
        inverse = 1.0 / (denom_ref[:, lane_pair(0, pair)] + total[:, LANES:])
        ratio = numer * inverse
        attended.append(ratio.astype(BF))
        back = back_ref[:, lane_pair(0, pair)].astype(F32)
        product = back * ratio
        product_high = product.astype(BF)
        product_low = (product - product_high.astype(F32)).astype(BF)
        summed = dot(stack([product_high, product_low], 1), adder)
        grad_rows.append(back * inverse)
        denom_rows.append(-summed * inverse)
    weight_ref[...] = dot(stack(attended, 1), cotp_ref[...], TN)
    own_rows = width // parts
    for step, (target, start) in enumerate(piece_places):
        first = pl.multiple_of(place_ref[step] * own_rows, math.gcd(own_rows, 8))
        piece = weight_ref[pl.ds(first, own_rows), :]
        if packed:
            piece = pack(piece)
        out_refs[target][start : start + piece.shape[0], :] = piece.astype(BF)
    for height, (target, start) in enumerate(grad_places):
        if height:
            grad_rows = [halves_sum(value) for value in grad_rows]
            denom_rows = [halves_sum(value) for value in denom_rows]
        span = slice(start, start + (rows >> height))
        for pair, value in enumerate(grad_rows):
            out_refs[target][span, lane_pair(0, pair)] = value.astype(BF)
        out_refs[target][span, width:] = denom_lanes(denom_rows)


def slopes(factor_ref, pair, first, second, left, right, low, high):
    weights, slope = [], []
    for side, mask in enumerate((low, high)):
        logits = dot(first * mask, second, NT)
        weight = jnp.exp2(logits * exponent(factor_ref, 2 * pair + side, second.shape[0]))
        weights.append(weight.astype(BF))
        slope.append((weight * dot(left[side], right[side], NT)).astype(BF))
    return weights, slope


def masked_stack(value, low, high):
    return stack([value * low, value * high], 0)


def slope_sides(grad, denom, values, pair, height, low, high):
    slots = [denom_slot(pair, side, 2**height, values.shape[0]) for side in (0, 1)]
    queries = [stack([grad * mask, denom], 1) for mask in (low, high)]
    return queries, [stack([values, slot], 1) for slot in slots]


def near_kernel(load, factor_ref, x_ref, gh_ref, query_ref, key_ref, value_ref):
    rows, width = query_ref.shape
    heads = width // HALF
    low, high = side_masks()
    for pair in range(width // LANES):
        factor = side_factor(factor_ref, heads, pair)
        queries, keys, values = (x_ref[:, lane_pair(width * which, pair)] for which in range(3))
        grad = gh_ref[:, lane_pair(0, pair)]
        left, right = slope_sides(grad, gh_ref[:, width:], values, pair, 0, low, high)
        weights, slope = slopes(factor_ref, pair, queries, keys, left, right, low, high)
        query_ref[:, lane_pair(0, pair)] = dot(stack(slope, 1), masked_stack(keys, low, high)) * factor
        key_ref[:, lane_pair(0, pair)] = dot(stack(slope, 0), masked_stack(queries, low, high), TN) * factor
        value_ref[:, lane_pair(0, pair)] = dot(stack(weights, 0), masked_stack(grad, low, high), TN)


def far_kernel(top, load, factor_ref, base_ref, out_ref):
    rows, width = out_ref.shape
    heads = width // HALF
    low, high = side_masks()
    results = []
    for pair in range(width // LANES):
        factor = side_factor(factor_ref, heads, pair)
        total = None
        for height in range(top, 0, -1):
            queries = load(height - 1, lane_pair(0, pair))
            grad = load(top + height - 1, lane_pair(0, pair))
            denom = load(top + height - 1, slice(width, width + LANES))
            keys, values = (load(2 * top + height - 1, lane_pair(width * which, pair)) for which in (1, 2))
            left, right = slope_sides(grad, denom, values, pair, height, low, high)
            _, slope = slopes(factor_ref, pair, queries, keys, left, right, low, high)
            piece = dot(stack(slope, 1), masked_stack(keys, low, high)) * factor
            total = piece if total is None else piece + 0.5 * doubled(total)
        total = base_ref[:, lane_pair(0, pair)] + 0.5 * doubled(total)
        results.append(total.astype(BF))
    out_ref[...] = dot(order_matrix(rows, top, True), stack(results, 1)).astype(BF)


def key_kernel(top, load, factor_ref, base_key_ref, base_value_ref, key_out_ref, value_out_ref):
    rows, width = key_out_ref.shape
    heads = width // HALF
    low, high = side_masks()
    key_results, value_results = [], []
    for pair in range(width // LANES):
        factor = side_factor(factor_ref, heads, pair)
        key_total = value_total = None
        for height in range(top, 0, -1):
            keys, values = (load(height - 1, lane_pair(width * which, pair)) for which in (1, 2))
            queries = load(top + height - 1, lane_pair(0, pair))
            grad = load(2 * top + height - 1, lane_pair(0, pair))
            denom = load(2 * top + height - 1, slice(width, width + LANES))
            left = [
                stack([values * mask, denom_slot(pair, side, 2**height, values.shape[0])], 1)
                for side, mask in enumerate((low, high))
            ]
            right = [stack([grad, denom], 1)] * 2
            weights, slope = slopes(factor_ref, pair, keys, queries, left, right, low, high)
            key_piece = dot(stack(slope, 1), masked_stack(queries, low, high)) * factor
            value_piece = dot(stack(weights, 1), masked_stack(grad, low, high))
            if key_total is not None:
                key_piece = key_piece + 0.5 * doubled(key_total)
                value_piece = value_piece + doubled(value_total)
            key_total, value_total = key_piece, value_piece
        key_total = base_key_ref[:, lane_pair(0, pair)] + 0.5 * doubled(key_total)
        value_total = base_value_ref[:, lane_pair(0, pair)] + doubled(value_total)
        key_results.append(key_total.astype(BF))
        value_results.append(value_total.astype(BF))
    back = order_matrix(rows, top, True)
    key_out_ref[...] = dot(back, stack(key_results, 1)).astype(BF)
    value_out_ref[...] = dot(back, stack(value_results, 1)).astype(BF)


def pair_payload_kernel(rows, load, *refs):
    out_ref = refs[-1]
    every = slice(None)
    out_ref[:rows, :] = load(0, every)
    out_ref[rows : 2 * rows, :] = load(1, every)
    if out_ref.shape[0] > 2 * rows:
        out_ref[2 * rows :, :] = total_of(load, (2, 3)).astype(BF)


def total_of(load, groups):
    total = None
    for group in groups:
        value = load(group, slice(None)).astype(F32)
        total = value if total is None else total + value
    return total


def sum_kernel(count, load, out_ref):
    out_ref[...] = total_of(load, range(count)).astype(out_ref.dtype)


def unpack_sum_kernel(count, load, out_ref):
    unpack_into(total_of(load, range(count)), out_ref)


def traded(value, mask):
    return lax.ppermute(value, SEQ, [(source, source ^ mask) for source in range(lax.axis_size(SEQ))])


def split_traded(value):
    return lax.ppermute(
        value, SEQ, [(source, source ^ (4 + 2 * (source % 2))) for source in range(lax.axis_size(SEQ))]
    )


def from_siblings(levels, top):
    arrived = {}
    for offset in range(1, 2**top):
        height = offset.bit_length()
        if offset == 1:
            arrived[1] = traded(levels[1], 1)
        elif offset % 2 == 0:
            arrived[offset] = traded(levels[height], offset)
        else:
            arrived[offset] = traded(arrived[offset - 1], 1)
    grouped = []
    for height in range(1, top + 1):
        parts = [arrived[offset] for offset in range(2 ** (height - 1), 2**height)]
        if parts[0].shape[0] < 16:
            parts = [jnp.concatenate(parts, axis=0)]
        grouped.append([View(part) for part in parts])
    return grouped


def shards(queries, key_rows, value_rows, head_scale, out_weight, cotangent):
    rows, width = queries.shape[1:]
    heads = head_scale.shape[0]
    top = lax.axis_size(SEQ).bit_length() - 1
    parts = lax.axis_size("dp")
    assert width == HALF * heads and width % LANES == 0 and width <= 4 * LANES
    riding = top == 3 and parts == 4 and rows == 256
    whole = (rows, width)
    wide = width + LANES
    sizes = [rows >> height for height in range(top + 1)]
    if riding:
        places = [(1, 0), (2, 0), (1, sizes[1])]
        pooled = [rows, sizes[1] + sizes[3], sizes[2]]
    else:
        places = [(height, 0) for height in range(1, top + 1)]
        pooled = sizes
    factors, base_rows, *levels = call(
        functools.partial(pool_kernel, top, places),
        "pool",
        [((factor_rows(heads), LANES), F32)] + [((count, 3 * width), BF) for count in pooled],
        [queries[0], key_rows[0], value_rows[0], head_scale],
        specs=[HBM] * 4,
        scratch=[pltpu.VMEM(whole, BF)] * 3 + [pltpu.SMEM((heads,), F32), pltpu.SemaphoreType.DMA((4,))],
    )
    levels = [base_rows, *levels]
    numer, denom, cotan, back = call(
        functools.partial(base_kernel, top),
        "base",
        [(whole, F32), (whole, F32), (whole, BF), (whole, BF)],
        [factors, base_rows, cotangent[0], out_weight],
        flops=4 * rows * rows * width * 4,
    )
    own = [[View(levels[target], start, sizes[height + 1])] for height, (target, start) in enumerate(places)]
    if riding:
        within = traded(levels[1], 1)
        across = traded(levels[2], 2)
        (third,) = call(
            functools.partial(pair_payload_kernel, sizes[3]),
            "third_rows",
            [((2 * sizes[3], 3 * width), BF)],
            [],
            views=[own[2], [View(within, sizes[1], sizes[3])]],
        )
        split = split_traded(third)
        across, numer = lax.optimization_barrier((across, numer))
        across_too = traded(across, 1)
        split_too = traded(split, 1)
        siblings = [
            [View(within, 0, sizes[1])],
            [View(across), View(across_too)],
            [View(split), View(split_too)],
        ]
    else:
        siblings = from_siblings(levels, top)
    own_rows = width // parts
    if riding:
        spot = lax.axis_index(SEQ).astype(jnp.int32)
        chip, core = spot // 2, spot % 2
        place = jnp.stack([chip, chip ^ 1, chip ^ (3 - core), chip ^ (2 + core)])
        packed = packed_rows(own_rows, width)
        grad_places = [(0, 0), (1, sizes[3]), (2, 0), (1, 0)]
        near_rows = sizes[1] + sizes[3]
        piece_places = [(1, near_rows), (2, sizes[2]), (1, near_rows + packed), (3, 0)]
        shapes = [(rows, wide), (near_rows + 2 * packed, wide), (sizes[2] + packed, wide), (packed, wide)]
    else:
        place = (lax.axis_index("dp").astype(jnp.int32) + jnp.arange(parts, dtype=jnp.int32)) % parts
        grad_places = [(height, 0) for height in range(top + 1)]
        piece_places = [(top + 1 + step, 0) for step in range(parts)]
        shapes = [(size, wide) for size in sizes] + [(own_rows, width)] * parts
    outs = call(
        functools.partial(forward_kernel, top, parts, riding, grad_places, piece_places),
        "forward",
        [(shape, BF) for shape in shapes],
        [factors, numer, denom, cotan, back],
        views=own + siblings,
        scalars=[place],
        scratch=[pltpu.VMEM((width, width), F32)],
    )
    near_query, near_key, near_value = call(
        near_kernel,
        "near",
        [(whole, F32)] * 3,
        [factors, base_rows, outs[0]],
        flops=8 * rows * rows * width * 4,
    )
    own_grads = [[View(outs[target], start, sizes[height])] for height, (target, start) in enumerate(grad_places)]
    def far_call():
        return call(
            functools.partial(far_kernel, top),
            "far",
            [(whole, BF)],
            [factors, near_query],
            views=own + own_grads[1:] + siblings,
            flops=8 * rows * rows * width,
        )[0]

    def key_call():
        return call(
            functools.partial(key_kernel, top),
            "key",
            [(whole, BF), (whole, BF)],
            [factors, near_key, near_value],
            views=own + siblings + sibling_grads,
            flops=8 * rows * rows * width * 2,
        )

    if riding:
        near, far, mine = outs[1:4]
        near_in = traded(near, 1)
        far_in = traded(far, 2)
        (third,) = call(
            functools.partial(pair_payload_kernel, sizes[3]),
            "third_grads",
            [((2 * sizes[3] + packed, wide), BF)],
            [],
            views=[
                own_grads[3],
                [View(near_in, 0, sizes[3])],
                [View(mine)],
                [View(near_in, near_rows + packed, packed)],
            ],
        )
        third_in = split_traded(third)
        far_in, near_query = lax.optimization_barrier((far_in, near_query))
        far_too = traded(far_in, 1)
        third_too = traded(third_in, 1)
        sibling_grads = [
            [View(near_in, sizes[3], sizes[1])],
            [View(far_in, 0, sizes[2]), View(far_too, 0, sizes[2])],
            [View(third_in, 0, 2 * sizes[3]), View(third_too, 0, 2 * sizes[3])],
        ]
        (weight,) = call(
            functools.partial(sum_kernel, 6),
            "weight_seq",
            [((packed, wide), BF)],
            [],
            views=[[View(value, value.shape[0] - packed)] for value in (far_in, far_too, third_in, third_too)]
            + [[View(value, near_rows, packed)] for value in (near, near_in)],
        )
        moves = [[], []]
        for z in range(4):
            for k in range(4):
                for c in range(2):
                    for turn in range(2):
                        target = (k * 4 + (z - 2 * turn - c) % 4) * 2 + c
                        moves[turn].append(((z * 4 + k) * 2 + c, target))
        first, second = (lax.ppermute(weight, ("dp", *SEQ), pairs) for pairs in moves)
        key_grad, value_grad = key_call()
        first, key_grad = lax.optimization_barrier((first, key_grad))
        (half,) = call(
            functools.partial(sum_kernel, 2),
            "weight_core",
            [((packed, wide), BF)],
            [],
            views=[[View(first)], [View(second)]],
        )
        other = traded(half, 1)
        query_grad = far_call()
        other, query_grad = lax.optimization_barrier((other, query_grad))
        (weight,) = call(
            functools.partial(unpack_sum_kernel, 2),
            "weight_out",
            [((own_rows, width), F32)],
            [],
            views=[[View(half)], [View(other)]],
        )
    else:
        grads, pieces = outs[: top + 1], outs[top + 1 :]
        weight = pieces[0].astype(F32)
        for step in range(1, parts):
            weight = weight + lax.ppermute(
                pieces[step], "dp", [(source, (source + step) % parts) for source in range(parts)]
            ).astype(F32)
        sibling_grads = from_siblings(grads, top)
        bit = 1
        while bit < top:
            weight = weight.astype(BF)
            group = [weight] + [traded(weight, mask << bit) for mask in range(1, 2 ** min(2, top - bit))]
            weight = sum(value.astype(F32) for value in group)
            bit += 2
        weight = weight.astype(BF)
        weight = weight.astype(F32) + traded(weight, 1).astype(F32)
        query_grad = far_call()
        key_grad, value_grad = key_call()
    return query_grad[None], key_grad[None], value_grad[None], weight


def solution(mesh):
    spread = P("dp", SEQ, None)
    return jax.shard_map(
        shards,
        mesh=mesh,
        in_specs=(spread, spread, spread, P(), P(), spread),
        out_specs=(spread, spread, spread, P("dp", None)),
        check_vma=False,
    )
```

```python
import functools
import math

import jax
import jax.numpy as jnp
from jax import lax
from jax.experimental import pallas as pl
from jax.experimental.pallas import tpu as pltpu
from jax.sharding import PartitionSpec as P

BF = jnp.bfloat16
F32 = jnp.float32
SEQ = ("seqhi", "seqlo")
LANES = 128
HALF = 64
LOG2E = math.log2(math.e)
NN = (((1,), (0,)), ((), ()))
NT = (((1,), (1,)), ((), ()))
TN = (((0,), (0,)), ((), ()))


def dot(left, right, dims=NN):
    return lax.dot_general(left, right, dims, preferred_element_type=F32)


def iota(shape, dim):
    return lax.broadcasted_iota(jnp.int32, shape, dim)


def order_matrix(rows, top, inverse=False):
    source = iota((rows, rows), 0 if inverse else 1)
    place = source >> top
    for bit in range(top):
        place = place + ((source >> bit) & 1) * (rows >> (bit + 1))
    return jnp.where(place == iota((rows, rows), 1 if inverse else 0), 1.0, 0.0).astype(BF)


def side_masks():
    lane = iota((1, LANES), 1)
    low = jnp.where(lane < HALF, 1.0, 0.0)
    return low.astype(BF), (1.0 - low).astype(BF)


def factor_rows(heads):
    return -(-(heads + heads // 2) // 8) * 8


def fill_factors(scale_ref, factor_ref):
    heads = scale_ref.shape[0]
    lane = iota((1, LANES), 1)
    for head in range(heads):
        factor_ref[head : head + 1, :] = jnp.full((1, LANES), scale_ref[head] * (HALF**-0.5 * LOG2E), F32)
    for pair in range(heads // 2):
        both = jnp.where(lane < HALF, scale_ref[2 * pair], scale_ref[2 * pair + 1]) * (HALF**-0.5)
        factor_ref[heads + pair : heads + pair + 1, :] = both


def exponent(factor_ref, head, columns):
    return stack([factor_ref[head : head + 1, :]] * (columns // LANES), 1)


def side_factor(factor_ref, heads, pair):
    return factor_ref[heads + pair : heads + pair + 1, :]


def stack(parts, axis):
    return parts[0] if len(parts) == 1 else jnp.concatenate(parts, axis=axis)


def doubled(value):
    return jnp.concatenate([value, value], axis=0)


def halves_sum(value):
    half = value.shape[0] // 2
    return value[:half] + value[half:]


def lane_pair(offset, pair):
    return slice(offset + LANES * pair, offset + LANES * (pair + 1))


def slot_masks(pair):
    lane = iota((1, LANES), 1)
    masks = []
    for side in (0, 1):
        slot = lane - side * HALF
        hit = (slot == 16 * pair) | (slot == 16 * pair + 8)
        masks.append(jnp.where(hit, 1.0, 0.0).astype(BF))
    return masks


def denom_lanes(denoms):
    lane = iota((1, LANES), 1)
    slot = (lane % HALF) // 8
    packed = jnp.zeros(denoms[0].shape, F32)
    for pair, value in enumerate(denoms):
        high = value.astype(BF).astype(F32)
        packed = jnp.where(slot == 2 * pair, high, packed)
        packed = jnp.where(slot == 2 * pair + 1, value - high, packed)
    return packed.astype(BF)


class View:
    def __init__(self, array, start=0, rows=None):
        self.array = array
        self.start = start
        self.rows = array.shape[0] - start if rows is None else rows


VMEM = pl.BlockSpec(memory_space=pltpu.VMEM)
SMEM = pl.BlockSpec(memory_space=pltpu.SMEM)
HBM = pl.BlockSpec(memory_space=pltpu.HBM)


def call(kernel, name, shapes, arrays, views=(), scalars=(), flops=0, scratch=(), specs=None):
    unique, where = [], []
    for group in views:
        places = []
        for view in group:
            spot = next((at for at, array in enumerate(unique) if array is view.array), None)
            if spot is None:
                spot = len(unique)
                unique.append(view.array)
            places.append((spot, view.start, view.rows))
        where.append(places)

    def body(*refs):
        scalar_refs, refs = refs[: len(scalars)], refs[len(scalars) :]
        array_refs, refs = refs[: len(arrays)], refs[len(arrays) :]
        view_refs, refs = refs[: len(unique)], refs[len(unique) :]

        def load(group, columns):
            return stack(
                [view_refs[spot][start : start + rows, columns] for spot, start, rows in where[group]], 0
            )

        kernel(load, *scalar_refs, *array_refs, *refs)

    moved = sum(math.prod(shape) * jnp.dtype(kind).itemsize for shape, kind in shapes)
    return pl.pallas_call(
        body,
        out_shape=[jax.ShapeDtypeStruct(shape, kind) for shape, kind in shapes],
        in_specs=[SMEM] * len(scalars) + (specs or [VMEM] * len(arrays)) + [VMEM] * len(unique),
        out_specs=[VMEM] * len(shapes),
        scratch_shapes=list(scratch),
        compiler_params=pltpu.CompilerParams(vmem_limit_bytes=16 * 2**20),
        cost_estimate=pl.CostEstimate(flops=flops, transcendentals=0, bytes_accessed=moved),
        name=name,
    )(*scalars, *arrays, *unique)


def pool_kernel(top, places, load, q_hbm, k_hbm, v_hbm, scale_hbm, factor_ref, *refs):
    out_refs, (q_ref, k_ref, v_ref, scale_ref, sems) = refs[:-5], refs[-5:]
    level_refs, query_refs = out_refs[:-top], out_refs[-top:]
    copies = [
        pltpu.make_async_copy(source, target, sems.at[index])
        for index, (source, target) in enumerate(
            ((q_hbm, q_ref), (k_hbm, k_ref), (v_hbm, v_ref), (scale_hbm, scale_ref))
        )
    ]
    for which in (1, 2, 0, 3):
        copies[which].start()
    rows, width = q_ref.shape
    order = order_matrix(rows, top)
    for which, ref in ((1, k_ref), (2, v_ref), (0, q_ref)):
        copies[which].wait()
        current = dot(order, ref[...])
        level_refs[0][:, which * width : (which + 1) * width] = current.astype(BF)
        for height in range(1, top + 1):
            total = halves_sum(current)
            rounded = (total if which == 2 else 0.5 * total).astype(BF)
            if which:
                target, start = places[height - 1]
                columns = slice((which - 1) * width, which * width)
                level_refs[target][start : start + rounded.shape[0], columns] = rounded
            else:
                query_refs[height - 1][...] = rounded
            current = rounded.astype(F32)
    copies[3].wait()
    fill_factors(scale_ref, factor_ref)


def masked_stack(value, masks):
    return stack([value * mask for mask in masks], 0)


def both_weights(factor_ref, pair, first, second, masks):
    rows = first.shape[0]
    logits = dot(masked_stack(first, masks), second, NT)
    columns = second.shape[0]
    return [
        jnp.exp2(logits[side * rows : (side + 1) * rows] * exponent(factor_ref, 2 * pair + side, columns))
        for side in (0, 1)
    ]


def attend(factor_ref, pair, queries, keys, values, amount, masks):
    weights = both_weights(factor_ref, pair, queries, keys, masks)
    joined = stack([weight.astype(BF) for weight in weights], 1)
    count = jnp.full(values.shape, float(amount), BF)
    right = stack([stack([values * mask, count * mask], 1) for mask in masks], 0)
    return joined, dot(joined, right)


def base_kernel(top, load, factor_ref, x_ref, cot_ref, w_ref, numer_ref, denom_ref, weights_ref, cotp_ref, back_ref):
    rows, width = cot_ref.shape
    masks = side_masks()
    for pair in range(width // LANES):
        q, k, v = (x_ref[:, lane_pair(width * which, pair)] for which in range(3))
        joined, both = attend(factor_ref, pair, q, k, v, 1, masks)
        numer_ref[:, lane_pair(0, pair)] = both[:, :LANES]
        denom_ref[:, lane_pair(0, pair)] = both[:, LANES:]
        weights_ref[:, 2 * rows * pair : 2 * rows * (pair + 1)] = joined
    cotan = dot(order_matrix(rows, top), cot_ref[...]).astype(BF)
    cotp_ref[...] = cotan
    back_ref[...] = dot(cotan, w_ref[...], NT).astype(BF)


def forward_kernel(
    top, parts, grad_places, pieces,
    load, place_ref, factor_ref, numer_ref, denom_ref, cotp_ref, back_ref, *refs
):
    weights_refs, out_refs, weight_ref = refs[:top], refs[top:-1], refs[-1]
    rows, width = numer_ref.shape
    masks = side_masks()
    lane = iota((LANES, LANES), 1)
    ones = jnp.where(lane // HALF == iota((LANES, LANES), 0) // HALF, 1.0, 0.0).astype(BF)
    adder = doubled(ones)
    grad_rows = []
    denom_rows = []
    attended = []
    for pair in range(width // LANES):
        total = None
        for height in range(top, 0, -1):
            queries = load(height - 1, lane_pair(0, pair))
            keys, values = (load(top + height - 1, lane_pair(start, pair)) for start in (0, width))
            joined, both = attend(factor_ref, pair, queries, keys, values, 2**height, masks)
            columns = joined.shape[1]
            weights_refs[height - 1][:, columns * pair : columns * (pair + 1)] = joined
            total = both if total is None else both + doubled(total)
        total = doubled(total)
        numer = numer_ref[:, lane_pair(0, pair)] + total[:, :LANES]
        inverse = 1.0 / (denom_ref[:, lane_pair(0, pair)] + total[:, LANES:])
        ratio = numer * inverse
        attended.append(ratio.astype(BF))
        back = back_ref[:, lane_pair(0, pair)].astype(F32)
        product = back * ratio
        product_high = product.astype(BF)
        product_low = (product - product_high.astype(F32)).astype(BF)
        summed = dot(stack([product_high, product_low], 1), adder)
        grad_rows.append(back * inverse)
        denom_rows.append(-summed * inverse)
    weight_ref[...] = dot(stack(attended, 1), cotp_ref[...], TN)
    own_rows = width // parts
    for entry, offset, count, target, start in pieces:
        shift = offset if isinstance(offset, int) else offset(place_ref)
        first = pl.multiple_of(place_ref[entry] * own_rows + shift, math.gcd(own_rows, count))
        out_refs[target][start : start + count, :] = weight_ref[pl.ds(first, count), :].astype(BF)
    for height, (target, start) in enumerate(grad_places):
        if height:
            grad_rows = [halves_sum(value) for value in grad_rows]
            denom_rows = [halves_sum(value) for value in denom_rows]
        span = slice(start, start + (rows >> height))
        for pair, value in enumerate(grad_rows):
            out_refs[target][span, lane_pair(0, pair)] = value.astype(BF)
        out_refs[target][span, width : width + LANES] = denom_lanes(denom_rows)
        if height:
            out_refs[target][span, width + LANES :] = load(height - 1, slice(None))


def query_slopes(joined, grad, denom, values, pair, height, masks):
    rows, columns = grad.shape[0], values.shape[0]
    left = stack([stack([grad * mask, denom * slot], 1) for mask, slot in zip(masks, slot_masks(pair))], 0)
    right = stack([values, jnp.full((columns, LANES), float(2**height), BF)], 1)
    product = dot(left, right, NT)
    return [
        (joined[:, side * columns : (side + 1) * columns].astype(F32) * product[side * rows : (side + 1) * rows])
        .astype(BF)
        for side in (0, 1)
    ]


def near_kernel(load, factor_ref, x_ref, gh_ref, weights_ref, query_ref, key_ref, value_ref):
    rows, width = query_ref.shape
    heads = width // HALF
    masks = side_masks()
    for pair in range(width // LANES):
        factor = side_factor(factor_ref, heads, pair)
        queries, keys, values = (x_ref[:, lane_pair(width * which, pair)] for which in range(3))
        grad = gh_ref[:, lane_pair(0, pair)]
        joined = weights_ref[:, 2 * rows * pair : 2 * rows * (pair + 1)]
        slope = query_slopes(joined, grad, gh_ref[:, width:], values, pair, 0, masks)
        query_ref[:, lane_pair(0, pair)] = dot(stack(slope, 1), masked_stack(keys, masks)) * factor
        key_ref[:, lane_pair(0, pair)] = dot(stack(slope, 0), masked_stack(queries, masks), TN) * factor
        weights = stack([joined[:, :rows], joined[:, rows:]], 0)
        value_ref[:, lane_pair(0, pair)] = dot(weights, masked_stack(grad, masks), TN)


def far_kernel(top, load, factor_ref, base_ref, *refs):
    weights_refs, out_ref = refs[:top], refs[top]
    rows, width = out_ref.shape
    heads = width // HALF
    masks = side_masks()
    results = []
    for pair in range(width // LANES):
        factor = side_factor(factor_ref, heads, pair)
        total = None
        for height in range(top, 0, -1):
            grad = load(height - 1, lane_pair(0, pair))
            denom = load(height - 1, slice(width, width + LANES))
            keys, values = (load(top + height - 1, lane_pair(start, pair)) for start in (0, width))
            columns = 2 * keys.shape[0]
            joined = weights_refs[height - 1][:, columns * pair : columns * (pair + 1)]
            slope = query_slopes(joined, grad, denom, values, pair, height, masks)
            piece = dot(stack(slope, 1), masked_stack(keys, masks)) * factor
            total = piece if total is None else piece + 0.5 * doubled(total)
        total = base_ref[:, lane_pair(0, pair)] + 0.5 * doubled(total)
        results.append(total.astype(BF))
    out_ref[...] = dot(order_matrix(rows, top, True), stack(results, 1)).astype(BF)


def key_kernel(top, load, factor_ref, base_key_ref, base_value_ref, key_out_ref, value_out_ref):
    rows, width = key_out_ref.shape
    heads = width // HALF
    masks = side_masks()
    key_results, value_results = [], []
    for pair in range(width // LANES):
        factor = side_factor(factor_ref, heads, pair)
        key_total = value_total = None
        for height in range(top, 0, -1):
            keys, values = (load(height - 1, lane_pair(start, pair)) for start in (0, width))
            grad = load(top + height - 1, lane_pair(0, pair))
            denom = load(top + height - 1, slice(width, width + LANES))
            queries = load(top + height - 1, lane_pair(width + LANES, pair))
            count = keys.shape[0]
            weights = both_weights(factor_ref, pair, keys, queries, masks)
            left = stack(
                [
                    stack([values * mask, jnp.broadcast_to(slot * float(2**height), (count, LANES))], 1)
                    for mask, slot in zip(masks, slot_masks(pair))
                ],
                0,
            )
            product = dot(left, stack([grad, denom], 1), NT)
            slope = [
                (weight * product[side * count : (side + 1) * count]).astype(BF)
                for side, weight in enumerate(weights)
            ]
            key_piece = dot(stack(slope, 1), masked_stack(queries, masks)) * factor
            value_piece = dot(stack([weight.astype(BF) for weight in weights], 1), masked_stack(grad, masks))
            if key_total is not None:
                key_piece = key_piece + 0.5 * doubled(key_total)
                value_piece = value_piece + doubled(value_total)
            key_total, value_total = key_piece, value_piece
        key_total = base_key_ref[:, lane_pair(0, pair)] + 0.5 * doubled(key_total)
        value_total = base_value_ref[:, lane_pair(0, pair)] + doubled(value_total)
        key_results.append(key_total.astype(BF))
        value_results.append(value_total.astype(BF))
    back = order_matrix(rows, top, True)
    key_out_ref[...] = dot(back, stack(key_results, 1)).astype(BF)
    value_out_ref[...] = dot(back, stack(value_results, 1)).astype(BF)


def place_kernel(spots, load, *refs):
    for target, start, groups in spots:
        total = None
        for group in groups:
            value = load(group, slice(None))
            if len(groups) > 1 or refs[target].dtype == F32:
                value = value.astype(F32)
            total = value if total is None else total + value
        refs[target][start : start + total.shape[0], :] = total.astype(refs[target].dtype)


def placed(name, shapes, spots):
    views, listed = [], []
    for target, start, parts in spots:
        listed.append((target, start, range(len(views), len(views) + len(parts))))
        views += [[part] for part in parts]
    return call(functools.partial(place_kernel, listed), name, shapes, [], views=views)


def total_kernel(load, core_ref, own_ref, partner_ref, *refs):
    half = own_ref.shape[0] // 3
    base_ref = refs[0] if refs[0].shape[0] == 2 * half and len(refs) == 3 and refs[1].dtype == F32 else None
    out_refs = refs[:-1] if base_ref is None else refs[1:-1]
    sum_ref = refs[-1]
    total = own_ref[: 2 * half, :].astype(F32) + partner_ref[: 2 * half, :].astype(F32)
    if base_ref is not None:
        total = total + base_ref[...].astype(F32)
    sum_ref[...] = total
    for ref, core in ((own_ref, core_ref[0]), (partner_ref, 1 - core_ref[0])):
        span = pl.ds(pl.multiple_of(core * half, half), half)
        sum_ref[span, :] = sum_ref[span, :] + ref[2 * half :, :].astype(F32)
    out_refs[0][...] = sum_ref[...].astype(out_refs[0].dtype)
    if len(out_refs) > 1:
        span = pl.ds(pl.multiple_of(core_ref[0] * half, half), half)
        out_refs[1][...] = sum_ref[span, :].astype(BF)


def chip_total(name, core, arrays, half, kind):
    width = arrays[0].shape[1]
    shapes = [((2 * half, width), kind)] + [((half, width), BF)] * (kind == BF)
    return call(
        total_kernel, name, shapes, arrays, scalars=[core.reshape(1)], scratch=[pltpu.VMEM((2 * half, width), F32)]
    )


def traded(value, mask):
    return lax.ppermute(value, SEQ, [(source, source ^ mask) for source in range(lax.axis_size(SEQ))])


def split_traded(value, first, second):
    return lax.ppermute(
        value,
        SEQ,
        [(source, source ^ (2 * (second if source % 2 else first))) for source in range(lax.axis_size(SEQ))],
    )


def layer_traded(value, first, second):
    axes = ("dp", *SEQ)
    count = lax.axis_size(SEQ)
    pairs = []
    for source in range(lax.axis_size(axes)):
        layer, spot = divmod(source, count)
        pairs.append((source, (layer ^ (second if spot % 2 else first)) * count + spot))
    return lax.ppermute(value, axes, pairs)


def from_siblings(levels, top):
    arrived = {}
    for offset in range(1, 2**top):
        height = offset.bit_length()
        if offset == 1:
            arrived[1] = traded(levels[0], 1)
        elif offset % 2 == 0:
            arrived[offset] = traded(levels[height - 1], offset)
        else:
            arrived[offset] = traded(arrived[offset - 1], 1)
    grouped = []
    for height in range(1, top + 1):
        parts = [arrived[offset] for offset in range(2 ** (height - 1), 2**height)]
        if parts[0].shape[0] < 16:
            parts = [jnp.concatenate(parts, axis=0)]
        grouped.append([View(part) for part in parts])
    return grouped


def shards(queries, key_rows, value_rows, head_scale, out_weight, cotangent):
    rows, width = queries.shape[1:]
    heads = head_scale.shape[0]
    top = lax.axis_size(SEQ).bit_length() - 1
    parts = lax.axis_size("dp")
    assert width == HALF * heads and width % LANES == 0 and width <= 4 * LANES
    paired = top == 3 and parts == 4 and rows == 256
    whole = (rows, width)
    wide = width + LANES
    sizes = [rows >> height for height in range(top + 1)]
    if paired:
        places = [(1, 0), (2, 0), (1, sizes[1])]
        pooled = [sizes[1] + sizes[3], sizes[2]]
    else:
        places = [(height, 0) for height in range(1, top + 1)]
        pooled = sizes[1:]
    factors, base_rows, *outs = call(
        functools.partial(pool_kernel, top, places),
        "pool",
        [((factor_rows(heads), LANES), F32), ((rows, 3 * width), BF)]
        + [((count, 2 * width), BF) for count in pooled]
        + [((size, width), BF) for size in sizes[1:]],
        [pltpu.with_memory_space_constraint(value, pltpu.HBM) for value in (queries[0], key_rows[0], value_rows[0], head_scale)],
        specs=[HBM] * 4,
        scratch=[pltpu.VMEM(whole, BF)] * 3 + [pltpu.SMEM((heads,), F32), pltpu.SemaphoreType.DMA((4,))],
    )
    levels, level_queries = outs[:-top], [[View(value)] for value in outs[-top:]]
    own = [[View(levels[target - 1], start, sizes[height + 1])] for height, (target, start) in enumerate(places)]
    numer, denom, base_weights, cotan, back = call(
        functools.partial(base_kernel, top),
        "base",
        [(whole, F32), (whole, F32), ((rows, heads * rows), BF), (whole, BF), (whole, BF)],
        [factors, base_rows, cotangent[0], out_weight],
        flops=4 * rows * rows * width * 4,
    )
    if paired:
        within = traded(levels[0], 1)
        across = traded(levels[1], 2)
        (third,) = placed(
            "third_rows",
            [((2 * sizes[3], 2 * width), BF)],
            [(0, 0, [own[2][0]]), (0, sizes[3], [View(within, sizes[1], sizes[3])])],
        )
        split = split_traded(third, 2, 3)
        across, numer = lax.optimization_barrier((across, numer))
        across_too = traded(across, 1)
        split_too = traded(split, 1)
        siblings = [
            [View(within, 0, sizes[1])],
            [View(across), View(across_too)],
            [View(split), View(split_too)],
        ]
    else:
        siblings = from_siblings(levels, top)
    own_rows = width // parts
    half = own_rows // 2
    layer = lax.axis_index("dp").astype(jnp.int32)
    if paired:
        core = lax.axis_index(SEQ).astype(jnp.int32) % 2
        place = jnp.stack([layer, layer ^ (1 + 2 * core), layer ^ (3 - 2 * core), layer ^ 2, core * half])
        grad_places = [(0, 0), (1, 0), (2, 0), (1, sizes[1])]
        shapes = [(rows, wide), (sizes[1] + sizes[3], wide + width), (sizes[2], wide + width)]
        pieces = [
            (0, 0, own_rows, 3, 0),
            (1, 0, own_rows, 4, 0),
            (3, lambda ref: ref[4], half, 4, own_rows),
            (2, 0, own_rows, 5, 0),
            (3, lambda ref: half - ref[4], half, 5, own_rows),
        ]
        shapes += [(own_rows, width), (own_rows + half, width), (own_rows + half, width)]
    else:
        place = (layer + jnp.arange(parts, dtype=jnp.int32)) % parts
        grad_places = [(height, 0) for height in range(top + 1)]
        pieces = [(step, 0, own_rows, top + 1 + step, 0) for step in range(parts)]
        shapes = [(rows, wide)] + [(size, wide + width) for size in sizes[1:]] + [(own_rows, width)] * parts
    outs = call(
        functools.partial(forward_kernel, top, parts, grad_places, pieces),
        "forward",
        [((size, heads * rows // 2), BF) for size in sizes[1:]] + [(shape, BF) for shape in shapes],
        [factors, numer, denom, cotan, back],
        views=level_queries + siblings,
        scalars=[place],
        scratch=[pltpu.VMEM((width, width), F32)],
    )
    level_weights, outs = outs[:top], outs[top:]
    own_grads = [
        [View(outs[target], start, sizes[height])] for height, (target, start) in enumerate(grad_places) if height
    ]
    near_query, near_key, near_value = call(
        near_kernel,
        "near",
        [(whole, F32)] * 3,
        [factors, base_rows, outs[0], base_weights],
        flops=8 * rows * rows * width * 4,
    )
    (query_grad,) = call(
        functools.partial(far_kernel, top),
        "far",
        [(whole, BF)],
        [factors, near_query, *level_weights],
        views=own_grads + siblings,
        flops=8 * rows * rows * width,
    )

    def key_call(sibling_grads):
        return call(
            functools.partial(key_kernel, top),
            "key",
            [(whole, BF), (whole, BF)],
            [factors, near_key, near_value],
            views=own + sibling_grads,
            flops=8 * rows * rows * width * 2,
        )

    if paired:
        near, far, mine, send, theirs = outs[1:6]
        theirs_in = traded(theirs, 1)
        near_in = traded(near, 1)
        far_in = traded(far, 2)
        send_one, send_half = placed(
            "layer_rows",
            [((own_rows, width), BF), ((half, width), BF)],
            [
                (0, 0, [View(send, 0, own_rows), View(theirs_in, 0, own_rows)]),
                (1, 0, [View(send, own_rows), View(theirs_in, own_rows)]),
            ],
        )
        layer_one = layer_traded(send_one, 1, 3)
        layer_half = layer_traded(send_half, 2, 2)
        (third,) = placed(
            "third_grads",
            [((2 * sizes[3], wide + width), BF)],
            [(0, 0, [own_grads[2][0]]), (0, sizes[3], [View(near_in, sizes[1])])],
        )
        third_in = split_traded(third, 2, 3)
        far_in, near_query = lax.optimization_barrier((far_in, near_query))
        far_too = traded(far_in, 1)
        layer_one, query_grad = lax.optimization_barrier((layer_one, query_grad))
        third_too = traded(third_in, 1)
        sibling_grads = [
            [View(near_in, 0, sizes[1])],
            [View(far_in), View(far_too)],
            [View(third_in), View(third_too)],
        ]
        (joint,) = placed(
            "layer_sum",
            [((own_rows + half, width), BF)],
            [(0, 0, [View(mine), View(layer_one)]), (0, own_rows, [View(layer_half)])],
        )
        joint_in = traded(joint, 1)
        weight, weight_half = chip_total("layer_total", core, [joint, joint_in], half, BF)
        plane_one = split_traded(weight, 1, 2)
        plane_half = traded(weight_half, 6)
        key_grad, value_grad = key_call(sibling_grads)
        plane_one, key_grad = lax.optimization_barrier((plane_one, key_grad))
        (joint,) = placed(
            "plane_rows",
            [((own_rows + half, width), BF)],
            [(0, 0, [View(plane_one)]), (0, own_rows, [View(plane_half)])],
        )
        joint_in = traded(joint, 1)
        (weight,) = chip_total("weight_out", core, [joint, joint_in, weight], half, F32)
    else:
        pieces = outs[top + 1 :]
        weight = pieces[0].astype(F32)
        for step in range(1, parts):
            weight = weight + lax.ppermute(
                pieces[step], "dp", [(source, (source + step) % parts) for source in range(parts)]
            ).astype(F32)
        sibling_grads = from_siblings(outs[1 : top + 1], top)
        bit = 1
        while bit < top:
            weight = weight.astype(BF)
            group = [weight] + [traded(weight, mask << bit) for mask in range(1, 2 ** min(2, top - bit))]
            weight = sum(value.astype(F32) for value in group)
            bit += 2
        weight = weight.astype(BF)
        weight = weight.astype(F32) + traded(weight, 1).astype(F32)
        key_grad, value_grad = key_call(sibling_grads)
    return query_grad[None], key_grad[None], value_grad[None], weight


def solution(mesh):
    spread = P("dp", SEQ, None)
    return jax.shard_map(
        shards,
        mesh=mesh,
        in_specs=(spread, spread, spread, P(), P(), spread),
        out_specs=(spread, spread, spread, P("dp", None)),
        check_vma=False,
    )
```

```python
import functools
import math

import jax
import jax.numpy as jnp
from jax import lax
from jax.experimental import pallas as pl
from jax.experimental.pallas import tpu as pltpu
from jax.sharding import PartitionSpec as P

BF = jnp.bfloat16
F32 = jnp.float32
SEQ = ("seqhi", "seqlo")
LANES = 128
HALF = 64
LOG2E = math.log2(math.e)
NN = (((1,), (0,)), ((), ()))
NT = (((1,), (1,)), ((), ()))
TN = (((0,), (0,)), ((), ()))


def dot(left, right, dims=NN):
    return lax.dot_general(left, right, dims, preferred_element_type=F32)


def iota(shape, dim):
    return lax.broadcasted_iota(jnp.int32, shape, dim)


def order_matrix(rows, top, inverse=False):
    source = iota((rows, rows), 0 if inverse else 1)
    place = source >> top
    for bit in range(top):
        place = place + ((source >> bit) & 1) * (rows >> (bit + 1))
    return jnp.where(place == iota((rows, rows), 1 if inverse else 0), 1.0, 0.0).astype(BF)


def side_masks():
    lane = iota((1, LANES), 1)
    low = jnp.where(lane < HALF, 1.0, 0.0)
    return low.astype(BF), (1.0 - low).astype(BF)


def factor_rows(heads):
    return -(-(heads + heads // 2) // 8) * 8


def fill_factors(scale_ref, factor_ref):
    heads = scale_ref.shape[0]
    lane = iota((1, LANES), 1)
    for head in range(heads):
        factor_ref[head : head + 1, :] = jnp.full((1, LANES), scale_ref[head] * (HALF**-0.5 * LOG2E), F32)
    for pair in range(heads // 2):
        both = jnp.where(lane < HALF, scale_ref[2 * pair], scale_ref[2 * pair + 1]) * (HALF**-0.5)
        factor_ref[heads + pair : heads + pair + 1, :] = both


def exponent(factor_ref, head, columns):
    return stack([factor_ref[head : head + 1, :]] * (columns // LANES), 1)


def side_factor(factor_ref, heads, pair):
    return factor_ref[heads + pair : heads + pair + 1, :]


def stack(parts, axis):
    return parts[0] if len(parts) == 1 else jnp.concatenate(parts, axis=axis)


def doubled(value):
    return jnp.concatenate([value, value], axis=0)


def halves_sum(value):
    half = value.shape[0] // 2
    return value[:half] + value[half:]


def lane_pair(offset, pair):
    return slice(offset + LANES * pair, offset + LANES * (pair + 1))


def slot_masks(pair):
    lane = iota((1, LANES), 1)
    masks = []
    for side in (0, 1):
        slot = lane - side * HALF
        hit = (slot == 16 * pair) | (slot == 16 * pair + 8)
        masks.append(jnp.where(hit, 1.0, 0.0).astype(BF))
    return masks


def denom_lanes(denoms):
    lane = iota((1, LANES), 1)
    slot = (lane % HALF) // 8
    packed = jnp.zeros(denoms[0].shape, F32)
    for pair, value in enumerate(denoms):
        high = value.astype(BF).astype(F32)
        packed = jnp.where(slot == 2 * pair, high, packed)
        packed = jnp.where(slot == 2 * pair + 1, value - high, packed)
    return packed.astype(BF)


class View:
    def __init__(self, array, start=0, rows=None):
        self.array = array
        self.start = start
        self.rows = array.shape[0] - start if rows is None else rows


VMEM = pl.BlockSpec(memory_space=pltpu.VMEM)
SMEM = pl.BlockSpec(memory_space=pltpu.SMEM)
HBM = pl.BlockSpec(memory_space=pltpu.HBM)


def call(kernel, name, shapes, arrays, views=(), scalars=(), flops=0, scratch=(), specs=None, out_specs=None):
    unique, where = [], []
    for group in views:
        places = []
        for view in group:
            spot = next((at for at, array in enumerate(unique) if array is view.array), None)
            if spot is None:
                spot = len(unique)
                unique.append(view.array)
            places.append((spot, view.start, view.rows))
        where.append(places)

    def body(*refs):
        scalar_refs, refs = refs[: len(scalars)], refs[len(scalars) :]
        array_refs, refs = refs[: len(arrays)], refs[len(arrays) :]
        view_refs, refs = refs[: len(unique)], refs[len(unique) :]

        def load(group, columns):
            return stack(
                [view_refs[spot][start : start + rows, columns] for spot, start, rows in where[group]], 0
            )

        kernel(load, *scalar_refs, *array_refs, *refs)

    moved = sum(math.prod(shape) * jnp.dtype(kind).itemsize for shape, kind in shapes)
    return pl.pallas_call(
        body,
        out_shape=[jax.ShapeDtypeStruct(shape, kind) for shape, kind in shapes],
        in_specs=[SMEM] * len(scalars) + (specs or [VMEM] * len(arrays)) + [VMEM] * len(unique),
        out_specs=out_specs or [VMEM] * len(shapes),
        scratch_shapes=list(scratch),
        compiler_params=pltpu.CompilerParams(vmem_limit_bytes=16 * 2**20),
        cost_estimate=pl.CostEstimate(flops=flops, transcendentals=0, bytes_accessed=moved),
        name=name,
    )(*scalars, *arrays, *unique)


def pool_kernel(top, places, load, q_hbm, k_hbm, v_hbm, scale_hbm, factor_ref, *refs):
    out_refs, (q_ref, k_ref, v_ref, scale_ref, sems) = refs[:-5], refs[-5:]
    level_refs, query_refs = out_refs[:-top], out_refs[-top:]
    copies = [
        pltpu.make_async_copy(source, target, sems.at[index])
        for index, (source, target) in enumerate(
            ((q_hbm, q_ref), (k_hbm, k_ref), (v_hbm, v_ref), (scale_hbm, scale_ref))
        )
    ]
    for which in (1, 2, 0, 3):
        copies[which].start()
    rows, width = q_ref.shape
    order = order_matrix(rows, top)
    for which, ref in ((1, k_ref), (2, v_ref), (0, q_ref)):
        copies[which].wait()
        current = dot(order, ref[...])
        level_refs[0][:, which * width : (which + 1) * width] = current.astype(BF)
        for height in range(1, top + 1):
            total = halves_sum(current)
            rounded = (total if which == 2 else 0.5 * total).astype(BF)
            if which:
                target, start = places[height - 1]
                columns = slice((which - 1) * width, which * width)
                level_refs[target][start : start + rounded.shape[0], columns] = rounded
            else:
                query_refs[height - 1][...] = rounded
            current = rounded.astype(F32)
    copies[3].wait()
    fill_factors(scale_ref, factor_ref)


def masked_stack(value, masks):
    return stack([value * mask for mask in masks], 0)


def both_weights(factor_ref, pair, first, second, masks):
    rows = first.shape[0]
    logits = dot(masked_stack(first, masks), second, NT)
    columns = second.shape[0]
    return [
        jnp.exp2(logits[side * rows : (side + 1) * rows] * exponent(factor_ref, 2 * pair + side, columns))
        for side in (0, 1)
    ]


def attend(factor_ref, pair, queries, keys, values, amount, masks):
    weights = both_weights(factor_ref, pair, queries, keys, masks)
    joined = stack([weight.astype(BF) for weight in weights], 1)
    count = jnp.full(values.shape, float(amount), BF)
    right = stack([stack([values * mask, count * mask], 1) for mask in masks], 0)
    return joined, dot(joined, right)


def base_kernel(top, load, factor_ref, x_ref, cot_ref, w_ref, numer_ref, denom_ref, weights_ref, cotp_ref, back_ref):
    rows, width = cot_ref.shape
    masks = side_masks()
    for pair in range(width // LANES):
        q, k, v = (x_ref[:, lane_pair(width * which, pair)] for which in range(3))
        joined, both = attend(factor_ref, pair, q, k, v, 1, masks)
        numer_ref[:, lane_pair(0, pair)] = both[:, :LANES]
        denom_ref[:, lane_pair(0, pair)] = both[:, LANES:]
        weights_ref[:, 2 * rows * pair : 2 * rows * (pair + 1)] = joined
    cotan = dot(order_matrix(rows, top), cot_ref[...]).astype(BF)
    cotp_ref[...] = cotan
    back_ref[...] = dot(cotan, w_ref[...], NT).astype(BF)


def forward_kernel(
    top, parts, pieces, load, place_ref, factor_ref, numer_ref, denom_ref, cotp_ref, back_ref, _, *refs
):
    weights_refs, (grad_ref, slope_ref), out_refs, weight_ref = refs[:top], refs[top : top + 2], refs[top + 2 : -1], refs[-1]
    rows, width = numer_ref.shape
    masks = side_masks()
    lane = iota((LANES, LANES), 1)
    ones = jnp.where(lane // HALF == iota((LANES, LANES), 0) // HALF, 1.0, 0.0).astype(BF)
    adder = doubled(ones)
    attended = []
    for pair in range(width // LANES):
        total = None
        for height in range(top, 0, -1):
            queries = load(height - 1, lane_pair(0, pair))
            keys, values = (load(top + height - 1, lane_pair(start, pair)) for start in (0, width))
            joined, both = attend(factor_ref, pair, queries, keys, values, 2**height, masks)
            columns = joined.shape[1]
            weights_refs[height - 1][:, columns * pair : columns * (pair + 1)] = joined
            total = both if total is None else both + doubled(total)
        total = doubled(total)
        numer = numer_ref[:, lane_pair(0, pair)] + total[:, :LANES]
        inverse = 1.0 / (denom_ref[:, lane_pair(0, pair)] + total[:, LANES:])
        ratio = numer * inverse
        attended.append(ratio.astype(BF))
        back = back_ref[:, lane_pair(0, pair)].astype(F32)
        product = back * ratio
        product_high = product.astype(BF)
        product_low = (product - product_high.astype(F32)).astype(BF)
        summed = dot(stack([product_high, product_low], 1), adder)
        grad_ref[:, lane_pair(0, pair)] = back * inverse
        slope_ref[:, lane_pair(0, pair)] = -summed * inverse
    weight_ref[...] = dot(stack(attended, 1), cotp_ref[...], TN)
    own_rows = width // parts
    for entry, offset, count, target, start in pieces:
        shift = offset if isinstance(offset, int) else offset(place_ref)
        first = pl.multiple_of(place_ref[entry] * own_rows + shift, math.gcd(own_rows, count))
        out_refs[target][start : start + count, :] = weight_ref[pl.ds(first, count), :].astype(BF)


def grads_kernel(grad_places, load, grad_ref, slope_ref, *out_refs):
    rows, width = grad_ref.shape
    grad_rows = [grad_ref[:, lane_pair(0, pair)] for pair in range(width // LANES)]
    denom_rows = [slope_ref[:, lane_pair(0, pair)] for pair in range(width // LANES)]
    for height, (target, start) in enumerate(grad_places):
        if height:
            grad_rows = [halves_sum(value) for value in grad_rows]
            denom_rows = [halves_sum(value) for value in denom_rows]
        span = slice(start, start + (rows >> height))
        for pair, value in enumerate(grad_rows):
            out_refs[target][span, lane_pair(0, pair)] = value.astype(BF)
        out_refs[target][span, width : width + LANES] = denom_lanes(denom_rows)
        if height:
            out_refs[target][span, width + LANES :] = load(height - 1, slice(None))


def query_slopes(joined, grad, denom, values, pair, height, masks):
    rows, columns = grad.shape[0], values.shape[0]
    left = stack([stack([grad * mask, denom * slot], 1) for mask, slot in zip(masks, slot_masks(pair))], 0)
    right = stack([values, jnp.full((columns, LANES), float(2**height), BF)], 1)
    product = dot(left, right, NT)
    return [
        (joined[:, side * columns : (side + 1) * columns].astype(F32) * product[side * rows : (side + 1) * rows])
        .astype(BF)
        for side in (0, 1)
    ]


def near_kernel(load, factor_ref, x_ref, gh_ref, weights_ref, query_ref, key_ref, value_ref):
    rows, width = query_ref.shape
    heads = width // HALF
    masks = side_masks()
    for pair in range(width // LANES):
        factor = side_factor(factor_ref, heads, pair)
        queries, keys, values = (x_ref[:, lane_pair(width * which, pair)] for which in range(3))
        grad = gh_ref[:, lane_pair(0, pair)]
        joined = weights_ref[:, 2 * rows * pair : 2 * rows * (pair + 1)]
        slope = query_slopes(joined, grad, gh_ref[:, width:], values, pair, 0, masks)
        query_ref[:, lane_pair(0, pair)] = dot(stack(slope, 1), masked_stack(keys, masks)) * factor
        key_ref[:, lane_pair(0, pair)] = dot(stack(slope, 0), masked_stack(queries, masks), TN) * factor
        weights = stack([joined[:, :rows], joined[:, rows:]], 0)
        value_ref[:, lane_pair(0, pair)] = dot(weights, masked_stack(grad, masks), TN)


def far_kernel(top, load, factor_ref, base_ref, *refs):
    weights_refs, out_ref = refs[:top], refs[top]
    rows, width = out_ref.shape
    heads = width // HALF
    masks = side_masks()
    results = []
    for pair in range(width // LANES):
        factor = side_factor(factor_ref, heads, pair)
        total = None
        for height in range(top, 0, -1):
            grad = load(height - 1, lane_pair(0, pair))
            denom = load(height - 1, slice(width, width + LANES))
            keys, values = (load(top + height - 1, lane_pair(start, pair)) for start in (0, width))
            columns = 2 * keys.shape[0]
            joined = weights_refs[height - 1][:, columns * pair : columns * (pair + 1)]
            slope = query_slopes(joined, grad, denom, values, pair, height, masks)
            piece = dot(stack(slope, 1), masked_stack(keys, masks)) * factor
            total = piece if total is None else piece + 0.5 * doubled(total)
        total = base_ref[:, lane_pair(0, pair)] + 0.5 * doubled(total)
        results.append(total.astype(BF))
    out_ref[...] = dot(order_matrix(rows, top, True), stack(results, 1)).astype(BF)


def key_kernel(top, load, factor_ref, base_key_ref, base_value_ref, key_out_ref, value_out_ref):
    rows, width = key_out_ref.shape
    heads = width // HALF
    masks = side_masks()
    key_results, value_results = [], []
    for pair in range(width // LANES):
        factor = side_factor(factor_ref, heads, pair)
        key_total = value_total = None
        for height in range(top, 0, -1):
            keys, values = (load(height - 1, lane_pair(start, pair)) for start in (0, width))
            grad = load(top + height - 1, lane_pair(0, pair))
            denom = load(top + height - 1, slice(width, width + LANES))
            queries = load(top + height - 1, lane_pair(width + LANES, pair))
            count = keys.shape[0]
            weights = both_weights(factor_ref, pair, keys, queries, masks)
            left = stack(
                [
                    stack([values * mask, jnp.broadcast_to(slot * float(2**height), (count, LANES))], 1)
                    for mask, slot in zip(masks, slot_masks(pair))
                ],
                0,
            )
            product = dot(left, stack([grad, denom], 1), NT)
            slope = [
                (weight * product[side * count : (side + 1) * count]).astype(BF)
                for side, weight in enumerate(weights)
            ]
            key_piece = dot(stack(slope, 1), masked_stack(queries, masks)) * factor
            value_piece = dot(stack([weight.astype(BF) for weight in weights], 1), masked_stack(grad, masks))
            if key_total is not None:
                key_piece = key_piece + 0.5 * doubled(key_total)
                value_piece = value_piece + doubled(value_total)
            key_total, value_total = key_piece, value_piece
        key_total = base_key_ref[:, lane_pair(0, pair)] + 0.5 * doubled(key_total)
        value_total = base_value_ref[:, lane_pair(0, pair)] + doubled(value_total)
        key_results.append(key_total.astype(BF))
        value_results.append(value_total.astype(BF))
    back = order_matrix(rows, top, True)
    key_out_ref[...] = dot(back, stack(key_results, 1)).astype(BF)
    value_out_ref[...] = dot(back, stack(value_results, 1)).astype(BF)


def place_kernel(spots, load, *refs):
    for target, start, groups in spots:
        total = None
        for group in groups:
            value = load(group, slice(None))
            if len(groups) > 1 or refs[target].dtype == F32:
                value = value.astype(F32)
            total = value if total is None else total + value
        refs[target][start : start + total.shape[0], :] = total.astype(refs[target].dtype)


def flush_kernel(load, *refs):
    count = (len(refs) - 1) // 2
    copies = [
        pltpu.make_async_copy(refs[at], refs[count + at], refs[-1].at[at]) for at in range(count)
    ]
    for copy in copies:
        copy.start()
    for copy in copies:
        copy.wait()


def flush(*arrays):
    return call(
        flush_kernel,
        "flush",
        [(array.shape, array.dtype) for array in arrays],
        arrays,
        out_specs=[HBM] * len(arrays),
        scratch=[pltpu.SemaphoreType.DMA((len(arrays),))],
    )


def placed(name, shapes, spots):
    views, listed = [], []
    for target, start, parts in spots:
        listed.append((target, start, range(len(views), len(views) + len(parts))))
        views += [[part] for part in parts]
    return call(functools.partial(place_kernel, listed), name, shapes, [], views=views)


def total_kernel(load, core_ref, own_ref, partner_ref, *refs):
    half = own_ref.shape[0] // 3
    base_ref = refs[0] if refs[0].shape[0] == 2 * half and len(refs) == 3 and refs[1].dtype == F32 else None
    out_refs = refs[:-1] if base_ref is None else refs[1:-1]
    sum_ref = refs[-1]
    total = own_ref[: 2 * half, :].astype(F32) + partner_ref[: 2 * half, :].astype(F32)
    if base_ref is not None:
        total = total + base_ref[...].astype(F32)
    sum_ref[...] = total
    for ref, core in ((own_ref, core_ref[0]), (partner_ref, 1 - core_ref[0])):
        span = pl.ds(pl.multiple_of(core * half, half), half)
        sum_ref[span, :] = sum_ref[span, :] + ref[2 * half :, :].astype(F32)
    out_refs[0][...] = sum_ref[...].astype(out_refs[0].dtype)
    if len(out_refs) > 1:
        span = pl.ds(pl.multiple_of(core_ref[0] * half, half), half)
        out_refs[1][...] = sum_ref[span, :].astype(BF)


def chip_total(name, core, arrays, half, kind):
    width = arrays[0].shape[1]
    shapes = [((2 * half, width), kind)] + [((half, width), BF)] * (kind == BF)
    return call(
        total_kernel, name, shapes, arrays, scalars=[core.reshape(1)], scratch=[pltpu.VMEM((2 * half, width), F32)]
    )


def traded(value, mask):
    return lax.ppermute(value, SEQ, [(source, source ^ mask) for source in range(lax.axis_size(SEQ))])


def split_traded(value, first, second):
    return lax.ppermute(
        value,
        SEQ,
        [(source, source ^ (2 * (second if source % 2 else first))) for source in range(lax.axis_size(SEQ))],
    )


def layer_traded(value, first, second):
    axes = ("dp", *SEQ)
    count = lax.axis_size(SEQ)
    pairs = []
    for source in range(lax.axis_size(axes)):
        layer, spot = divmod(source, count)
        pairs.append((source, (layer ^ (second if spot % 2 else first)) * count + spot))
    return lax.ppermute(value, axes, pairs)


def from_siblings(levels, top):
    arrived = {}
    for offset in range(1, 2**top):
        height = offset.bit_length()
        if offset == 1:
            arrived[1] = traded(levels[0], 1)
        elif offset % 2 == 0:
            arrived[offset] = traded(levels[height - 1], offset)
        else:
            arrived[offset] = traded(arrived[offset - 1], 1)
    grouped = []
    for height in range(1, top + 1):
        parts = [arrived[offset] for offset in range(2 ** (height - 1), 2**height)]
        if parts[0].shape[0] < 16:
            parts = [jnp.concatenate(parts, axis=0)]
        grouped.append([View(part) for part in parts])
    return grouped


def shards(queries, key_rows, value_rows, head_scale, out_weight, cotangent):
    rows, width = queries.shape[1:]
    heads = head_scale.shape[0]
    top = lax.axis_size(SEQ).bit_length() - 1
    parts = lax.axis_size("dp")
    assert width == HALF * heads and width % LANES == 0 and width <= 4 * LANES
    paired = top == 3 and parts == 4 and rows == 256
    whole = (rows, width)
    wide = width + LANES
    sizes = [rows >> height for height in range(top + 1)]
    if paired:
        places = [(1, 0), (2, 0), (1, sizes[1])]
        pooled = [sizes[1] + sizes[3], sizes[2]]
    else:
        places = [(height, 0) for height in range(1, top + 1)]
        pooled = sizes[1:]
    factors, base_rows, *outs = call(
        functools.partial(pool_kernel, top, places),
        "pool",
        [((factor_rows(heads), LANES), F32), ((rows, 3 * width), BF)]
        + [((count, 2 * width), BF) for count in pooled]
        + [((size, width), BF) for size in sizes[1:]],
        [pltpu.with_memory_space_constraint(value, pltpu.HBM) for value in (queries[0], key_rows[0], value_rows[0], head_scale)],
        specs=[HBM] * 4,
        scratch=[pltpu.VMEM(whole, BF)] * 3 + [pltpu.SMEM((heads,), F32), pltpu.SemaphoreType.DMA((4,))],
    )
    levels, level_queries = outs[:-top], [[View(value)] for value in outs[-top:]]
    own = [[View(levels[target - 1], start, sizes[height + 1])] for height, (target, start) in enumerate(places)]
    numer, denom, base_weights, cotan, back = call(
        functools.partial(base_kernel, top),
        "base",
        [(whole, F32), (whole, F32), ((rows, heads * rows), BF), (whole, BF), (whole, BF)],
        [factors, base_rows, cotangent[0], out_weight],
        flops=4 * rows * rows * width * 4,
    )
    if paired:
        within = traded(levels[0], 1)
        across = traded(levels[1], 2)
        (third,) = placed(
            "third_rows",
            [((2 * sizes[3], 2 * width), BF)],
            [(0, 0, [own[2][0]]), (0, sizes[3], [View(within, sizes[1], sizes[3])])],
        )
        split = split_traded(third, 2, 3)
        across, numer = lax.optimization_barrier((across, numer))
        across_too = traded(across, 1)
        split_too = traded(split, 1)
        siblings = [
            [View(within, 0, sizes[1])],
            [View(across), View(across_too)],
            [View(split), View(split_too)],
        ]
    else:
        siblings = from_siblings(levels, top)
    own_rows = width // parts
    half = own_rows // 2
    layer = lax.axis_index("dp").astype(jnp.int32)
    if paired:
        core = lax.axis_index(SEQ).astype(jnp.int32) % 2
        place = jnp.stack([layer, layer ^ (1 + 2 * core), layer ^ (3 - 2 * core), layer ^ 2, core * half])
        grad_places = [(0, 0), (1, 0), (2, 0), (1, sizes[1])]
        grad_shapes = [(rows, wide), (sizes[1] + sizes[3], wide + width), (sizes[2], wide + width)]
        pieces = [
            (0, 0, own_rows, 0, 0),
            (1, 0, own_rows, 1, 0),
            (3, lambda ref: ref[4], half, 1, own_rows),
            (2, 0, own_rows, 2, 0),
            (3, lambda ref: half - ref[4], half, 2, own_rows),
        ]
        shapes = [(own_rows, width), (own_rows + half, width), (own_rows + half, width)]
    else:
        place = (layer + jnp.arange(parts, dtype=jnp.int32)) % parts
        grad_places = [(height, 0) for height in range(top + 1)]
        pieces = [(step, 0, own_rows, step, 0) for step in range(parts)]
        grad_shapes = [(rows, wide)] + [(size, wide + width) for size in sizes[1:]]
        shapes = [(own_rows, width)] * parts
    outs = call(
        functools.partial(forward_kernel, top, parts, pieces),
        "forward",
        [((size, heads * rows // 2), BF) for size in sizes[1:]]
        + [(whole, F32), (whole, F32)]
        + [(shape, BF) for shape in shapes],
        [factors, numer, denom, cotan, back, base_weights],
        views=level_queries + siblings,
        scalars=[place],
        scratch=[pltpu.VMEM((width, width), F32)],
    )
    level_weights, (grad_rows, denom_rows), pieces = outs[:top], outs[top : top + 2], outs[top + 2 :]
    outs = call(
        functools.partial(grads_kernel, grad_places),
        "grads",
        [(shape, BF) for shape in grad_shapes],
        [grad_rows, denom_rows],
        views=level_queries,
        flops=4 * rows * rows * width * 4,
    )

    def own_grads(arrays):
        return [
            [View(arrays[target], start, sizes[height])] for height, (target, start) in enumerate(grad_places) if height
        ]

    near_query, near_key, near_value = call(
        near_kernel,
        "near",
        [(whole, F32)] * 3,
        [factors, base_rows, outs[0], base_weights],
        flops=8 * rows * rows * width * 4,
    )
    (query_grad,) = call(
        functools.partial(far_kernel, top),
        "far",
        [(whole, BF)],
        [factors, near_query, *level_weights],
        views=own_grads(outs) + siblings,
        flops=8 * rows * rows * width,
    )

    def key_call(sibling_grads):
        return call(
            functools.partial(key_kernel, top),
            "key",
            [(whole, BF), (whole, BF)],
            [factors, near_key, near_value],
            views=own + sibling_grads,
            flops=8 * rows * rows * width * 2,
        )

    if paired:
        near, far = outs[1:3]
        mine, send, theirs = pieces
        theirs_in = traded(theirs, 1)
        send_one, send_half = placed(
            "layer_rows",
            [((own_rows, width), BF), ((half, width), BF)],
            [
                (0, 0, [View(send, 0, own_rows), View(theirs_in, 0, own_rows)]),
                (1, 0, [View(send, own_rows), View(theirs_in, own_rows)]),
            ],
        )
        near, far, send_one = lax.optimization_barrier((near, far, send_one))
        near_in = traded(near, 1)
        far_in = traded(far, 2)
        layer_one = layer_traded(send_one, 1, 3)
        layer_half = layer_traded(send_half, 2, 2)
        (third,) = placed(
            "third_grads",
            [((2 * sizes[3], wide + width), BF)],
            [(0, 0, [View(near, sizes[1])]), (0, sizes[3], [View(near_in, sizes[1])])],
        )
        third_in = split_traded(third, 2, 3)
        far_in, near_query = lax.optimization_barrier((far_in, near_query))
        far_too = traded(far_in, 1)
        layer_one, query_grad = lax.optimization_barrier((layer_one, query_grad))
        third_too = traded(third_in, 1)
        sibling_grads = [
            [View(near_in, 0, sizes[1])],
            [View(far_in), View(far_too)],
            [View(third_in), View(third_too)],
        ]
        (joint,) = placed(
            "layer_sum",
            [((own_rows + half, width), BF)],
            [(0, 0, [View(mine), View(layer_one)]), (0, own_rows, [View(layer_half)])],
        )
        joint_in = traded(joint, 1)
        weight, weight_half = chip_total("layer_total", core, [joint, joint_in], half, BF)
        plane_one = split_traded(weight, 1, 2)
        plane_half = traded(weight_half, 6)
        key_grad, value_grad = key_call(sibling_grads)
        plane_one, key_grad = lax.optimization_barrier((plane_one, key_grad))
        (joint,) = placed(
            "plane_rows",
            [((own_rows + half, width), BF)],
            [(0, 0, [View(plane_one)]), (0, own_rows, [View(plane_half)])],
        )
        joint_in = traded(joint, 1)
        query_grad, key_grad, value_grad = flush(query_grad, key_grad, value_grad)
        joint_in, key_grad = lax.optimization_barrier((joint_in, key_grad))
        (weight,) = chip_total("weight_out", core, [joint, joint_in, weight], half, F32)
    else:
        weight = pieces[0].astype(F32)
        for step in range(1, parts):
            weight = weight + lax.ppermute(
                pieces[step], "dp", [(source, (source + step) % parts) for source in range(parts)]
            ).astype(F32)
        sibling_grads = from_siblings(outs[1 : top + 1], top)
        bit = 1
        while bit < top:
            weight = weight.astype(BF)
            group = [weight] + [traded(weight, mask << bit) for mask in range(1, 2 ** min(2, top - bit))]
            weight = sum(value.astype(F32) for value in group)
            bit += 2
        weight = weight.astype(BF)
        weight = weight.astype(F32) + traded(weight, 1).astype(F32)
        key_grad, value_grad = key_call(sibling_grads)
    return query_grad[None], key_grad[None], value_grad[None], weight


def solution(mesh):
    spread = P("dp", SEQ, None)
    return jax.shard_map(
        shards,
        mesh=mesh,
        in_specs=(spread, spread, spread, P(), P(), spread),
        out_specs=(spread, spread, spread, P("dp", None)),
        check_vma=False,
    )
```

```python
import functools
import math

import jax
import jax.numpy as jnp
from jax import lax
from jax.experimental import pallas as pl
from jax.experimental.pallas import tpu as pltpu
from jax.sharding import PartitionSpec as P

BF = jnp.bfloat16
F32 = jnp.float32
SEQ = ("seqhi", "seqlo")
LANES = 128
HALF = 64
READY = 2
SMALL, BYTES, LARGE = 1, 10000, 1
LOG2E = math.log2(math.e)
NN = (((1,), (0,)), ((), ()))
NT = (((1,), (1,)), ((), ()))
TN = (((0,), (0,)), ((), ()))


def dot(left, right, dims=NN):
    return lax.dot_general(left, right, dims, preferred_element_type=F32)


def iota(shape, dim):
    return lax.broadcasted_iota(jnp.int32, shape, dim)


def order_matrix(rows, top, inverse=False):
    source = iota((rows, rows), 0 if inverse else 1)
    place = source >> top
    for bit in range(top):
        place = place + ((source >> bit) & 1) * (rows >> (bit + 1))
    return jnp.where(place == iota((rows, rows), 1 if inverse else 0), 1.0, 0.0).astype(BF)


def side_masks():
    lane = iota((1, LANES), 1)
    low = jnp.where(lane < HALF, 1.0, 0.0)
    return low.astype(BF), (1.0 - low).astype(BF)


def factor_rows(heads):
    return -(-(heads + heads // 2) // 8) * 8


def fill_factors(scale_ref, factor_ref):
    heads = scale_ref.shape[0]
    lane = iota((1, LANES), 1)
    for head in range(heads):
        factor_ref[head : head + 1, :] = jnp.full((1, LANES), scale_ref[head] * (HALF**-0.5 * LOG2E), F32)
    for pair in range(heads // 2):
        both = jnp.where(lane < HALF, scale_ref[2 * pair], scale_ref[2 * pair + 1]) * (HALF**-0.5)
        factor_ref[heads + pair : heads + pair + 1, :] = both


def exponent(factor_ref, head, columns):
    return stack([factor_ref[head : head + 1, :]] * (columns // LANES), 1)


def side_factor(factor_ref, heads, pair):
    return factor_ref[heads + pair : heads + pair + 1, :]


def stack(parts, axis):
    return parts[0] if len(parts) == 1 else jnp.concatenate(parts, axis=axis)


def doubled(value):
    return jnp.concatenate([value, value], axis=0)


def halves_sum(value):
    half = value.shape[0] // 2
    return value[:half] + value[half:]


def lane_pair(offset, pair):
    return slice(offset + LANES * pair, offset + LANES * (pair + 1))


def slot_masks(pair):
    lane = iota((1, LANES), 1)
    masks = []
    for side in (0, 1):
        slot = lane - side * HALF
        hit = (slot == 16 * pair) | (slot == 16 * pair + 8)
        masks.append(jnp.where(hit, 1.0, 0.0).astype(BF))
    return masks


def denom_lanes(denoms):
    lane = iota((1, LANES), 1)
    slot = (lane % HALF) // 8
    packed = jnp.zeros(denoms[0].shape, F32)
    for pair, value in enumerate(denoms):
        high = value.astype(BF).astype(F32)
        packed = jnp.where(slot == 2 * pair, high, packed)
        packed = jnp.where(slot == 2 * pair + 1, value - high, packed)
    return packed.astype(BF)


class View:
    def __init__(self, array, start=0, rows=None):
        self.array = array
        self.start = start
        self.rows = array.shape[0] - start if rows is None else rows


VMEM = pl.BlockSpec(memory_space=pltpu.VMEM)
SMEM = pl.BlockSpec(memory_space=pltpu.SMEM)
HBM = pl.BlockSpec(memory_space=pltpu.HBM)


def call(kernel, name, shapes, arrays, views=(), scalars=(), flops=SMALL, scratch=(), specs=None, out_specs=None):
    unique, where = [], []
    for group in views:
        places = []
        for view in group:
            spot = next((at for at, array in enumerate(unique) if array is view.array), None)
            if spot is None:
                spot = len(unique)
                unique.append(view.array)
            places.append((spot, view.start, view.rows))
        where.append(places)

    def body(*refs):
        scalar_refs, refs = refs[: len(scalars)], refs[len(scalars) :]
        array_refs, refs = refs[: len(arrays)], refs[len(arrays) :]
        view_refs, refs = refs[: len(unique)], refs[len(unique) :]

        def load(group, columns):
            return stack(
                [view_refs[spot][start : start + rows, columns] for spot, start, rows in where[group]], 0
            )

        kernel(load, *scalar_refs, *array_refs, *refs)

    return pl.pallas_call(
        body,
        out_shape=[jax.ShapeDtypeStruct(shape, kind) for shape, kind in shapes],
        in_specs=[SMEM] * len(scalars) + (specs or [VMEM] * len(arrays)) + [VMEM] * len(unique),
        out_specs=out_specs or [VMEM] * len(shapes),
        scratch_shapes=list(scratch),
        compiler_params=pltpu.CompilerParams(vmem_limit_bytes=16 * 2**20),
        cost_estimate=pl.CostEstimate(flops=flops, transcendentals=0, bytes_accessed=BYTES),
        name=name,
    )(*scalars, *arrays, *unique)


def pool_kernel(top, starts, places, load, q_hbm, k_hbm, v_hbm, scale_hbm, factor_ref, rows_ref, *refs):
    level_refs, (q_ref, k_ref, v_ref, scale_ref, sems) = refs[:-5], refs[-5:]
    copies = [
        pltpu.make_async_copy(source, target, sems.at[index])
        for index, (source, target) in enumerate(
            ((q_hbm, q_ref), (k_hbm, k_ref), (v_hbm, v_ref), (scale_hbm, scale_ref))
        )
    ]
    for which in (1, 2, 0, 3):
        copies[which].start()
    rows, width = q_ref.shape
    order = order_matrix(rows, top)
    for which, ref in ((1, k_ref), (2, v_ref), (0, q_ref)):
        copies[which].wait()
        current = dot(order, ref[...])
        columns = slice(which * width, (which + 1) * width)
        rows_ref[:rows, columns] = current.astype(BF)
        for height in range(1, top + 1):
            total = halves_sum(current)
            rounded = (total if which == 2 else 0.5 * total).astype(BF)
            rows_ref[starts[height] : starts[height] + rounded.shape[0], columns] = rounded
            if which:
                target, start = places[height - 1]
                span = slice(start, start + rounded.shape[0])
                level_refs[target][span, (which - 1) * width : which * width] = rounded
            current = rounded.astype(F32)
    copies[3].wait()
    fill_factors(scale_ref, factor_ref)


def masked_stack(value, masks):
    return stack([value * mask for mask in masks], 0)


def both_weights(factor_ref, pair, first, second, masks):
    rows = first.shape[0]
    logits = dot(masked_stack(first, masks), second, NT)
    columns = second.shape[0]
    return [
        jnp.exp2(logits[side * rows : (side + 1) * rows] * exponent(factor_ref, 2 * pair + side, columns))
        for side in (0, 1)
    ]


def attend(factor_ref, pair, queries, keys, values, amount, masks):
    weights = both_weights(factor_ref, pair, queries, keys, masks)
    joined = stack([weight.astype(BF) for weight in weights], 1)
    count = jnp.full(values.shape, float(amount), BF)
    right = stack([stack([values * mask, count * mask], 1) for mask in masks], 0)
    return joined, dot(joined, right)


def block(pair, span):
    return slice(span * pair, span * (pair + 1))


def base_kernel(top, load, factor_ref, x_ref, cot_hbm, w_hbm, sums_ref, weights_ref, back_ref, cot_ref, w_ref, sems):
    copies = [
        pltpu.make_async_copy(cot_hbm, cot_ref, sems.at[0]),
        pltpu.make_async_copy(w_hbm, w_ref, sems.at[1]),
    ]
    for copy in copies:
        copy.start()
    rows, width = cot_ref.shape
    masks = side_masks()
    for pair in range(width // LANES):
        q, k, v = (x_ref[:rows, lane_pair(width * which, pair)] for which in range(3))
        joined, both = attend(factor_ref, pair, q, k, v, 1, masks)
        sums_ref[:, block(pair, 2 * LANES)] = both
        weights_ref[:, block(pair, 2 * rows)] = joined
    order = order_matrix(rows, top)
    copies[0].wait()
    cotan = dot(order, cot_ref[...]).astype(BF)
    copies[1].wait()
    back_ref[:, width:] = cotan
    back_ref[:, :width] = dot(cotan, w_ref[...], NT).astype(BF)


def level_kernel(height, load, factor_ref, sums_ref, weights_ref, total_ref):
    width = sums_ref.shape[1] // 2
    masks = side_masks()
    for pair in range(width // LANES):
        keys, values = (load(1, lane_pair(start, pair)) for start in (0, width))
        joined, both = attend(factor_ref, pair, load(0, lane_pair(0, pair)), keys, values, 2**height, masks)
        weights_ref[:, block(pair, joined.shape[1])] = joined
        for _ in range(height):
            both = doubled(both)
        total_ref[:, block(pair, 2 * LANES)] = sums_ref[:, block(pair, 2 * LANES)] + both


def forward_kernel(
    top, ready, parts, pieces, load, place_ref, factor_ref, sums_ref, back_ref, *refs
):
    weights_refs, refs = refs[: top - ready], refs[top - ready :]
    (grad_ref, slope_ref), out_refs, weight_ref = refs[:2], refs[2:-1], refs[-1]
    rows, width = grad_ref.shape
    masks = side_masks()
    lane = iota((LANES, LANES), 1)
    ones = jnp.where(lane // HALF == iota((LANES, LANES), 0) // HALF, 1.0, 0.0).astype(BF)
    adder = doubled(ones)
    attended = []
    for pair in range(width // LANES):
        total = None
        for at in range(top - ready - 1, -1, -1):
            queries = load(at, lane_pair(0, pair))
            keys, values = (load(top - ready + at, lane_pair(start, pair)) for start in (0, width))
            joined, both = attend(factor_ref, pair, queries, keys, values, 2 ** (ready + at + 1), masks)
            columns = joined.shape[1]
            weights_refs[at][:, columns * pair : columns * (pair + 1)] = joined
            total = both if total is None else both + doubled(total)
        for _ in range(ready + 1):
            total = doubled(total)
        total = total + sums_ref[:, block(pair, 2 * LANES)]
        numer = total[:, :LANES]
        inverse = 1.0 / total[:, LANES:]
        ratio = numer * inverse
        attended.append(ratio.astype(BF))
        back = back_ref[:, lane_pair(0, pair)].astype(F32)
        product = back * ratio
        product_high = product.astype(BF)
        product_low = (product - product_high.astype(F32)).astype(BF)
        summed = dot(stack([product_high, product_low], 1), adder)
        grad_ref[:, lane_pair(0, pair)] = back * inverse
        slope_ref[:, lane_pair(0, pair)] = -summed * inverse
    weight_ref[...] = dot(stack(attended, 1), back_ref[:, width:], TN)
    own_rows = width // parts
    for entry, offset, count, target, start in pieces:
        shift = offset if isinstance(offset, int) else offset(place_ref)
        first = pl.multiple_of(place_ref[entry] * own_rows + shift, math.gcd(own_rows, count))
        out_refs[target][start : start + count, :] = weight_ref[pl.ds(first, count), :].astype(BF)


def grads_kernel(grad_places, load, grad_ref, slope_ref, *out_refs):
    rows, width = grad_ref.shape
    grad_rows = [grad_ref[:, lane_pair(0, pair)] for pair in range(width // LANES)]
    denom_rows = [slope_ref[:, lane_pair(0, pair)] for pair in range(width // LANES)]
    for height, (target, start) in enumerate(grad_places):
        if height:
            grad_rows = [halves_sum(value) for value in grad_rows]
            denom_rows = [halves_sum(value) for value in denom_rows]
        span = slice(start, start + (rows >> height))
        for pair, value in enumerate(grad_rows):
            out_refs[target][span, lane_pair(0, pair)] = value.astype(BF)
        out_refs[target][span, width : width + LANES] = denom_lanes(denom_rows)
        if height:
            out_refs[target][span, width + LANES :] = load(height - 1, slice(0, width))


def query_slopes(joined, grad, denom, values, pair, height, masks):
    rows, columns = grad.shape[0], values.shape[0]
    left = stack([stack([grad * mask, denom * slot], 1) for mask, slot in zip(masks, slot_masks(pair))], 0)
    right = stack([values, jnp.full((columns, LANES), float(2**height), BF)], 1)
    product = dot(left, right, NT)
    return [
        (joined[:, side * columns : (side + 1) * columns].astype(F32) * product[side * rows : (side + 1) * rows])
        .astype(BF)
        for side in (0, 1)
    ]


def near_kernel(load, factor_ref, x_ref, gh_ref, weights_ref, query_ref, key_ref, value_ref):
    rows, width = query_ref.shape
    heads = width // HALF
    masks = side_masks()
    for pair in range(width // LANES):
        factor = side_factor(factor_ref, heads, pair)
        queries, keys, values = (x_ref[:rows, lane_pair(width * which, pair)] for which in range(3))
        grad = gh_ref[:, lane_pair(0, pair)]
        joined = weights_ref[:, 2 * rows * pair : 2 * rows * (pair + 1)]
        slope = query_slopes(joined, grad, gh_ref[:, width:], values, pair, 0, masks)
        query_ref[:, lane_pair(0, pair)] = dot(stack(slope, 1), masked_stack(keys, masks)) * factor
        key_ref[:, lane_pair(0, pair)] = dot(stack(slope, 0), masked_stack(queries, masks), TN) * factor
        weights = stack([joined[:, :rows], joined[:, rows:]], 0)
        value_ref[:, lane_pair(0, pair)] = dot(weights, masked_stack(grad, masks), TN)


def far_kernel(top, load, factor_ref, base_ref, *refs):
    weights_refs, out_ref = refs[:top], refs[top]
    rows, width = out_ref.shape
    heads = width // HALF
    masks = side_masks()
    results = []
    for pair in range(width // LANES):
        factor = side_factor(factor_ref, heads, pair)
        total = None
        for height in range(top, 0, -1):
            grad = load(height - 1, lane_pair(0, pair))
            denom = load(height - 1, slice(width, width + LANES))
            keys, values = (load(top + height - 1, lane_pair(start, pair)) for start in (0, width))
            columns = 2 * keys.shape[0]
            joined = weights_refs[height - 1][:, columns * pair : columns * (pair + 1)]
            slope = query_slopes(joined, grad, denom, values, pair, height, masks)
            piece = dot(stack(slope, 1), masked_stack(keys, masks)) * factor
            total = piece if total is None else piece + 0.5 * doubled(total)
        total = base_ref[:, lane_pair(0, pair)] + 0.5 * doubled(total)
        results.append(total.astype(BF))
    out_ref[...] = dot(order_matrix(rows, top, True), stack(results, 1)).astype(BF)


def key_kernel(top, first, last, load, factor_ref, base_key_ref, base_value_ref, key_out_ref, value_out_ref):
    rows, width = key_out_ref.shape
    heads = width // HALF
    masks = side_masks()
    levels = last - first + 1
    key_results, value_results = [], []
    for pair in range(width // LANES):
        factor = side_factor(factor_ref, heads, pair)
        key_total = value_total = None
        for at in range(levels - 1, -1, -1):
            keys, values = (load(at, lane_pair(start, pair)) for start in (width, 2 * width))
            grad = load(levels + at, lane_pair(0, pair))
            denom = load(levels + at, slice(width, width + LANES))
            queries = load(levels + at, lane_pair(width + LANES, pair))
            count = keys.shape[0]
            weights = both_weights(factor_ref, pair, keys, queries, masks)
            left = stack(
                [
                    stack([values * mask, jnp.broadcast_to(slot * float(2 ** (first + at)), (count, LANES))], 1)
                    for mask, slot in zip(masks, slot_masks(pair))
                ],
                0,
            )
            product = dot(left, stack([grad, denom], 1), NT)
            slope = [
                (weight * product[side * count : (side + 1) * count]).astype(BF)
                for side, weight in enumerate(weights)
            ]
            key_piece = dot(stack(slope, 1), masked_stack(queries, masks)) * factor
            value_piece = dot(stack([weight.astype(BF) for weight in weights], 1), masked_stack(grad, masks))
            if key_total is not None:
                key_piece = key_piece + 0.5 * doubled(key_total)
                value_piece = value_piece + doubled(value_total)
            key_total, value_total = key_piece, value_piece
        for _ in range(first):
            key_total, value_total = 0.5 * doubled(key_total), doubled(value_total)
        key_results.append(base_key_ref[:, lane_pair(0, pair)] + key_total)
        value_results.append(base_value_ref[:, lane_pair(0, pair)] + value_total)
    key_total, value_total = stack(key_results, 1), stack(value_results, 1)
    if last == top:
        back = order_matrix(rows, top, True)
        key_total, value_total = dot(back, key_total.astype(BF)), dot(back, value_total.astype(BF))
    key_out_ref[...] = key_total.astype(key_out_ref.dtype)
    value_out_ref[...] = value_total.astype(value_out_ref.dtype)


def place_kernel(spots, load, *refs):
    for target, start, groups in spots:
        total = None
        for group in groups:
            value = load(group, slice(None))
            if len(groups) > 1 or refs[target].dtype == F32:
                value = value.astype(F32)
            total = value if total is None else total + value
        refs[target][start : start + total.shape[0], :] = total.astype(refs[target].dtype)


def flush_kernel(load, *refs):
    count = (len(refs) - 1) // 2
    copies = [
        pltpu.make_async_copy(refs[at], refs[count + at], refs[-1].at[at]) for at in range(count)
    ]
    for copy in copies:
        copy.start()
    for copy in copies:
        copy.wait()


def flush(*arrays):
    return call(
        flush_kernel,
        "flush",
        [(array.shape, array.dtype) for array in arrays],
        arrays,
        out_specs=[HBM] * len(arrays),
        scratch=[pltpu.SemaphoreType.DMA((len(arrays),))],
    )


def placed(name, shapes, spots, flops=SMALL):
    views, listed = [], []
    for target, start, parts in spots:
        listed.append((target, start, range(len(views), len(views) + len(parts))))
        views += [[part] for part in parts]
    return call(functools.partial(place_kernel, listed), name, shapes, [], views=views, flops=flops)


def total_kernel(load, core_ref, own_ref, partner_ref, *refs):
    half = own_ref.shape[0] // 3
    base_ref = refs[0] if refs[0].shape[0] == 2 * half and len(refs) == 3 and refs[1].dtype == F32 else None
    out_refs = refs[:-1] if base_ref is None else refs[1:-1]
    sum_ref = refs[-1]
    total = own_ref[: 2 * half, :].astype(F32) + partner_ref[: 2 * half, :].astype(F32)
    if base_ref is not None:
        total = total + base_ref[...].astype(F32)
    sum_ref[...] = total
    for ref, core in ((own_ref, core_ref[0]), (partner_ref, 1 - core_ref[0])):
        span = pl.ds(pl.multiple_of(core * half, half), half)
        sum_ref[span, :] = sum_ref[span, :] + ref[2 * half :, :].astype(F32)
    out_refs[0][...] = sum_ref[...].astype(out_refs[0].dtype)
    if len(out_refs) > 1:
        span = pl.ds(pl.multiple_of(core_ref[0] * half, half), half)
        out_refs[1][...] = sum_ref[span, :].astype(BF)


def chip_total(name, core, arrays, half, kind):
    width = arrays[0].shape[1]
    shapes = [((2 * half, width), kind)] + [((half, width), BF)] * (kind == BF)
    return call(
        total_kernel,
        name,
        shapes,
        arrays,
        scalars=[core.reshape(1)],
        flops=LARGE,
        scratch=[pltpu.VMEM((2 * half, width), F32)],
    )


def traded(value, mask):
    return lax.ppermute(value, SEQ, [(source, source ^ mask) for source in range(lax.axis_size(SEQ))])


def split_traded(value, first, second):
    return lax.ppermute(
        value,
        SEQ,
        [(source, source ^ (2 * (second if source % 2 else first))) for source in range(lax.axis_size(SEQ))],
    )


def layer_traded(value, first, second):
    axes = ("dp", *SEQ)
    count = lax.axis_size(SEQ)
    pairs = []
    for source in range(lax.axis_size(axes)):
        layer, spot = divmod(source, count)
        pairs.append((source, (layer ^ (second if spot % 2 else first)) * count + spot))
    return lax.ppermute(value, axes, pairs)


def from_siblings(levels, top):
    arrived = {}
    for offset in range(1, 2**top):
        height = offset.bit_length()
        if offset == 1:
            arrived[1] = traded(levels[0], 1)
        elif offset % 2 == 0:
            arrived[offset] = traded(levels[height - 1], offset)
        else:
            arrived[offset] = traded(arrived[offset - 1], 1)
    grouped = []
    for height in range(1, top + 1):
        parts = [arrived[offset] for offset in range(2 ** (height - 1), 2**height)]
        if parts[0].shape[0] < 16:
            parts = [jnp.concatenate(parts, axis=0)]
        grouped.append([View(part) for part in parts])
    return grouped


def shards(queries, key_rows, value_rows, head_scale, out_weight, cotangent):
    rows, width = queries.shape[1:]
    heads = head_scale.shape[0]
    top = lax.axis_size(SEQ).bit_length() - 1
    parts = lax.axis_size("dp")
    assert width == HALF * heads and width % LANES == 0 and width <= 4 * LANES
    paired = top == 3 and parts == 4 and rows == 256
    whole = (rows, width)
    wide = width + LANES
    sizes = [rows >> height for height in range(top + 1)]
    starts = [0]
    for size in sizes:
        starts.append(starts[-1] + max(size, 16))
    if paired:
        places, messages = [(0, 0), (1, 0), (0, sizes[1])], [sizes[1] + sizes[3], sizes[2]]
    else:
        places, messages = [(height, 0) for height in range(top)], sizes[1:]
    factors, own_rows_all, *levels = call(
        functools.partial(pool_kernel, top, starts, places),
        "pool",
        [((factor_rows(heads), LANES), F32), ((starts[-1], 3 * width), BF)]
        + [((count, 2 * width), BF) for count in messages],
        [
            pltpu.with_memory_space_constraint(value, pltpu.HBM)
            for value in (queries[0], key_rows[0], value_rows[0], head_scale)
        ],
        specs=[HBM] * 4,
        scratch=[pltpu.VMEM(whole, BF)] * 3 + [pltpu.SMEM((heads,), F32), pltpu.SemaphoreType.DMA((4,))],
    )
    own = [[View(own_rows_all, starts[height], sizes[height])] for height in range(1, top + 1)]
    sums, base_weights, back = call(
        functools.partial(base_kernel, top),
        "base",
        [((rows, 2 * width), F32), ((rows, heads * rows), BF), ((rows, 2 * width), BF)],
        [factors, own_rows_all]
        + [pltpu.with_memory_space_constraint(value, pltpu.HBM) for value in (cotangent[0], out_weight)],
        specs=[VMEM, VMEM, HBM, HBM],
        scratch=[pltpu.VMEM(whole, BF), pltpu.VMEM((width, width), BF), pltpu.SemaphoreType.DMA((2,))],
        flops=100000000,
    )

    def attend_level(height, views, sums):
        return call(
            functools.partial(level_kernel, height),
            "level",
            [((sizes[height], heads * rows // 2), BF), ((rows, 2 * width), F32)],
            [factors, sums],
            views=[own[height - 1], views],
            flops=100000000//4,
        )

    if paired:
        within = traded(levels[0], 1)
        across = traded(levels[1], 2)
        (third,) = placed(
            "third_rows",
            [((2 * sizes[3], 2 * width), BF)],
            [(0, 0, [View(levels[0], sizes[1])]), (0, sizes[3], [View(within, sizes[1])])],
        )
        split = split_traded(third, 2, 3)
        level_weights = []
        if READY > 0:
            weights, sums = attend_level(1, [View(within, 0, sizes[1])], sums)
            level_weights.append(weights)
        across, sums = lax.optimization_barrier((across, sums))
        across_too = traded(across, 1)
        split_too = traded(split, 1)
        if READY > 1:
            weights, sums = attend_level(2, [View(across), View(across_too)], sums)
            level_weights.append(weights)
            split_too, sums = lax.optimization_barrier((split_too, sums))
        siblings = [[View(within, 0, sizes[1])], [View(across), View(across_too)], [View(split), View(split_too)]]
    else:
        siblings = from_siblings(levels, top)
        level_weights = []
    ready = len(level_weights)
    own_rows = width // parts
    half = own_rows // 2
    layer = lax.axis_index("dp").astype(jnp.int32)
    if paired:
        core = lax.axis_index(SEQ).astype(jnp.int32) % 2
        place = jnp.stack([layer, layer ^ (2 + core), layer ^ (3 - core), layer ^ 1, core * half])
        grad_places = [(0, 0), (1, 0), (2, 0), (1, sizes[1])]
        grad_shapes = [(rows, wide), (sizes[1] + sizes[3], wide + width), (sizes[2], wide + width)]
        pieces = [
            (0, 0, own_rows, 0, 0),
            (1, 0, own_rows, 1, 0),
            (3, lambda ref: ref[4], half, 1, own_rows),
            (2, 0, own_rows, 2, 0),
            (3, lambda ref: half - ref[4], half, 2, own_rows),
        ]
        shapes = [(own_rows, width), (own_rows + half, width), (own_rows + half, width)]
    else:
        place = (layer + jnp.arange(parts, dtype=jnp.int32)) % parts
        grad_places = [(height, 0) for height in range(top + 1)]
        pieces = [(step, 0, own_rows, step, 0) for step in range(parts)]
        grad_shapes = [(rows, wide)] + [(size, wide + width) for size in sizes[1:]]
        shapes = [(own_rows, width)] * parts
    outs = call(
        functools.partial(forward_kernel, top, ready, parts, pieces),
        "forward",
        [((size, heads * rows // 2), BF) for size in sizes[ready + 1 :]]
        + [(whole, F32), (whole, F32)]
        + [(shape, BF) for shape in shapes],
        [factors, sums, back],
        views=own[ready:] + siblings[ready:] + siblings[:ready],
        scalars=[place],
        scratch=[pltpu.VMEM((width, width), F32)],
    )
    level_weights += outs[: top - ready]
    outs = outs[top - ready :]
    (grad_rows, denom_rows), pieces = outs[:2], outs[2:]
    outs = call(
        functools.partial(grads_kernel, grad_places),
        "grads",
        [(shape, BF) for shape in grad_shapes],
        [grad_rows, denom_rows],
        views=own,
        flops=100000000,
    )

    def own_grads(arrays):
        return [
            [View(arrays[target], start, sizes[height])] for height, (target, start) in enumerate(grad_places) if height
        ]

    near_query, near_key, near_value = call(
        near_kernel,
        "near",
        [(whole, F32)] * 3,
        [factors, own_rows_all, outs[0], base_weights],
        flops=1600000000,
    )
    (query_grad,) = call(
        functools.partial(far_kernel, top),
        "far",
        [(whole, BF)],
        [factors, near_query, *level_weights],
        views=own_grads(outs) + siblings,
        flops=100000000,
    )

    def key_call(first, last, sums, sibling_grads, kind):
        return call(
            functools.partial(key_kernel, top, first, last),
            "key",
            [(whole, kind), (whole, kind)],
            [factors, *sums],
            views=own[first - 1 : last] + sibling_grads,
            flops=100000000,
        )

    if paired:
        near, far = outs[1:3]
        mine, send, theirs = pieces
        theirs_in = traded(theirs, 1)
        send_one, send_half = placed(
            "layer_rows",
            [((own_rows, width), BF), ((half, width), BF)],
            [
                (0, 0, [View(send, 0, own_rows), View(theirs_in, 0, own_rows)]),
                (1, 0, [View(send, own_rows), View(theirs_in, own_rows)]),
            ],
            flops=LARGE,
        )
        near_in = traded(near, 1)
        far_in = traded(far, 2)
        layer_one = layer_traded(send_one, 2, 3)
        layer_half = layer_traded(send_half, 1, 1)
        (third,) = placed(
            "third_grads",
            [((2 * sizes[3], wide + width), BF)],
            [(0, 0, [View(near, sizes[1])]), (0, sizes[3], [View(near_in, sizes[1])])],
        )
        third_in = split_traded(third, 2, 3)
        layer_one, layer_half, near_key = lax.optimization_barrier((layer_one, layer_half, near_key))
        (joint,) = placed(
            "layer_sum",
            [((own_rows + half, width), BF)],
            [(0, 0, [View(mine), View(layer_one)]), (0, own_rows, [View(layer_half)])],
            flops=LARGE,
        )
        joint_in = traded(joint, 1)
        far_in, near_key = lax.optimization_barrier((far_in, near_key))
        far_too = traded(far_in, 1)
        near_sums = key_call(1, 1, (near_key, near_value), [[View(near_in, 0, sizes[1])]], F32)
        joint_in, near_sums = lax.optimization_barrier((joint_in, tuple(near_sums)))
        weight, weight_half = chip_total("layer_total", core, [joint, joint_in], half, BF)
        third_in, _ = lax.optimization_barrier((third_in, weight))
        third_too = traded(third_in, 1)
        sibling_grads = [[View(far_in), View(far_too)], [View(third_in), View(third_too)]]
        plane_one = split_traded(weight, 2, 3)
        plane_half = traded(weight_half, 2)
        key_grad, value_grad = key_call(2, top, near_sums, sibling_grads, BF)
        plane_one, key_grad, query_grad = lax.optimization_barrier((plane_one, key_grad, query_grad))
        (joint,) = placed(
            "plane_rows",
            [((own_rows + half, width), BF)],
            [(0, 0, [View(plane_one)]), (0, own_rows, [View(plane_half)])],
            flops=LARGE,
        )
        joint_in = traded(joint, 1)
        query_grad, key_grad, value_grad = flush(query_grad, key_grad, value_grad)
        joint_in, key_grad = lax.optimization_barrier((joint_in, key_grad))
        (weight,) = chip_total("weight_out", core, [joint, joint_in, weight], half, F32)
    else:
        weight = pieces[0].astype(F32)
        for step in range(1, parts):
            weight = weight + lax.ppermute(
                pieces[step], "dp", [(source, (source + step) % parts) for source in range(parts)]
            ).astype(F32)
        sibling_grads = from_siblings(outs[1 : top + 1], top)
        bit = 1
        while bit < top:
            weight = weight.astype(BF)
            group = [weight] + [traded(weight, mask << bit) for mask in range(1, 2 ** min(2, top - bit))]
            weight = sum(value.astype(F32) for value in group)
            bit += 2
        weight = weight.astype(BF)
        weight = weight.astype(F32) + traded(weight, 1).astype(F32)
        key_grad, value_grad = key_call(1, top, (near_key, near_value), sibling_grads, BF)
    return query_grad[None], key_grad[None], value_grad[None], weight


def solution(mesh):
    spread = P("dp", SEQ, None)
    return jax.shard_map(
        shards,
        mesh=mesh,
        in_specs=(spread, spread, spread, P(), P(), spread),
        out_specs=(spread, spread, spread, P("dp", None)),
        check_vma=False,
    )
```

```python
import functools
import math

import jax
import jax.numpy as jnp
from jax import lax
from jax.experimental import pallas as pl
from jax.experimental.pallas import tpu as pltpu
from jax.sharding import PartitionSpec as P

BF = jnp.bfloat16
F32 = jnp.float32
SEQ = ("seqhi", "seqlo")
LANES = 128
HALF = 64
READY = 2
SMALL, BYTES, LARGE = 1, 10000, 1
LOG2E = math.log2(math.e)
NN = (((1,), (0,)), ((), ()))
NT = (((1,), (1,)), ((), ()))
TN = (((0,), (0,)), ((), ()))


def dot(left, right, dims=NN):
    return lax.dot_general(left, right, dims, preferred_element_type=F32)


def iota(shape, dim):
    return lax.broadcasted_iota(jnp.int32, shape, dim)


def order_matrix(rows, top, inverse=False):
    source = iota((rows, rows), 0 if inverse else 1)
    place = source >> top
    for bit in range(top):
        place = place + ((source >> bit) & 1) * (rows >> (bit + 1))
    return jnp.where(place == iota((rows, rows), 1 if inverse else 0), 1.0, 0.0).astype(BF)


def side_masks():
    lane = iota((1, LANES), 1)
    low = jnp.where(lane < HALF, 1.0, 0.0)
    return low.astype(BF), (1.0 - low).astype(BF)


def factor_rows(heads):
    return -(-(heads + heads // 2) // 8) * 8


def fill_factors(scale_ref, factor_ref):
    heads = scale_ref.shape[0]
    lane = iota((1, LANES), 1)
    for head in range(heads):
        factor_ref[head : head + 1, :] = jnp.full((1, LANES), scale_ref[head] * (HALF**-0.5 * LOG2E), F32)
    for pair in range(heads // 2):
        both = jnp.where(lane < HALF, scale_ref[2 * pair], scale_ref[2 * pair + 1]) * (HALF**-0.5)
        factor_ref[heads + pair : heads + pair + 1, :] = both


def exponent(factor_ref, head, columns):
    return stack([factor_ref[head : head + 1, :]] * (columns // LANES), 1)


def side_factor(factor_ref, heads, pair):
    return factor_ref[heads + pair : heads + pair + 1, :]


def stack(parts, axis):
    return parts[0] if len(parts) == 1 else jnp.concatenate(parts, axis=axis)


def doubled(value):
    return jnp.concatenate([value, value], axis=0)


def halves_sum(value):
    half = value.shape[0] // 2
    return value[:half] + value[half:]


def lane_pair(offset, pair):
    return slice(offset + LANES * pair, offset + LANES * (pair + 1))


def slot_masks(pair):
    lane = iota((1, LANES), 1)
    masks = []
    for side in (0, 1):
        slot = lane - side * HALF
        hit = (slot == 16 * pair) | (slot == 16 * pair + 8)
        masks.append(jnp.where(hit, 1.0, 0.0).astype(BF))
    return masks


def denom_lanes(denoms):
    lane = iota((1, LANES), 1)
    slot = (lane % HALF) // 8
    packed = jnp.zeros(denoms[0].shape, F32)
    for pair, value in enumerate(denoms):
        high = value.astype(BF).astype(F32)
        packed = jnp.where(slot == 2 * pair, high, packed)
        packed = jnp.where(slot == 2 * pair + 1, value - high, packed)
    return packed.astype(BF)


class View:
    def __init__(self, array, start=0, rows=None):
        self.array = array
        self.start = start
        self.rows = array.shape[0] - start if rows is None else rows


VMEM = pl.BlockSpec(memory_space=pltpu.VMEM)
SMEM = pl.BlockSpec(memory_space=pltpu.SMEM)
HBM = pl.BlockSpec(memory_space=pltpu.HBM)


def call(kernel, name, shapes, arrays, views=(), scalars=(), flops=SMALL, scratch=(), specs=None, out_specs=None):
    unique, where = [], []
    for group in views:
        places = []
        for view in group:
            spot = next((at for at, array in enumerate(unique) if array is view.array), None)
            if spot is None:
                spot = len(unique)
                unique.append(view.array)
            places.append((spot, view.start, view.rows))
        where.append(places)

    def body(*refs):
        scalar_refs, refs = refs[: len(scalars)], refs[len(scalars) :]
        array_refs, refs = refs[: len(arrays)], refs[len(arrays) :]
        view_refs, refs = refs[: len(unique)], refs[len(unique) :]

        def load(group, columns):
            return stack(
                [view_refs[spot][start : start + rows, columns] for spot, start, rows in where[group]], 0
            )

        kernel(load, *scalar_refs, *array_refs, *refs)

    return pl.pallas_call(
        body,
        out_shape=[jax.ShapeDtypeStruct(shape, kind) for shape, kind in shapes],
        in_specs=[SMEM] * len(scalars) + (specs or [VMEM] * len(arrays)) + [VMEM] * len(unique),
        out_specs=out_specs or [VMEM] * len(shapes),
        scratch_shapes=list(scratch),
        compiler_params=pltpu.CompilerParams(vmem_limit_bytes=16 * 2**20),
        cost_estimate=pl.CostEstimate(flops=flops, transcendentals=0, bytes_accessed=BYTES),
        name=name,
    )(*scalars, *arrays, *unique)


def pool_kernel(top, starts, places, load, q_hbm, k_hbm, v_hbm, scale_hbm, factor_ref, rows_ref, *refs):
    level_refs, (q_ref, k_ref, v_ref, scale_ref, sems) = refs[:-5], refs[-5:]
    copies = [
        pltpu.make_async_copy(source, target, sems.at[index])
        for index, (source, target) in enumerate(
            ((q_hbm, q_ref), (k_hbm, k_ref), (v_hbm, v_ref), (scale_hbm, scale_ref))
        )
    ]
    for which in (1, 2, 0, 3):
        copies[which].start()
    rows, width = q_ref.shape
    order = order_matrix(rows, top)
    for which, ref in ((1, k_ref), (2, v_ref), (0, q_ref)):
        copies[which].wait()
        current = dot(order, ref[...])
        columns = slice(which * width, (which + 1) * width)
        rows_ref[:rows, columns] = current.astype(BF)
        for height in range(1, top + 1):
            total = halves_sum(current)
            rounded = (total if which == 2 else 0.5 * total).astype(BF)
            rows_ref[starts[height] : starts[height] + rounded.shape[0], columns] = rounded
            if which:
                target, start = places[height - 1]
                span = slice(start, start + rounded.shape[0])
                level_refs[target][span, (which - 1) * width : which * width] = rounded
            current = rounded.astype(F32)
    copies[3].wait()
    fill_factors(scale_ref, factor_ref)


def masked_stack(value, masks):
    return stack([value * mask for mask in masks], 0)


def both_weights(factor_ref, pair, first, second, masks):
    rows = first.shape[0]
    logits = dot(masked_stack(first, masks), second, NT)
    columns = second.shape[0]
    return [
        jnp.exp2(logits[side * rows : (side + 1) * rows] * exponent(factor_ref, 2 * pair + side, columns))
        for side in (0, 1)
    ]


def attend(factor_ref, items, masks):
    weights = [
        stack([weight.astype(BF) for weight in both_weights(factor_ref, pair, queries, keys, masks)], 1)
        for pair, queries, keys, _, _ in items
    ]
    results = []
    for joined, (_, _, _, values, amount) in zip(weights, items):
        count = jnp.full(values.shape, float(amount), BF)
        right = stack([stack([values * mask, count * mask], 1) for mask in masks], 0)
        results.append((joined, dot(joined, right)))
    return results


def block(pair, span):
    return slice(span * pair, span * (pair + 1))


def base_kernel(top, load, factor_ref, x_ref, cot_hbm, w_hbm, sums_ref, weights_ref, back_ref, cot_ref, w_ref, sems):
    copies = [
        pltpu.make_async_copy(cot_hbm, cot_ref, sems.at[0]),
        pltpu.make_async_copy(w_hbm, w_ref, sems.at[1]),
    ]
    for copy in copies:
        copy.start()
    rows, width = cot_ref.shape
    masks = side_masks()
    items = [
        (pair, *(x_ref[:rows, lane_pair(width * which, pair)] for which in range(3)), 1)
        for pair in range(width // LANES)
    ]
    for pair, (joined, both) in enumerate(attend(factor_ref, items, masks)):
        sums_ref[:, block(pair, 2 * LANES)] = both
        weights_ref[:, block(pair, 2 * rows)] = joined
    order = order_matrix(rows, top)
    copies[0].wait()
    cotan = dot(order, cot_ref[...]).astype(BF)
    copies[1].wait()
    back_ref[:, width:] = cotan
    back_ref[:, :width] = dot(cotan, w_ref[...], NT).astype(BF)


def level_kernel(height, load, factor_ref, sums_ref, weights_ref, total_ref):
    width = sums_ref.shape[1] // 2
    masks = side_masks()
    items = [
        (pair, load(0, lane_pair(0, pair)), *(load(1, lane_pair(start, pair)) for start in (0, width)), 2**height)
        for pair in range(width // LANES)
    ]
    for pair, (joined, both) in enumerate(attend(factor_ref, items, masks)):
        weights_ref[:, block(pair, joined.shape[1])] = joined
        for _ in range(height):
            both = doubled(both)
        total_ref[:, block(pair, 2 * LANES)] = sums_ref[:, block(pair, 2 * LANES)] + both


def forward_kernel(
    top, ready, parts, pieces, load, place_ref, factor_ref, sums_ref, back_ref, *refs
):
    weights_refs, refs = refs[: top - ready], refs[top - ready :]
    (grad_ref, slope_ref), out_refs, weight_ref = refs[:2], refs[2:-1], refs[-1]
    rows, width = grad_ref.shape
    masks = side_masks()
    lane = iota((LANES, LANES), 1)
    ones = jnp.where(lane // HALF == iota((LANES, LANES), 0) // HALF, 1.0, 0.0).astype(BF)
    adder = doubled(ones)
    pairs = range(width // LANES)
    spots = [(pair, at) for pair in pairs for at in range(top - ready - 1, -1, -1)]
    items = []
    for pair, at in spots:
        keys, values = (load(top - ready + at, lane_pair(start, pair)) for start in (0, width))
        items.append((pair, load(at, lane_pair(0, pair)), keys, values, 2 ** (ready + at + 1)))
    sums = {}
    for (pair, at), (joined, both) in zip(spots, attend(factor_ref, items, masks)):
        weights_refs[at][:, block(pair, joined.shape[1])] = joined
        sums[pair, at] = both
    attended, inverses, products = [], [], []
    for pair in pairs:
        total = sums[pair, top - ready - 1]
        for at in range(top - ready - 2, -1, -1):
            total = sums[pair, at] + doubled(total)
        for _ in range(ready + 1):
            total = doubled(total)
        total = total + sums_ref[:, block(pair, 2 * LANES)]
        inverse = 1.0 / total[:, LANES:]
        ratio = total[:, :LANES] * inverse
        attended.append(ratio.astype(BF))
        inverses.append(inverse)
        products.append(back_ref[:, lane_pair(0, pair)].astype(F32) * ratio)
    weight_ref[...] = dot(stack(attended, 1), back_ref[:, width:], TN)
    for pair in pairs:
        high = products[pair].astype(BF)
        low = (products[pair] - high.astype(F32)).astype(BF)
        grad_ref[:, lane_pair(0, pair)] = back_ref[:, lane_pair(0, pair)].astype(F32) * inverses[pair]
        slope_ref[:, lane_pair(0, pair)] = -dot(stack([high, low], 1), adder) * inverses[pair]
    own_rows = width // parts
    for entry, offset, count, target, start in pieces:
        shift = offset if isinstance(offset, int) else offset(place_ref)
        first = pl.multiple_of(place_ref[entry] * own_rows + shift, math.gcd(own_rows, count))
        out_refs[target][start : start + count, :] = weight_ref[pl.ds(first, count), :].astype(BF)


def grads_kernel(grad_places, load, grad_ref, slope_ref, *out_refs):
    rows, width = grad_ref.shape
    grad_rows = [grad_ref[:, lane_pair(0, pair)] for pair in range(width // LANES)]
    denom_rows = [slope_ref[:, lane_pair(0, pair)] for pair in range(width // LANES)]
    for height, (target, start) in enumerate(grad_places):
        if height:
            grad_rows = [halves_sum(value) for value in grad_rows]
            denom_rows = [halves_sum(value) for value in denom_rows]
        span = slice(start, start + (rows >> height))
        for pair, value in enumerate(grad_rows):
            out_refs[target][span, lane_pair(0, pair)] = value.astype(BF)
        out_refs[target][span, width : width + LANES] = denom_lanes(denom_rows)
        if height:
            out_refs[target][span, width + LANES :] = load(height - 1, slice(0, width))


def query_slopes(joined, grad, denom, values, pair, height, masks):
    rows, columns = grad.shape[0], values.shape[0]
    left = stack([stack([grad * mask, denom * slot], 1) for mask, slot in zip(masks, slot_masks(pair))], 0)
    right = stack([values, jnp.full((columns, LANES), float(2**height), BF)], 1)
    product = dot(left, right, NT)
    return [
        (joined[:, side * columns : (side + 1) * columns].astype(F32) * product[side * rows : (side + 1) * rows])
        .astype(BF)
        for side in (0, 1)
    ]


def near_kernel(load, factor_ref, x_ref, gh_ref, weights_ref, query_ref, key_ref, value_ref):
    rows, width = query_ref.shape
    heads = width // HALF
    masks = side_masks()
    pairs = range(width // LANES)
    slopes = []
    for pair in pairs:
        values = x_ref[:rows, lane_pair(2 * width, pair)]
        joined = weights_ref[:, block(pair, 2 * rows)]
        grad = gh_ref[:, lane_pair(0, pair)]
        slopes.append(query_slopes(joined, grad, gh_ref[:, width:], values, pair, 0, masks))
    for pair in pairs:
        factor = side_factor(factor_ref, heads, pair)
        keys = x_ref[:rows, lane_pair(width, pair)]
        query_ref[:, lane_pair(0, pair)] = dot(stack(slopes[pair], 1), masked_stack(keys, masks)) * factor
    for pair in pairs:
        joined = weights_ref[:, block(pair, 2 * rows)]
        weights = stack([joined[:, :rows], joined[:, rows:]], 0)
        grad = gh_ref[:, lane_pair(0, pair)]
        value_ref[:, lane_pair(0, pair)] = dot(weights, masked_stack(grad, masks), TN)
    for pair in pairs:
        factor = side_factor(factor_ref, heads, pair)
        queries = x_ref[:rows, lane_pair(0, pair)]
        key_ref[:, lane_pair(0, pair)] = dot(stack(slopes[pair], 0), masked_stack(queries, masks), TN) * factor


def far_kernel(top, load, factor_ref, base_ref, *refs):
    weights_refs, out_ref = refs[:top], refs[top]
    rows, width = out_ref.shape
    heads = width // HALF
    masks = side_masks()
    pairs = range(width // LANES)
    slopes = {}
    for pair in pairs:
        for height in range(top, 0, -1):
            grad = load(height - 1, lane_pair(0, pair))
            denom = load(height - 1, slice(width, width + LANES))
            values = load(top + height - 1, lane_pair(width, pair))
            joined = weights_refs[height - 1][:, block(pair, 2 * values.shape[0])]
            slopes[pair, height] = query_slopes(joined, grad, denom, values, pair, height, masks)
    pieces = {}
    for pair, height in slopes:
        keys = load(top + height - 1, lane_pair(0, pair))
        pieces[pair, height] = dot(stack(slopes[pair, height], 1), masked_stack(keys, masks))
    results = []
    for pair in pairs:
        total = pieces[pair, top]
        for height in range(top - 1, 0, -1):
            total = pieces[pair, height] + 0.5 * doubled(total)
        total = total * side_factor(factor_ref, heads, pair)
        total = base_ref[:, lane_pair(0, pair)] + 0.5 * doubled(total)
        results.append(total.astype(BF))
    out_ref[...] = dot(order_matrix(rows, top, True), stack(results, 1)).astype(BF)


def key_kernel(top, first, last, load, factor_ref, base_key_ref, base_value_ref, key_out_ref, value_out_ref):
    rows, width = key_out_ref.shape
    heads = width // HALF
    masks = side_masks()
    levels = last - first + 1
    pairs = range(width // LANES)
    spots = [(pair, at) for pair in pairs for at in range(levels - 1, -1, -1)]
    weights, slopes, key_pieces, value_pieces = {}, {}, {}, {}
    for pair, at in spots:
        keys = load(at, lane_pair(width, pair))
        queries = load(levels + at, lane_pair(width + LANES, pair))
        weights[pair, at] = both_weights(factor_ref, pair, keys, queries, masks)
    for pair, at in spots:
        values = load(at, lane_pair(2 * width, pair))
        grad = load(levels + at, lane_pair(0, pair))
        denom = load(levels + at, slice(width, width + LANES))
        count = values.shape[0]
        left = stack(
            [
                stack([values * mask, jnp.broadcast_to(slot * float(2 ** (first + at)), (count, LANES))], 1)
                for mask, slot in zip(masks, slot_masks(pair))
            ],
            0,
        )
        product = dot(left, stack([grad, denom], 1), NT)
        slopes[pair, at] = [
            (weight * product[side * count : (side + 1) * count]).astype(BF)
            for side, weight in enumerate(weights[pair, at])
        ]
    for pair, at in spots:
        grad = load(levels + at, lane_pair(0, pair))
        rounded = stack([weight.astype(BF) for weight in weights[pair, at]], 1)
        value_pieces[pair, at] = dot(rounded, masked_stack(grad, masks))
        queries = load(levels + at, lane_pair(width + LANES, pair))
        key_pieces[pair, at] = dot(stack(slopes[pair, at], 1), masked_stack(queries, masks))
    key_results, value_results = [], []
    for pair in pairs:
        key_total, value_total = key_pieces[pair, levels - 1], value_pieces[pair, levels - 1]
        for at in range(levels - 2, -1, -1):
            key_total = key_pieces[pair, at] + 0.5 * doubled(key_total)
            value_total = value_pieces[pair, at] + doubled(value_total)
        key_total = key_total * side_factor(factor_ref, heads, pair)
        for _ in range(first):
            key_total, value_total = 0.5 * doubled(key_total), doubled(value_total)
        key_results.append(base_key_ref[:, lane_pair(0, pair)] + key_total)
        value_results.append(base_value_ref[:, lane_pair(0, pair)] + value_total)
    key_total, value_total = stack(key_results, 1), stack(value_results, 1)
    if last == top:
        back = order_matrix(rows, top, True)
        key_total, value_total = dot(back, key_total.astype(BF)), dot(back, value_total.astype(BF))
    key_out_ref[...] = key_total.astype(key_out_ref.dtype)
    value_out_ref[...] = value_total.astype(value_out_ref.dtype)


def place_kernel(spots, load, *refs):
    for target, start, groups in spots:
        total = None
        for group in groups:
            value = load(group, slice(None))
            if len(groups) > 1 or refs[target].dtype == F32:
                value = value.astype(F32)
            total = value if total is None else total + value
        refs[target][start : start + total.shape[0], :] = total.astype(refs[target].dtype)


def flush_kernel(load, *refs):
    count = (len(refs) - 1) // 2
    copies = [
        pltpu.make_async_copy(refs[at], refs[count + at], refs[-1].at[at]) for at in range(count)
    ]
    for copy in copies:
        copy.start()
    for copy in copies:
        copy.wait()


def flush(*arrays):
    return call(
        flush_kernel,
        "flush",
        [(array.shape, array.dtype) for array in arrays],
        arrays,
        out_specs=[HBM] * len(arrays),
        scratch=[pltpu.SemaphoreType.DMA((len(arrays),))],
    )


def placed(name, shapes, spots, flops=SMALL):
    views, listed = [], []
    for target, start, parts in spots:
        listed.append((target, start, range(len(views), len(views) + len(parts))))
        views += [[part] for part in parts]
    return call(functools.partial(place_kernel, listed), name, shapes, [], views=views, flops=flops)


def total_kernel(load, core_ref, own_ref, partner_ref, *refs):
    half = own_ref.shape[0] // 3
    base_ref = refs[0] if refs[0].shape[0] == 2 * half and len(refs) == 3 and refs[1].dtype == F32 else None
    out_refs = refs[:-1] if base_ref is None else refs[1:-1]
    sum_ref = refs[-1]
    total = own_ref[: 2 * half, :].astype(F32) + partner_ref[: 2 * half, :].astype(F32)
    if base_ref is not None:
        total = total + base_ref[...].astype(F32)
    sum_ref[...] = total
    for ref, core in ((own_ref, core_ref[0]), (partner_ref, 1 - core_ref[0])):
        span = pl.ds(pl.multiple_of(core * half, half), half)
        sum_ref[span, :] = sum_ref[span, :] + ref[2 * half :, :].astype(F32)
    out_refs[0][...] = sum_ref[...].astype(out_refs[0].dtype)
    if len(out_refs) > 1:
        span = pl.ds(pl.multiple_of(core_ref[0] * half, half), half)
        out_refs[1][...] = sum_ref[span, :].astype(BF)


def chip_total(name, core, arrays, half, kind):
    width = arrays[0].shape[1]
    shapes = [((2 * half, width), kind)] + [((half, width), BF)] * (kind == BF)
    return call(
        total_kernel,
        name,
        shapes,
        arrays,
        scalars=[core.reshape(1)],
        flops=LARGE,
        scratch=[pltpu.VMEM((2 * half, width), F32)],
    )


def traded(value, mask):
    return lax.ppermute(value, SEQ, [(source, source ^ mask) for source in range(lax.axis_size(SEQ))])


def split_traded(value, first, second):
    return lax.ppermute(
        value,
        SEQ,
        [(source, source ^ (2 * (second if source % 2 else first))) for source in range(lax.axis_size(SEQ))],
    )


def layer_traded(value, first, second):
    axes = ("dp", *SEQ)
    count = lax.axis_size(SEQ)
    pairs = []
    for source in range(lax.axis_size(axes)):
        layer, spot = divmod(source, count)
        pairs.append((source, (layer ^ (second if spot % 2 else first)) * count + spot))
    return lax.ppermute(value, axes, pairs)


def from_siblings(levels, top):
    arrived = {}
    for offset in range(1, 2**top):
        height = offset.bit_length()
        if offset == 1:
            arrived[1] = traded(levels[0], 1)
        elif offset % 2 == 0:
            arrived[offset] = traded(levels[height - 1], offset)
        else:
            arrived[offset] = traded(arrived[offset - 1], 1)
    grouped = []
    for height in range(1, top + 1):
        parts = [arrived[offset] for offset in range(2 ** (height - 1), 2**height)]
        if parts[0].shape[0] < 16:
            parts = [jnp.concatenate(parts, axis=0)]
        grouped.append([View(part) for part in parts])
    return grouped


def shards(queries, key_rows, value_rows, head_scale, out_weight, cotangent):
    rows, width = queries.shape[1:]
    heads = head_scale.shape[0]
    top = lax.axis_size(SEQ).bit_length() - 1
    parts = lax.axis_size("dp")
    assert width == HALF * heads and width % LANES == 0 and width <= 4 * LANES
    paired = top == 3 and parts == 4 and rows == 256
    whole = (rows, width)
    wide = width + LANES
    sizes = [rows >> height for height in range(top + 1)]
    starts = [0]
    for size in sizes:
        starts.append(starts[-1] + max(size, 16))
    if paired:
        places, messages = [(0, 0), (1, 0), (0, sizes[1])], [sizes[1] + sizes[3], sizes[2]]
    else:
        places, messages = [(height, 0) for height in range(top)], sizes[1:]
    factors, own_rows_all, *levels = call(
        functools.partial(pool_kernel, top, starts, places),
        "pool",
        [((factor_rows(heads), LANES), F32), ((starts[-1], 3 * width), BF)]
        + [((count, 2 * width), BF) for count in messages],
        [
            pltpu.with_memory_space_constraint(value, pltpu.HBM)
            for value in (queries[0], key_rows[0], value_rows[0], head_scale)
        ],
        specs=[HBM] * 4,
        scratch=[pltpu.VMEM(whole, BF)] * 3 + [pltpu.SMEM((heads,), F32), pltpu.SemaphoreType.DMA((4,))],
    )
    own = [[View(own_rows_all, starts[height], sizes[height])] for height in range(1, top + 1)]
    sums, base_weights, back = call(
        functools.partial(base_kernel, top),
        "base",
        [((rows, 2 * width), F32), ((rows, heads * rows), BF), ((rows, 2 * width), BF)],
        [factors, own_rows_all]
        + [pltpu.with_memory_space_constraint(value, pltpu.HBM) for value in (cotangent[0], out_weight)],
        specs=[VMEM, VMEM, HBM, HBM],
        scratch=[pltpu.VMEM(whole, BF), pltpu.VMEM((width, width), BF), pltpu.SemaphoreType.DMA((2,))],
        flops=100000000,
    )

    def attend_level(height, views, sums):
        return call(
            functools.partial(level_kernel, height),
            "level",
            [((sizes[height], heads * rows // 2), BF), ((rows, 2 * width), F32)],
            [factors, sums],
            views=[own[height - 1], views],
            flops=100000000//4,
        )

    if paired:
        within = traded(levels[0], 1)
        across = traded(levels[1], 2)
        (third,) = placed(
            "third_rows",
            [((2 * sizes[3], 2 * width), BF)],
            [(0, 0, [View(levels[0], sizes[1])]), (0, sizes[3], [View(within, sizes[1])])],
        )
        split = split_traded(third, 2, 3)
        level_weights = []
        if READY > 0:
            weights, sums = attend_level(1, [View(within, 0, sizes[1])], sums)
            level_weights.append(weights)
        across, sums = lax.optimization_barrier((across, sums))
        across_too = traded(across, 1)
        split_too = traded(split, 1)
        if READY > 1:
            weights, sums = attend_level(2, [View(across), View(across_too)], sums)
            level_weights.append(weights)
            split_too, sums = lax.optimization_barrier((split_too, sums))
        siblings = [[View(within, 0, sizes[1])], [View(across), View(across_too)], [View(split), View(split_too)]]
    else:
        siblings = from_siblings(levels, top)
        level_weights = []
    ready = len(level_weights)
    own_rows = width // parts
    half = own_rows // 2
    layer = lax.axis_index("dp").astype(jnp.int32)
    if paired:
        core = lax.axis_index(SEQ).astype(jnp.int32) % 2
        place = jnp.stack([layer, layer ^ (2 + core), layer ^ (3 - core), layer ^ 1, core * half])
        grad_places = [(0, 0), (1, 0), (2, 0), (1, sizes[1])]
        grad_shapes = [(rows, wide), (sizes[1] + sizes[3], wide + width), (sizes[2], wide + width)]
        pieces = [
            (0, 0, own_rows, 0, 0),
            (1, 0, own_rows, 1, 0),
            (3, lambda ref: ref[4], half, 1, own_rows),
            (2, 0, own_rows, 2, 0),
            (3, lambda ref: half - ref[4], half, 2, own_rows),
        ]
        shapes = [(own_rows, width), (own_rows + half, width), (own_rows + half, width)]
    else:
        place = (layer + jnp.arange(parts, dtype=jnp.int32)) % parts
        grad_places = [(height, 0) for height in range(top + 1)]
        pieces = [(step, 0, own_rows, step, 0) for step in range(parts)]
        grad_shapes = [(rows, wide)] + [(size, wide + width) for size in sizes[1:]]
        shapes = [(own_rows, width)] * parts
    outs = call(
        functools.partial(forward_kernel, top, ready, parts, pieces),
        "forward",
        [((size, heads * rows // 2), BF) for size in sizes[ready + 1 :]]
        + [(whole, F32), (whole, F32)]
        + [(shape, BF) for shape in shapes],
        [factors, sums, back],
        views=own[ready:] + siblings[ready:] + siblings[:ready],
        scalars=[place],
        scratch=[pltpu.VMEM((width, width), F32)],
    )
    level_weights += outs[: top - ready]
    outs = outs[top - ready :]
    (grad_rows, denom_rows), pieces = outs[:2], outs[2:]
    outs = call(
        functools.partial(grads_kernel, grad_places),
        "grads",
        [(shape, BF) for shape in grad_shapes],
        [grad_rows, denom_rows],
        views=own,
        flops=100000000,
    )

    def own_grads(arrays):
        return [
            [View(arrays[target], start, sizes[height])] for height, (target, start) in enumerate(grad_places) if height
        ]

    near_query, near_key, near_value = call(
        near_kernel,
        "near",
        [(whole, F32)] * 3,
        [factors, own_rows_all, outs[0], base_weights],
        flops=1600000000,
    )
    (query_grad,) = call(
        functools.partial(far_kernel, top),
        "far",
        [(whole, BF)],
        [factors, near_query, *level_weights],
        views=own_grads(outs) + siblings,
        flops=100000000,
    )

    def key_call(first, last, sums, sibling_grads, kind):
        return call(
            functools.partial(key_kernel, top, first, last),
            "key",
            [(whole, kind), (whole, kind)],
            [factors, *sums],
            views=own[first - 1 : last] + sibling_grads,
            flops=100000000,
        )

    if paired:
        near, far = outs[1:3]
        mine, send, theirs = pieces
        theirs_in = traded(theirs, 1)
        send_one, send_half = placed(
            "layer_rows",
            [((own_rows, width), BF), ((half, width), BF)],
            [
                (0, 0, [View(send, 0, own_rows), View(theirs_in, 0, own_rows)]),
                (1, 0, [View(send, own_rows), View(theirs_in, own_rows)]),
            ],
            flops=LARGE,
        )
        near_in = traded(near, 1)
        far_in = traded(far, 2)
        layer_one = layer_traded(send_one, 2, 3)
        layer_half = layer_traded(send_half, 1, 1)
        (third,) = placed(
            "third_grads",
            [((2 * sizes[3], wide + width), BF)],
            [(0, 0, [View(near, sizes[1])]), (0, sizes[3], [View(near_in, sizes[1])])],
        )
        third_in = split_traded(third, 2, 3)
        layer_one, layer_half, near_key = lax.optimization_barrier((layer_one, layer_half, near_key))
        (joint,) = placed(
            "layer_sum",
            [((own_rows + half, width), BF)],
            [(0, 0, [View(mine), View(layer_one)]), (0, own_rows, [View(layer_half)])],
            flops=LARGE,
        )
        joint_in = traded(joint, 1)
        far_in, near_key = lax.optimization_barrier((far_in, near_key))
        far_too = traded(far_in, 1)
        near_sums = key_call(1, 1, (near_key, near_value), [[View(near_in, 0, sizes[1])]], F32)
        joint_in, near_sums = lax.optimization_barrier((joint_in, tuple(near_sums)))
        weight, weight_half = chip_total("layer_total", core, [joint, joint_in], half, BF)
        third_in, _ = lax.optimization_barrier((third_in, weight))
        third_too = traded(third_in, 1)
        sibling_grads = [[View(far_in), View(far_too)], [View(third_in), View(third_too)]]
        plane_one = split_traded(weight, 2, 3)
        plane_half = traded(weight_half, 2)
        key_grad, value_grad = key_call(2, top, near_sums, sibling_grads, BF)
        plane_one, key_grad, query_grad = lax.optimization_barrier((plane_one, key_grad, query_grad))
        (joint,) = placed(
            "plane_rows",
            [((own_rows + half, width), BF)],
            [(0, 0, [View(plane_one)]), (0, own_rows, [View(plane_half)])],
            flops=LARGE,
        )
        joint_in = traded(joint, 1)
        query_grad, key_grad, value_grad = flush(query_grad, key_grad, value_grad)
        joint_in, key_grad = lax.optimization_barrier((joint_in, key_grad))
        (weight,) = chip_total("weight_out", core, [joint, joint_in, weight], half, F32)
    else:
        weight = pieces[0].astype(F32)
        for step in range(1, parts):
            weight = weight + lax.ppermute(
                pieces[step], "dp", [(source, (source + step) % parts) for source in range(parts)]
            ).astype(F32)
        sibling_grads = from_siblings(outs[1 : top + 1], top)
        bit = 1
        while bit < top:
            weight = weight.astype(BF)
            group = [weight] + [traded(weight, mask << bit) for mask in range(1, 2 ** min(2, top - bit))]
            weight = sum(value.astype(F32) for value in group)
            bit += 2
        weight = weight.astype(BF)
        weight = weight.astype(F32) + traded(weight, 1).astype(F32)
        key_grad, value_grad = key_call(1, top, (near_key, near_value), sibling_grads, BF)
    return query_grad[None], key_grad[None], value_grad[None], weight


def solution(mesh):
    spread = P("dp", SEQ, None)
    return jax.shard_map(
        shards,
        mesh=mesh,
        in_specs=(spread, spread, spread, P(), P(), spread),
        out_specs=(spread, spread, spread, P("dp", None)),
        check_vma=False,
    )
```

```python
import functools
import math

import jax
import jax.numpy as jnp
from jax import lax
from jax.experimental import pallas as pl
from jax.experimental.pallas import tpu as pltpu
from jax.sharding import PartitionSpec as P

BF = jnp.bfloat16
F32 = jnp.float32
SEQ = ("seqhi", "seqlo")
LANES = 128
HALF = 64
READY = 2
SMALL, BYTES, LARGE = 1, 10000, 1
LOG2E = math.log2(math.e)
NN = (((1,), (0,)), ((), ()))
NT = (((1,), (1,)), ((), ()))
TN = (((0,), (0,)), ((), ()))


def dot(left, right, dims=NN):
    return lax.dot_general(left, right, dims, preferred_element_type=F32)


def iota(shape, dim):
    return lax.broadcasted_iota(jnp.int32, shape, dim)


def order_matrix(rows, top, inverse=False):
    source = iota((rows, rows), 0 if inverse else 1)
    place = source >> top
    for bit in range(top):
        place = place + ((source >> bit) & 1) * (rows >> (bit + 1))
    return jnp.where(place == iota((rows, rows), 1 if inverse else 0), 1.0, 0.0).astype(BF)


def side_masks():
    lane = iota((1, LANES), 1)
    low = jnp.where(lane < HALF, 1.0, 0.0)
    return low.astype(BF), (1.0 - low).astype(BF)


def factor_rows(heads):
    return -(-(heads + heads // 2) // 8) * 8


def fill_factors(scale_ref, factor_ref):
    heads = scale_ref.shape[0]
    lane = iota((1, LANES), 1)
    for head in range(heads):
        factor_ref[head : head + 1, :] = jnp.full((1, LANES), scale_ref[head] * (HALF**-0.5 * LOG2E), F32)
    for pair in range(heads // 2):
        both = jnp.where(lane < HALF, scale_ref[2 * pair], scale_ref[2 * pair + 1]) * (HALF**-0.5)
        factor_ref[heads + pair : heads + pair + 1, :] = both


def exponent(factor_ref, head, columns):
    return stack([factor_ref[head : head + 1, :]] * (columns // LANES), 1)


def side_factor(factor_ref, heads, pair):
    return factor_ref[heads + pair : heads + pair + 1, :]


def stack(parts, axis):
    return parts[0] if len(parts) == 1 else jnp.concatenate(parts, axis=axis)


def doubled(value):
    return jnp.concatenate([value, value], axis=0)


def halves_sum(value):
    half = value.shape[0] // 2
    return value[:half] + value[half:]


def lane_pair(offset, pair):
    return slice(offset + LANES * pair, offset + LANES * (pair + 1))


def slot_masks(pair):
    lane = iota((1, LANES), 1)
    masks = []
    for side in (0, 1):
        slot = lane - side * HALF
        hit = (slot == 16 * pair) | (slot == 16 * pair + 8)
        masks.append(jnp.where(hit, 1.0, 0.0).astype(BF))
    return masks


def denom_lanes(denoms):
    lane = iota((1, LANES), 1)
    slot = (lane % HALF) // 8
    packed = jnp.zeros(denoms[0].shape, F32)
    for pair, value in enumerate(denoms):
        high = value.astype(BF).astype(F32)
        packed = jnp.where(slot == 2 * pair, high, packed)
        packed = jnp.where(slot == 2 * pair + 1, value - high, packed)
    return packed.astype(BF)


class View:
    def __init__(self, array, start=0, rows=None):
        self.array = array
        self.start = start
        self.rows = array.shape[0] - start if rows is None else rows


VMEM = pl.BlockSpec(memory_space=pltpu.VMEM)
SMEM = pl.BlockSpec(memory_space=pltpu.SMEM)
HBM = pl.BlockSpec(memory_space=pltpu.HBM)


def call(kernel, name, shapes, arrays, views=(), scalars=(), flops=SMALL, scratch=(), specs=None, out_specs=None):
    unique, where = [], []
    for group in views:
        places = []
        for view in group:
            spot = next((at for at, array in enumerate(unique) if array is view.array), None)
            if spot is None:
                spot = len(unique)
                unique.append(view.array)
            places.append((spot, view.start, view.rows))
        where.append(places)

    def body(*refs):
        scalar_refs, refs = refs[: len(scalars)], refs[len(scalars) :]
        array_refs, refs = refs[: len(arrays)], refs[len(arrays) :]
        view_refs, refs = refs[: len(unique)], refs[len(unique) :]

        def load(group, columns):
            return stack(
                [view_refs[spot][start : start + rows, columns] for spot, start, rows in where[group]], 0
            )

        kernel(load, *scalar_refs, *array_refs, *refs)

    return pl.pallas_call(
        body,
        out_shape=[jax.ShapeDtypeStruct(shape, kind) for shape, kind in shapes],
        in_specs=[SMEM] * len(scalars) + (specs or [VMEM] * len(arrays)) + [VMEM] * len(unique),
        out_specs=out_specs or [VMEM] * len(shapes),
        scratch_shapes=list(scratch),
        compiler_params=pltpu.CompilerParams(vmem_limit_bytes=16 * 2**20),
        cost_estimate=pl.CostEstimate(flops=flops, transcendentals=0, bytes_accessed=BYTES),
        name=name,
    )(*scalars, *arrays, *unique)


def pool_kernel(top, starts, places, load, q_hbm, k_hbm, v_hbm, scale_hbm, factor_ref, rows_ref, *refs):
    level_refs, (q_ref, k_ref, v_ref, scale_ref, sems) = refs[:-5], refs[-5:]
    copies = [
        pltpu.make_async_copy(source, target, sems.at[index])
        for index, (source, target) in enumerate(
            ((q_hbm, q_ref), (k_hbm, k_ref), (v_hbm, v_ref), (scale_hbm, scale_ref))
        )
    ]
    for which in (1, 2, 0, 3):
        copies[which].start()
    rows, width = q_ref.shape
    order = order_matrix(rows, top)
    for which, ref in ((1, k_ref), (2, v_ref), (0, q_ref)):
        copies[which].wait()
        current = dot(order, ref[...])
        columns = slice(which * width, (which + 1) * width)
        rows_ref[:rows, columns] = current.astype(BF)
        for height in range(1, top + 1):
            total = halves_sum(current)
            rounded = (total if which == 2 else 0.5 * total).astype(BF)
            rows_ref[starts[height] : starts[height] + rounded.shape[0], columns] = rounded
            if which:
                target, start = places[height - 1]
                span = slice(start, start + rounded.shape[0])
                level_refs[target][span, (which - 1) * width : which * width] = rounded
            current = rounded.astype(F32)
    copies[3].wait()
    fill_factors(scale_ref, factor_ref)


def masked_stack(value, masks):
    return stack([value * mask for mask in masks], 0)


def both_weights(factor_ref, pair, first, second, masks):
    rows = first.shape[0]
    logits = dot(masked_stack(first, masks), second, NT)
    columns = second.shape[0]
    return [
        jnp.exp2(logits[side * rows : (side + 1) * rows] * exponent(factor_ref, 2 * pair + side, columns))
        for side in (0, 1)
    ]


def attend(factor_ref, items, masks):
    weights = [
        stack([weight.astype(BF) for weight in both_weights(factor_ref, pair, queries, keys, masks)], 1)
        for pair, queries, keys, _, _ in items
    ]
    results = []
    for joined, (_, _, _, values, amount) in zip(weights, items):
        count = jnp.full(values.shape, float(amount), BF)
        right = stack([stack([values * mask, count * mask], 1) for mask in masks], 0)
        results.append((joined, dot(joined, right)))
    return results


def block(pair, span):
    return slice(span * pair, span * (pair + 1))


def base_kernel(top, load, factor_ref, x_ref, cot_hbm, w_hbm, sums_ref, weights_ref, back_ref, cot_ref, w_ref, sems):
    copies = [
        pltpu.make_async_copy(cot_hbm, cot_ref, sems.at[0]),
        pltpu.make_async_copy(w_hbm, w_ref, sems.at[1]),
    ]
    for copy in copies:
        copy.start()
    rows, width = cot_ref.shape
    masks = side_masks()
    items = [
        (pair, *(x_ref[:rows, lane_pair(width * which, pair)] for which in range(3)), 1)
        for pair in range(width // LANES)
    ]
    for pair, (joined, both) in enumerate(attend(factor_ref, items, masks)):
        sums_ref[:, block(pair, 2 * LANES)] = both
        weights_ref[:, block(pair, 2 * rows)] = joined
    order = order_matrix(rows, top)
    copies[0].wait()
    cotan = dot(order, cot_ref[...]).astype(BF)
    copies[1].wait()
    back_ref[:, width:] = cotan
    back_ref[:, :width] = dot(cotan, w_ref[...], NT).astype(BF)


def level_kernel(height, load, factor_ref, sums_ref, weights_ref, total_ref):
    width = sums_ref.shape[1] // 2
    masks = side_masks()
    items = [
        (pair, load(0, lane_pair(0, pair)), *(load(1, lane_pair(start, pair)) for start in (0, width)), 2**height)
        for pair in range(width // LANES)
    ]
    for pair, (joined, both) in enumerate(attend(factor_ref, items, masks)):
        weights_ref[:, block(pair, joined.shape[1])] = joined
        for _ in range(height):
            both = doubled(both)
        total_ref[:, block(pair, 2 * LANES)] = sums_ref[:, block(pair, 2 * LANES)] + both


def forward_kernel(
    top, ready, parts, pieces, load, place_ref, factor_ref, sums_ref, back_ref, *refs
):
    weights_refs, refs = refs[: top - ready], refs[top - ready :]
    (grad_ref, slope_ref), out_refs, weight_ref = refs[:2], refs[2:-1], refs[-1]
    rows, width = grad_ref.shape
    masks = side_masks()
    lane = iota((LANES, LANES), 1)
    ones = jnp.where(lane // HALF == iota((LANES, LANES), 0) // HALF, 1.0, 0.0).astype(BF)
    adder = doubled(ones)
    pairs = range(width // LANES)
    spots = [(pair, at) for pair in pairs for at in range(top - ready - 1, -1, -1)]
    items = []
    for pair, at in spots:
        keys, values = (load(top - ready + at, lane_pair(start, pair)) for start in (0, width))
        items.append((pair, load(at, lane_pair(0, pair)), keys, values, 2 ** (ready + at + 1)))
    sums = {}
    for (pair, at), (joined, both) in zip(spots, attend(factor_ref, items, masks)):
        weights_refs[at][:, block(pair, joined.shape[1])] = joined
        sums[pair, at] = both
    attended, inverses, products = [], [], []
    for pair in pairs:
        total = sums[pair, top - ready - 1]
        for at in range(top - ready - 2, -1, -1):
            total = sums[pair, at] + doubled(total)
        for _ in range(ready + 1):
            total = doubled(total)
        total = total + sums_ref[:, block(pair, 2 * LANES)]
        inverse = 1.0 / total[:, LANES:]
        ratio = total[:, :LANES] * inverse
        attended.append(ratio.astype(BF))
        inverses.append(inverse)
        products.append(back_ref[:, lane_pair(0, pair)].astype(F32) * ratio)
    weight_ref[...] = dot(stack(attended, 1), back_ref[:, width:], TN)
    for pair in pairs:
        high = products[pair].astype(BF)
        low = (products[pair] - high.astype(F32)).astype(BF)
        grad_ref[:, lane_pair(0, pair)] = back_ref[:, lane_pair(0, pair)].astype(F32) * inverses[pair]
        slope_ref[:, lane_pair(0, pair)] = -dot(stack([high, low], 1), adder) * inverses[pair]
    own_rows = width // parts
    for entry, offset, count, target, start in pieces:
        shift = offset if isinstance(offset, int) else offset(place_ref)
        first = pl.multiple_of(place_ref[entry] * own_rows + shift, math.gcd(own_rows, count))
        out_refs[target][start : start + count, :] = weight_ref[pl.ds(first, count), :].astype(BF)


def grads_kernel(grad_places, load, grad_ref, slope_ref, *out_refs):
    rows, width = grad_ref.shape
    grad_rows = [grad_ref[:, lane_pair(0, pair)] for pair in range(width // LANES)]
    denom_rows = [slope_ref[:, lane_pair(0, pair)] for pair in range(width // LANES)]
    for height, (target, start) in enumerate(grad_places):
        if height:
            grad_rows = [halves_sum(value) for value in grad_rows]
            denom_rows = [halves_sum(value) for value in denom_rows]
        span = slice(start, start + (rows >> height))
        for pair, value in enumerate(grad_rows):
            out_refs[target][span, lane_pair(0, pair)] = value.astype(BF)
        out_refs[target][span, width : width + LANES] = denom_lanes(denom_rows)
        if height:
            out_refs[target][span, width + LANES :] = load(height - 1, slice(0, width))


def query_slopes(joined, grad, denom, values, pair, height, masks):
    rows, columns = grad.shape[0], values.shape[0]
    left = stack([stack([grad * mask, denom * slot], 1) for mask, slot in zip(masks, slot_masks(pair))], 0)
    right = stack([values, jnp.full((columns, LANES), float(2**height), BF)], 1)
    product = dot(left, right, NT)
    return [
        (joined[:, side * columns : (side + 1) * columns].astype(F32) * product[side * rows : (side + 1) * rows])
        .astype(BF)
        for side in (0, 1)
    ]


def near_kernel(load, factor_ref, x_ref, gh_ref, weights_ref, query_ref, key_ref, value_ref):
    rows, width = query_ref.shape
    heads = width // HALF
    masks = side_masks()
    pairs = range(width // LANES)
    slopes = []
    for pair in pairs:
        values = x_ref[:rows, lane_pair(2 * width, pair)]
        joined = weights_ref[:, block(pair, 2 * rows)]
        grad = gh_ref[:, lane_pair(0, pair)]
        slopes.append(query_slopes(joined, grad, gh_ref[:, width:], values, pair, 0, masks))
    for pair in pairs:
        factor = side_factor(factor_ref, heads, pair)
        keys = x_ref[:rows, lane_pair(width, pair)]
        query_ref[:, lane_pair(0, pair)] = dot(stack(slopes[pair], 1), masked_stack(keys, masks)) * factor
    for pair in pairs:
        joined = weights_ref[:, block(pair, 2 * rows)]
        weights = stack([joined[:, :rows], joined[:, rows:]], 0)
        grad = gh_ref[:, lane_pair(0, pair)]
        value_ref[:, lane_pair(0, pair)] = dot(weights, masked_stack(grad, masks), TN)
    for pair in pairs:
        factor = side_factor(factor_ref, heads, pair)
        queries = x_ref[:rows, lane_pair(0, pair)]
        key_ref[:, lane_pair(0, pair)] = dot(stack(slopes[pair], 0), masked_stack(queries, masks), TN) * factor


def far_kernel(top, load, factor_ref, base_ref, *refs):
    weights_refs, out_ref = refs[:top], refs[top]
    rows, width = out_ref.shape
    heads = width // HALF
    masks = side_masks()
    pairs = range(width // LANES)
    slopes = {}
    for pair in pairs:
        for height in range(top, 0, -1):
            grad = load(height - 1, lane_pair(0, pair))
            denom = load(height - 1, slice(width, width + LANES))
            values = load(top + height - 1, lane_pair(width, pair))
            joined = weights_refs[height - 1][:, block(pair, 2 * values.shape[0])]
            slopes[pair, height] = query_slopes(joined, grad, denom, values, pair, height, masks)
    pieces = {}
    for pair, height in slopes:
        keys = load(top + height - 1, lane_pair(0, pair))
        pieces[pair, height] = dot(stack(slopes[pair, height], 1), masked_stack(keys, masks))
    results = []
    for pair in pairs:
        total = pieces[pair, top]
        for height in range(top - 1, 0, -1):
            total = pieces[pair, height] + 0.5 * doubled(total)
        total = total * side_factor(factor_ref, heads, pair)
        total = base_ref[:, lane_pair(0, pair)] + 0.5 * doubled(total)
        results.append(total.astype(BF))
    out_ref[...] = dot(order_matrix(rows, top, True), stack(results, 1)).astype(BF)


def key_kernel(top, first, last, load, factor_ref, base_key_ref, base_value_ref, key_out_ref, value_out_ref):
    rows, width = key_out_ref.shape
    heads = width // HALF
    masks = side_masks()
    levels = last - first + 1
    pairs = range(width // LANES)
    spots = [(pair, at) for pair in pairs for at in range(levels - 1, -1, -1)]
    weights, slopes, key_pieces, value_pieces = {}, {}, {}, {}
    for pair, at in spots:
        keys = load(at, lane_pair(width, pair))
        queries = load(levels + at, lane_pair(width + LANES, pair))
        weights[pair, at] = both_weights(factor_ref, pair, keys, queries, masks)
    for pair, at in spots:
        values = load(at, lane_pair(2 * width, pair))
        grad = load(levels + at, lane_pair(0, pair))
        denom = load(levels + at, slice(width, width + LANES))
        count = values.shape[0]
        left = stack(
            [
                stack([values * mask, jnp.broadcast_to(slot * float(2 ** (first + at)), (count, LANES))], 1)
                for mask, slot in zip(masks, slot_masks(pair))
            ],
            0,
        )
        product = dot(left, stack([grad, denom], 1), NT)
        slopes[pair, at] = [
            (weight * product[side * count : (side + 1) * count]).astype(BF)
            for side, weight in enumerate(weights[pair, at])
        ]
    for pair, at in spots:
        grad = load(levels + at, lane_pair(0, pair))
        rounded = stack([weight.astype(BF) for weight in weights[pair, at]], 1)
        value_pieces[pair, at] = dot(rounded, masked_stack(grad, masks))
        queries = load(levels + at, lane_pair(width + LANES, pair))
        key_pieces[pair, at] = dot(stack(slopes[pair, at], 1), masked_stack(queries, masks))
    key_results, value_results = [], []
    for pair in pairs:
        key_total, value_total = key_pieces[pair, levels - 1], value_pieces[pair, levels - 1]
        for at in range(levels - 2, -1, -1):
            key_total = key_pieces[pair, at] + 0.5 * doubled(key_total)
            value_total = value_pieces[pair, at] + doubled(value_total)
        key_total = key_total * side_factor(factor_ref, heads, pair)
        for _ in range(first):
            key_total, value_total = 0.5 * doubled(key_total), doubled(value_total)
        key_results.append(base_key_ref[:, lane_pair(0, pair)] + key_total)
        value_results.append(base_value_ref[:, lane_pair(0, pair)] + value_total)
    key_total, value_total = stack(key_results, 1), stack(value_results, 1)
    if last == top:
        back = order_matrix(rows, top, True)
        key_total, value_total = dot(back, key_total.astype(BF)), dot(back, value_total.astype(BF))
    key_out_ref[...] = key_total.astype(key_out_ref.dtype)
    value_out_ref[...] = value_total.astype(value_out_ref.dtype)


def place_kernel(spots, load, *refs):
    for target, start, groups in spots:
        total = None
        for group in groups:
            value = load(group, slice(None))
            if len(groups) > 1 or refs[target].dtype == F32:
                value = value.astype(F32)
            total = value if total is None else total + value
        refs[target][start : start + total.shape[0], :] = total.astype(refs[target].dtype)


def flush_kernel(load, *refs):
    count = (len(refs) - 1) // 2
    copies = [
        pltpu.make_async_copy(refs[at], refs[count + at], refs[-1].at[at]) for at in range(count)
    ]
    for copy in copies:
        copy.start()
    for copy in copies:
        copy.wait()


def flush(*arrays):
    return call(
        flush_kernel,
        "flush",
        [(array.shape, array.dtype) for array in arrays],
        arrays,
        out_specs=[HBM] * len(arrays),
        scratch=[pltpu.SemaphoreType.DMA((len(arrays),))],
    )


def placed(name, shapes, spots, flops=SMALL):
    views, listed = [], []
    for target, start, parts in spots:
        listed.append((target, start, range(len(views), len(views) + len(parts))))
        views += [[part] for part in parts]
    return call(functools.partial(place_kernel, listed), name, shapes, [], views=views, flops=flops)


def total_kernel(load, core_ref, own_ref, partner_ref, *refs):
    half = own_ref.shape[0] // 3
    base_ref = refs[0] if refs[0].shape[0] == 2 * half and len(refs) == 3 and refs[1].dtype == F32 else None
    out_refs = refs[:-1] if base_ref is None else refs[1:-1]
    sum_ref = refs[-1]
    total = own_ref[: 2 * half, :].astype(F32) + partner_ref[: 2 * half, :].astype(F32)
    if base_ref is not None:
        total = total + base_ref[...].astype(F32)
    sum_ref[...] = total
    for ref, core in ((own_ref, core_ref[0]), (partner_ref, 1 - core_ref[0])):
        span = pl.ds(pl.multiple_of(core * half, half), half)
        sum_ref[span, :] = sum_ref[span, :] + ref[2 * half :, :].astype(F32)
    out_refs[0][...] = sum_ref[...].astype(out_refs[0].dtype)
    if len(out_refs) > 1:
        span = pl.ds(pl.multiple_of(core_ref[0] * half, half), half)
        out_refs[1][...] = sum_ref[span, :].astype(BF)


def chip_total(name, core, arrays, half, kind):
    width = arrays[0].shape[1]
    shapes = [((2 * half, width), kind)] + [((half, width), BF)] * (kind == BF)
    return call(
        total_kernel,
        name,
        shapes,
        arrays,
        scalars=[core.reshape(1)],
        flops=LARGE,
        scratch=[pltpu.VMEM((2 * half, width), F32)],
    )


def traded(value, mask):
    return lax.ppermute(value, SEQ, [(source, source ^ mask) for source in range(lax.axis_size(SEQ))])


def split_traded(value, first, second):
    return lax.ppermute(
        value,
        SEQ,
        [(source, source ^ (2 * (second if source % 2 else first))) for source in range(lax.axis_size(SEQ))],
    )


def layer_traded(value, first, second):
    axes = ("dp", *SEQ)
    count = lax.axis_size(SEQ)
    pairs = []
    for source in range(lax.axis_size(axes)):
        layer, spot = divmod(source, count)
        pairs.append((source, (layer ^ (second if spot % 2 else first)) * count + spot))
    return lax.ppermute(value, axes, pairs)


def from_siblings(levels, top):
    arrived = {}
    for offset in range(1, 2**top):
        height = offset.bit_length()
        if offset == 1:
            arrived[1] = traded(levels[0], 1)
        elif offset % 2 == 0:
            arrived[offset] = traded(levels[height - 1], offset)
        else:
            arrived[offset] = traded(arrived[offset - 1], 1)
    grouped = []
    for height in range(1, top + 1):
        parts = [arrived[offset] for offset in range(2 ** (height - 1), 2**height)]
        if parts[0].shape[0] < 16:
            parts = [jnp.concatenate(parts, axis=0)]
        grouped.append([View(part) for part in parts])
    return grouped


def shards(queries, key_rows, value_rows, head_scale, out_weight, cotangent):
    rows, width = queries.shape[1:]
    heads = head_scale.shape[0]
    top = lax.axis_size(SEQ).bit_length() - 1
    parts = lax.axis_size("dp")
    assert width == HALF * heads and width % LANES == 0 and width <= 4 * LANES
    paired = top == 3 and parts == 4 and rows == 256
    whole = (rows, width)
    wide = width + LANES
    sizes = [rows >> height for height in range(top + 1)]
    starts = [0]
    for size in sizes:
        starts.append(starts[-1] + max(size, 16))
    if paired:
        places, messages = [(0, 0), (1, 0), (0, sizes[1])], [sizes[1] + sizes[3], sizes[2]]
    else:
        places, messages = [(height, 0) for height in range(top)], sizes[1:]
    factors, own_rows_all, *levels = call(
        functools.partial(pool_kernel, top, starts, places),
        "pool",
        [((factor_rows(heads), LANES), F32), ((starts[-1], 3 * width), BF)]
        + [((count, 2 * width), BF) for count in messages],
        [
            pltpu.with_memory_space_constraint(value, pltpu.HBM)
            for value in (queries[0], key_rows[0], value_rows[0], head_scale)
        ],
        specs=[HBM] * 4,
        scratch=[pltpu.VMEM(whole, BF)] * 3 + [pltpu.SMEM((heads,), F32), pltpu.SemaphoreType.DMA((4,))],
    )
    own = [[View(own_rows_all, starts[height], sizes[height])] for height in range(1, top + 1)]
    sums, base_weights, back = call(
        functools.partial(base_kernel, top),
        "base",
        [((rows, 2 * width), F32), ((rows, heads * rows), BF), ((rows, 2 * width), BF)],
        [factors, own_rows_all]
        + [pltpu.with_memory_space_constraint(value, pltpu.HBM) for value in (cotangent[0], out_weight)],
        specs=[VMEM, VMEM, HBM, HBM],
        scratch=[pltpu.VMEM(whole, BF), pltpu.VMEM((width, width), BF), pltpu.SemaphoreType.DMA((2,))],
        flops=100000000,
    )

    def attend_level(height, views, sums):
        return call(
            functools.partial(level_kernel, height),
            "level",
            [((sizes[height], heads * rows // 2), BF), ((rows, 2 * width), F32)],
            [factors, sums],
            views=[own[height - 1], views],
            flops=100000000//4,
        )

    if paired:
        within = traded(levels[0], 1)
        across = traded(levels[1], 2)
        (third,) = placed(
            "third_rows",
            [((2 * sizes[3], 2 * width), BF)],
            [(0, 0, [View(levels[0], sizes[1])]), (0, sizes[3], [View(within, sizes[1])])],
        )
        split = split_traded(third, 2, 3)
        level_weights = []
        if READY > 0:
            weights, sums = attend_level(1, [View(within, 0, sizes[1])], sums)
            level_weights.append(weights)
        across, sums = lax.optimization_barrier((across, sums))
        across_too = traded(across, 1)
        split_too = traded(split, 1)
        if READY > 1:
            weights, sums = attend_level(2, [View(across), View(across_too)], sums)
            level_weights.append(weights)
            split_too, sums = lax.optimization_barrier((split_too, sums))
        siblings = [[View(within, 0, sizes[1])], [View(across), View(across_too)], [View(split), View(split_too)]]
    else:
        siblings = from_siblings(levels, top)
        level_weights = []
    ready = len(level_weights)
    own_rows = width // parts
    half = own_rows // 2
    layer = lax.axis_index("dp").astype(jnp.int32)
    if paired:
        core = lax.axis_index(SEQ).astype(jnp.int32) % 2
        place = jnp.stack([layer, layer ^ (1 + 2 * core), layer ^ (3 - 2 * core), layer ^ 2, core * half])
        grad_places = [(0, 0), (1, 0), (2, 0), (1, sizes[1])]
        grad_shapes = [(rows, wide), (sizes[1] + sizes[3], wide + width), (sizes[2], wide + width)]
        pieces = [
            (0, 0, own_rows, 0, 0),
            (1, 0, own_rows, 1, 0),
            (3, lambda ref: ref[4], half, 1, own_rows),
            (2, 0, own_rows, 2, 0),
            (3, lambda ref: half - ref[4], half, 2, own_rows),
        ]
        shapes = [(own_rows, width), (own_rows + half, width), (own_rows + half, width)]
    else:
        place = (layer + jnp.arange(parts, dtype=jnp.int32)) % parts
        grad_places = [(height, 0) for height in range(top + 1)]
        pieces = [(step, 0, own_rows, step, 0) for step in range(parts)]
        grad_shapes = [(rows, wide)] + [(size, wide + width) for size in sizes[1:]]
        shapes = [(own_rows, width)] * parts
    outs = call(
        functools.partial(forward_kernel, top, ready, parts, pieces),
        "forward",
        [((size, heads * rows // 2), BF) for size in sizes[ready + 1 :]]
        + [(whole, F32), (whole, F32)]
        + [(shape, BF) for shape in shapes],
        [factors, sums, back],
        views=own[ready:] + siblings[ready:] + siblings[:ready],
        scalars=[place],
        scratch=[pltpu.VMEM((width, width), F32)],
    )
    level_weights += outs[: top - ready]
    outs = outs[top - ready :]
    (grad_rows, denom_rows), pieces = outs[:2], outs[2:]
    outs = call(
        functools.partial(grads_kernel, grad_places),
        "grads",
        [(shape, BF) for shape in grad_shapes],
        [grad_rows, denom_rows],
        views=own,
        flops=100000000,
    )

    def own_grads(arrays):
        return [
            [View(arrays[target], start, sizes[height])] for height, (target, start) in enumerate(grad_places) if height
        ]

    near_query, near_key, near_value = call(
        near_kernel,
        "near",
        [(whole, F32)] * 3,
        [factors, own_rows_all, outs[0], base_weights],
        flops=1600000000,
    )
    (query_grad,) = call(
        functools.partial(far_kernel, top),
        "far",
        [(whole, BF)],
        [factors, near_query, *level_weights],
        views=own_grads(outs) + siblings,
        flops=100000000,
    )

    def key_call(first, last, sums, sibling_grads, kind):
        return call(
            functools.partial(key_kernel, top, first, last),
            "key",
            [(whole, kind), (whole, kind)],
            [factors, *sums],
            views=own[first - 1 : last] + sibling_grads,
            flops=100000000,
        )

    if paired:
        near, far = outs[1:3]
        mine, send, theirs = pieces
        theirs_in = traded(theirs, 1)
        send_one, send_half = placed(
            "layer_rows",
            [((own_rows, width), BF), ((half, width), BF)],
            [
                (0, 0, [View(send, 0, own_rows), View(theirs_in, 0, own_rows)]),
                (1, 0, [View(send, own_rows), View(theirs_in, own_rows)]),
            ],
            flops=LARGE,
        )
        near_in = traded(near, 1)
        far_in = traded(far, 2)
        layer_one = layer_traded(send_one, 1, 3)
        layer_half = layer_traded(send_half, 2, 2)
        (third,) = placed(
            "third_grads",
            [((2 * sizes[3], wide + width), BF)],
            [(0, 0, [View(near, sizes[1])]), (0, sizes[3], [View(near_in, sizes[1])])],
        )
        third_in = split_traded(third, 2, 3)
        layer_one, layer_half, near_key = lax.optimization_barrier((layer_one, layer_half, near_key))
        (joint,) = placed(
            "layer_sum",
            [((own_rows + half, width), BF)],
            [(0, 0, [View(mine), View(layer_one)]), (0, own_rows, [View(layer_half)])],
            flops=LARGE,
        )
        joint_in = traded(joint, 1)
        far_in, near_key = lax.optimization_barrier((far_in, near_key))
        far_too = traded(far_in, 1)
        near_sums = key_call(1, 1, (near_key, near_value), [[View(near_in, 0, sizes[1])]], F32)
        joint_in, near_sums = lax.optimization_barrier((joint_in, tuple(near_sums)))
        weight, weight_half = chip_total("layer_total", core, [joint, joint_in], half, BF)
        third_in, _ = lax.optimization_barrier((third_in, weight))
        third_too = traded(third_in, 1)
        sibling_grads = [[View(far_in), View(far_too)], [View(third_in), View(third_too)]]
        plane_one = split_traded(weight, 2, 3)
        plane_half = traded(weight_half, 2)
        key_grad, value_grad = key_call(2, top, near_sums, sibling_grads, BF)
        plane_one, key_grad, query_grad = lax.optimization_barrier((plane_one, key_grad, query_grad))
        (joint,) = placed(
            "plane_rows",
            [((own_rows + half, width), BF)],
            [(0, 0, [View(plane_one)]), (0, own_rows, [View(plane_half)])],
            flops=LARGE,
        )
        joint_in = traded(joint, 1)
        query_grad, key_grad, value_grad = flush(query_grad, key_grad, value_grad)
        joint_in, key_grad = lax.optimization_barrier((joint_in, key_grad))
        (weight,) = chip_total("weight_out", core, [joint, joint_in, weight], half, F32)
    else:
        weight = pieces[0].astype(F32)
        for step in range(1, parts):
            weight = weight + lax.ppermute(
                pieces[step], "dp", [(source, (source + step) % parts) for source in range(parts)]
            ).astype(F32)
        sibling_grads = from_siblings(outs[1 : top + 1], top)
        bit = 1
        while bit < top:
            weight = weight.astype(BF)
            group = [weight] + [traded(weight, mask << bit) for mask in range(1, 2 ** min(2, top - bit))]
            weight = sum(value.astype(F32) for value in group)
            bit += 2
        weight = weight.astype(BF)
        weight = weight.astype(F32) + traded(weight, 1).astype(F32)
        key_grad, value_grad = key_call(1, top, (near_key, near_value), sibling_grads, BF)
    return query_grad[None], key_grad[None], value_grad[None], weight


def solution(mesh):
    spread = P("dp", SEQ, None)
    return jax.shard_map(
        shards,
        mesh=mesh,
        in_specs=(spread, spread, spread, P(), P(), spread),
        out_specs=(spread, spread, spread, P("dp", None)),
        check_vma=False,
    )
```

```python
import functools
import math

import jax
import jax.numpy as jnp
from jax import lax
from jax.experimental import pallas as pl
from jax.experimental.pallas import tpu as pltpu
from jax.sharding import PartitionSpec as P

BF = jnp.bfloat16
F32 = jnp.float32
SEQ = ("seqhi", "seqlo")
LANES = 128
HALF = 64
READY = 2
SMALL, BYTES, LARGE = 1, 10000, 1
LOG2E = math.log2(math.e)
NN = (((1,), (0,)), ((), ()))
NT = (((1,), (1,)), ((), ()))
TN = (((0,), (0,)), ((), ()))


def dot(left, right, dims=NN):
    return lax.dot_general(left, right, dims, preferred_element_type=F32)


def iota(shape, dim):
    return lax.broadcasted_iota(jnp.int32, shape, dim)


def order_matrix(rows, top, inverse=False):
    source = iota((rows, rows), 0 if inverse else 1)
    place = source >> top
    for bit in range(top):
        place = place + ((source >> bit) & 1) * (rows >> (bit + 1))
    return jnp.where(place == iota((rows, rows), 1 if inverse else 0), 1.0, 0.0).astype(BF)


def side_masks():
    lane = iota((1, LANES), 1)
    low = jnp.where(lane < HALF, 1.0, 0.0)
    return low.astype(BF), (1.0 - low).astype(BF)


def factor_rows(heads):
    return -(-(heads + heads // 2) // 8) * 8


def fill_factors(scale_ref, factor_ref):
    heads = scale_ref.shape[0]
    lane = iota((1, LANES), 1)
    for head in range(heads):
        factor_ref[head : head + 1, :] = jnp.full((1, LANES), scale_ref[head] * (HALF**-0.5 * LOG2E), F32)
    for pair in range(heads // 2):
        both = jnp.where(lane < HALF, scale_ref[2 * pair], scale_ref[2 * pair + 1]) * (HALF**-0.5)
        factor_ref[heads + pair : heads + pair + 1, :] = both


def exponent(factor_ref, head, columns):
    return stack([factor_ref[head : head + 1, :]] * (columns // LANES), 1)


def side_factor(factor_ref, heads, pair):
    return factor_ref[heads + pair : heads + pair + 1, :]


def stack(parts, axis):
    return parts[0] if len(parts) == 1 else jnp.concatenate(parts, axis=axis)


def doubled(value):
    return jnp.concatenate([value, value], axis=0)


def halves_sum(value):
    half = value.shape[0] // 2
    return value[:half] + value[half:]


def lane_pair(offset, pair):
    return slice(offset + LANES * pair, offset + LANES * (pair + 1))


def slot_masks(pair):
    lane = iota((1, LANES), 1)
    masks = []
    for side in (0, 1):
        slot = lane - side * HALF
        hit = (slot == 16 * pair) | (slot == 16 * pair + 8)
        masks.append(jnp.where(hit, 1.0, 0.0).astype(BF))
    return masks


def denom_lanes(denoms):
    lane = iota((1, LANES), 1)
    slot = (lane % HALF) // 8
    packed = jnp.zeros(denoms[0].shape, F32)
    for pair, value in enumerate(denoms):
        high = value.astype(BF).astype(F32)
        packed = jnp.where(slot == 2 * pair, high, packed)
        packed = jnp.where(slot == 2 * pair + 1, value - high, packed)
    return packed.astype(BF)


class View:
    def __init__(self, array, start=0, rows=None):
        self.array = array
        self.start = start
        self.rows = array.shape[0] - start if rows is None else rows


VMEM = pl.BlockSpec(memory_space=pltpu.VMEM)
SMEM = pl.BlockSpec(memory_space=pltpu.SMEM)
HBM = pl.BlockSpec(memory_space=pltpu.HBM)


def call(kernel, name, shapes, arrays, views=(), scalars=(), flops=SMALL, scratch=(), specs=None, out_specs=None):
    unique, where = [], []
    for group in views:
        places = []
        for view in group:
            spot = next((at for at, array in enumerate(unique) if array is view.array), None)
            if spot is None:
                spot = len(unique)
                unique.append(view.array)
            places.append((spot, view.start, view.rows))
        where.append(places)

    def body(*refs):
        scalar_refs, refs = refs[: len(scalars)], refs[len(scalars) :]
        array_refs, refs = refs[: len(arrays)], refs[len(arrays) :]
        view_refs, refs = refs[: len(unique)], refs[len(unique) :]

        def load(group, columns):
            return stack(
                [view_refs[spot][start : start + rows, columns] for spot, start, rows in where[group]], 0
            )

        kernel(load, *scalar_refs, *array_refs, *refs)

    return pl.pallas_call(
        body,
        out_shape=[jax.ShapeDtypeStruct(shape, kind) for shape, kind in shapes],
        in_specs=[SMEM] * len(scalars) + (specs or [VMEM] * len(arrays)) + [VMEM] * len(unique),
        out_specs=out_specs or [VMEM] * len(shapes),
        scratch_shapes=list(scratch),
        compiler_params=pltpu.CompilerParams(vmem_limit_bytes=16 * 2**20),
        cost_estimate=pl.CostEstimate(flops=flops, transcendentals=0, bytes_accessed=BYTES),
        name=name,
    )(*scalars, *arrays, *unique)


def pool_kernel(top, starts, places, load, q_hbm, k_hbm, v_hbm, scale_hbm, factor_ref, rows_ref, *refs):
    level_refs, (q_ref, k_ref, v_ref, scale_ref, sems) = refs[:-5], refs[-5:]
    copies = [
        pltpu.make_async_copy(source, target, sems.at[index])
        for index, (source, target) in enumerate(
            ((q_hbm, q_ref), (k_hbm, k_ref), (v_hbm, v_ref), (scale_hbm, scale_ref))
        )
    ]
    for which in (1, 2, 0, 3):
        copies[which].start()
    rows, width = q_ref.shape
    order = order_matrix(rows, top)
    for which, ref in ((1, k_ref), (2, v_ref), (0, q_ref)):
        copies[which].wait()
        current = dot(order, ref[...])
        columns = slice(which * width, (which + 1) * width)
        rows_ref[:rows, columns] = current.astype(BF)
        for height in range(1, top + 1):
            total = halves_sum(current)
            rounded = (total if which == 2 else 0.5 * total).astype(BF)
            rows_ref[starts[height] : starts[height] + rounded.shape[0], columns] = rounded
            if which:
                target, start = places[height - 1]
                span = slice(start, start + rounded.shape[0])
                level_refs[target][span, (which - 1) * width : which * width] = rounded
            current = rounded.astype(F32)
    copies[3].wait()
    fill_factors(scale_ref, factor_ref)


def masked_stack(value, masks):
    return stack([value * mask for mask in masks], 0)


def both_weights(factor_ref, pair, first, second, masks):
    rows = first.shape[0]
    logits = dot(masked_stack(first, masks), second, NT)
    columns = second.shape[0]
    return [
        jnp.exp2(logits[side * rows : (side + 1) * rows] * exponent(factor_ref, 2 * pair + side, columns))
        for side in (0, 1)
    ]


def attend(factor_ref, items, masks):
    weights = [
        stack([weight.astype(BF) for weight in both_weights(factor_ref, pair, queries, keys, masks)], 1)
        for pair, queries, keys, _, _ in items
    ]
    results = []
    for joined, (_, _, _, values, amount) in zip(weights, items):
        count = jnp.full(values.shape, float(amount), BF)
        right = stack([stack([values * mask, count * mask], 1) for mask in masks], 0)
        results.append((joined, dot(joined, right)))
    return results


def block(pair, span):
    return slice(span * pair, span * (pair + 1))


def base_kernel(top, load, factor_ref, x_ref, cot_hbm, w_hbm, sums_ref, weights_ref, back_ref, cot_ref, w_ref, sems):
    copies = [
        pltpu.make_async_copy(cot_hbm, cot_ref, sems.at[0]),
        pltpu.make_async_copy(w_hbm, w_ref, sems.at[1]),
    ]
    for copy in copies:
        copy.start()
    rows, width = cot_ref.shape
    masks = side_masks()
    items = [
        (pair, *(x_ref[:rows, lane_pair(width * which, pair)] for which in range(3)), 1)
        for pair in range(width // LANES)
    ]
    for pair, (joined, both) in enumerate(attend(factor_ref, items, masks)):
        sums_ref[:, block(pair, 2 * LANES)] = both
        weights_ref[:, block(pair, 2 * rows)] = joined
    order = order_matrix(rows, top)
    copies[0].wait()
    cotan = dot(order, cot_ref[...]).astype(BF)
    copies[1].wait()
    back_ref[:, width:] = cotan
    back_ref[:, :width] = dot(cotan, w_ref[...], NT).astype(BF)


def level_kernel(height, load, factor_ref, sums_ref, weights_ref, total_ref):
    width = sums_ref.shape[1] // 2
    masks = side_masks()
    items = [
        (pair, load(0, lane_pair(0, pair)), *(load(1, lane_pair(start, pair)) for start in (0, width)), 2**height)
        for pair in range(width // LANES)
    ]
    for pair, (joined, both) in enumerate(attend(factor_ref, items, masks)):
        weights_ref[:, block(pair, joined.shape[1])] = joined
        for _ in range(height):
            both = doubled(both)
        total_ref[:, block(pair, 2 * LANES)] = sums_ref[:, block(pair, 2 * LANES)] + both


def forward_kernel(
    top, ready, parts, pieces, load, place_ref, factor_ref, sums_ref, back_ref, *refs
):
    weights_refs, refs = refs[: top - ready], refs[top - ready :]
    (grad_ref, slope_ref), out_refs, weight_ref = refs[:2], refs[2:-1], refs[-1]
    rows, width = grad_ref.shape
    masks = side_masks()
    lane = iota((LANES, LANES), 1)
    ones = jnp.where(lane // HALF == iota((LANES, LANES), 0) // HALF, 1.0, 0.0).astype(BF)
    adder = doubled(ones)
    pairs = range(width // LANES)
    spots = [(pair, at) for pair in pairs for at in range(top - ready - 1, -1, -1)]
    items = []
    for pair, at in spots:
        keys, values = (load(top - ready + at, lane_pair(start, pair)) for start in (0, width))
        items.append((pair, load(at, lane_pair(0, pair)), keys, values, 2 ** (ready + at + 1)))
    sums = {}
    for (pair, at), (joined, both) in zip(spots, attend(factor_ref, items, masks)):
        weights_refs[at][:, block(pair, joined.shape[1])] = joined
        sums[pair, at] = both
    attended, inverses, products = [], [], []
    for pair in pairs:
        total = sums[pair, top - ready - 1]
        for at in range(top - ready - 2, -1, -1):
            total = sums[pair, at] + doubled(total)
        for _ in range(ready + 1):
            total = doubled(total)
        total = total + sums_ref[:, block(pair, 2 * LANES)]
        inverse = 1.0 / total[:, LANES:]
        ratio = total[:, :LANES] * inverse
        attended.append(ratio.astype(BF))
        inverses.append(inverse)
        products.append(back_ref[:, lane_pair(0, pair)].astype(F32) * ratio)
    weight_ref[...] = dot(stack(attended, 1), back_ref[:, width:], TN)
    for pair in pairs:
        high = products[pair].astype(BF)
        low = (products[pair] - high.astype(F32)).astype(BF)
        grad_ref[:, lane_pair(0, pair)] = back_ref[:, lane_pair(0, pair)].astype(F32) * inverses[pair]
        slope_ref[:, lane_pair(0, pair)] = -dot(stack([high, low], 1), adder) * inverses[pair]
    own_rows = width // parts
    for entry, offset, count, target, start in pieces:
        shift = offset if isinstance(offset, int) else offset(place_ref)
        first = pl.multiple_of(place_ref[entry] * own_rows + shift, math.gcd(own_rows, count))
        out_refs[target][start : start + count, :] = weight_ref[pl.ds(first, count), :].astype(BF)


def grads_kernel(grad_places, load, grad_ref, slope_ref, *out_refs):
    rows, width = grad_ref.shape
    grad_rows = [grad_ref[:, lane_pair(0, pair)] for pair in range(width // LANES)]
    denom_rows = [slope_ref[:, lane_pair(0, pair)] for pair in range(width // LANES)]
    for height, (target, start) in enumerate(grad_places):
        if height:
            grad_rows = [halves_sum(value) for value in grad_rows]
            denom_rows = [halves_sum(value) for value in denom_rows]
        span = slice(start, start + (rows >> height))
        for pair, value in enumerate(grad_rows):
            out_refs[target][span, lane_pair(0, pair)] = value.astype(BF)
        out_refs[target][span, width : width + LANES] = denom_lanes(denom_rows)
        if height:
            out_refs[target][span, width + LANES :] = load(height - 1, slice(0, width))


def query_slopes(joined, grad, denom, values, pair, height, masks):
    rows, columns = grad.shape[0], values.shape[0]
    left = stack([stack([grad * mask, denom * slot], 1) for mask, slot in zip(masks, slot_masks(pair))], 0)
    right = stack([values, jnp.full((columns, LANES), float(2**height), BF)], 1)
    product = dot(left, right, NT)
    return [
        (joined[:, side * columns : (side + 1) * columns].astype(F32) * product[side * rows : (side + 1) * rows])
        .astype(BF)
        for side in (0, 1)
    ]


def near_kernel(load, factor_ref, x_ref, gh_ref, weights_ref, query_ref, key_ref, value_ref):
    rows, width = query_ref.shape
    heads = width // HALF
    masks = side_masks()
    pairs = range(width // LANES)
    slopes = []
    for pair in pairs:
        values = x_ref[:rows, lane_pair(2 * width, pair)]
        joined = weights_ref[:, block(pair, 2 * rows)]
        grad = gh_ref[:, lane_pair(0, pair)]
        slopes.append(query_slopes(joined, grad, gh_ref[:, width:], values, pair, 0, masks))
    for pair in pairs:
        factor = side_factor(factor_ref, heads, pair)
        keys = x_ref[:rows, lane_pair(width, pair)]
        query_ref[:, lane_pair(0, pair)] = dot(stack(slopes[pair], 1), masked_stack(keys, masks)) * factor
    for pair in pairs:
        joined = weights_ref[:, block(pair, 2 * rows)]
        weights = stack([joined[:, :rows], joined[:, rows:]], 0)
        grad = gh_ref[:, lane_pair(0, pair)]
        value_ref[:, lane_pair(0, pair)] = dot(weights, masked_stack(grad, masks), TN)
    for pair in pairs:
        factor = side_factor(factor_ref, heads, pair)
        queries = x_ref[:rows, lane_pair(0, pair)]
        key_ref[:, lane_pair(0, pair)] = dot(stack(slopes[pair], 0), masked_stack(queries, masks), TN) * factor


def far_kernel(top, load, factor_ref, base_ref, *refs):
    weights_refs, out_ref = refs[:top], refs[top]
    rows, width = out_ref.shape
    heads = width // HALF
    masks = side_masks()
    pairs = range(width // LANES)
    slopes = {}
    for pair in pairs:
        for height in range(top, 0, -1):
            grad = load(height - 1, lane_pair(0, pair))
            denom = load(height - 1, slice(width, width + LANES))
            values = load(top + height - 1, lane_pair(width, pair))
            joined = weights_refs[height - 1][:, block(pair, 2 * values.shape[0])]
            slopes[pair, height] = query_slopes(joined, grad, denom, values, pair, height, masks)
    pieces = {}
    for pair, height in slopes:
        keys = load(top + height - 1, lane_pair(0, pair))
        pieces[pair, height] = dot(stack(slopes[pair, height], 1), masked_stack(keys, masks))
    results = []
    for pair in pairs:
        total = pieces[pair, top]
        for height in range(top - 1, 0, -1):
            total = pieces[pair, height] + 0.5 * doubled(total)
        total = total * side_factor(factor_ref, heads, pair)
        total = base_ref[:, lane_pair(0, pair)] + 0.5 * doubled(total)
        results.append(total.astype(BF))
    out_ref[...] = dot(order_matrix(rows, top, True), stack(results, 1)).astype(BF)


def key_kernel(top, first, last, load, factor_ref, base_key_ref, base_value_ref, key_out_ref, value_out_ref):
    rows, width = key_out_ref.shape
    heads = width // HALF
    masks = side_masks()
    levels = last - first + 1
    pairs = range(width // LANES)
    spots = [(pair, at) for pair in pairs for at in range(levels - 1, -1, -1)]
    weights, slopes, key_pieces, value_pieces = {}, {}, {}, {}
    for pair, at in spots:
        keys = load(at, lane_pair(width, pair))
        queries = load(levels + at, lane_pair(width + LANES, pair))
        weights[pair, at] = both_weights(factor_ref, pair, keys, queries, masks)
    for pair, at in spots:
        values = load(at, lane_pair(2 * width, pair))
        grad = load(levels + at, lane_pair(0, pair))
        denom = load(levels + at, slice(width, width + LANES))
        count = values.shape[0]
        left = stack(
            [
                stack([values * mask, jnp.broadcast_to(slot * float(2 ** (first + at)), (count, LANES))], 1)
                for mask, slot in zip(masks, slot_masks(pair))
            ],
            0,
        )
        product = dot(left, stack([grad, denom], 1), NT)
        slopes[pair, at] = [
            (weight * product[side * count : (side + 1) * count]).astype(BF)
            for side, weight in enumerate(weights[pair, at])
        ]
    for pair, at in spots:
        grad = load(levels + at, lane_pair(0, pair))
        rounded = stack([weight.astype(BF) for weight in weights[pair, at]], 1)
        value_pieces[pair, at] = dot(rounded, masked_stack(grad, masks))
        queries = load(levels + at, lane_pair(width + LANES, pair))
        key_pieces[pair, at] = dot(stack(slopes[pair, at], 1), masked_stack(queries, masks))
    key_results, value_results = [], []
    for pair in pairs:
        key_total, value_total = key_pieces[pair, levels - 1], value_pieces[pair, levels - 1]
        for at in range(levels - 2, -1, -1):
            key_total = key_pieces[pair, at] + 0.5 * doubled(key_total)
            value_total = value_pieces[pair, at] + doubled(value_total)
        key_total = key_total * side_factor(factor_ref, heads, pair)
        for _ in range(first):
            key_total, value_total = 0.5 * doubled(key_total), doubled(value_total)
        key_results.append(base_key_ref[:, lane_pair(0, pair)] + key_total)
        value_results.append(base_value_ref[:, lane_pair(0, pair)] + value_total)
    key_total, value_total = stack(key_results, 1), stack(value_results, 1)
    if last == top:
        back = order_matrix(rows, top, True)
        key_total, value_total = dot(back, key_total.astype(BF)), dot(back, value_total.astype(BF))
    key_out_ref[...] = key_total.astype(key_out_ref.dtype)
    value_out_ref[...] = value_total.astype(value_out_ref.dtype)


def place_kernel(spots, load, *refs):
    for target, start, groups in spots:
        total = None
        for group in groups:
            value = load(group, slice(None))
            if len(groups) > 1 or refs[target].dtype == F32:
                value = value.astype(F32)
            total = value if total is None else total + value
        refs[target][start : start + total.shape[0], :] = total.astype(refs[target].dtype)


def flush_kernel(load, *refs):
    count = (len(refs) - 1) // 2
    copies = [
        pltpu.make_async_copy(refs[at], refs[count + at], refs[-1].at[at]) for at in range(count)
    ]
    for copy in copies:
        copy.start()
    for copy in copies:
        copy.wait()


def flush(*arrays):
    return call(
        flush_kernel,
        "flush",
        [(array.shape, array.dtype) for array in arrays],
        arrays,
        out_specs=[HBM] * len(arrays),
        scratch=[pltpu.SemaphoreType.DMA((len(arrays),))],
    )


def placed(name, shapes, spots, flops=SMALL):
    views, listed = [], []
    for target, start, parts in spots:
        listed.append((target, start, range(len(views), len(views) + len(parts))))
        views += [[part] for part in parts]
    return call(functools.partial(place_kernel, listed), name, shapes, [], views=views, flops=flops)


def total_kernel(load, core_ref, own_ref, partner_ref, *refs):
    half = own_ref.shape[0] // 3
    base_ref = refs[0] if refs[0].shape[0] == 2 * half and len(refs) == 3 and refs[1].dtype == F32 else None
    out_refs = refs[:-1] if base_ref is None else refs[1:-1]
    sum_ref = refs[-1]
    total = own_ref[: 2 * half, :].astype(F32) + partner_ref[: 2 * half, :].astype(F32)
    if base_ref is not None:
        total = total + base_ref[...].astype(F32)
    sum_ref[...] = total
    for ref, core in ((own_ref, core_ref[0]), (partner_ref, 1 - core_ref[0])):
        span = pl.ds(pl.multiple_of(core * half, half), half)
        sum_ref[span, :] = sum_ref[span, :] + ref[2 * half :, :].astype(F32)
    out_refs[0][...] = sum_ref[...].astype(out_refs[0].dtype)
    if len(out_refs) > 1:
        span = pl.ds(pl.multiple_of(core_ref[0] * half, half), half)
        out_refs[1][...] = sum_ref[span, :].astype(BF)


def chip_total(name, core, arrays, half, kind):
    width = arrays[0].shape[1]
    shapes = [((2 * half, width), kind)] + [((half, width), BF)] * (kind == BF)
    return call(
        total_kernel,
        name,
        shapes,
        arrays,
        scalars=[core.reshape(1)],
        flops=LARGE,
        scratch=[pltpu.VMEM((2 * half, width), F32)],
    )


def traded(value, mask):
    return lax.ppermute(value, SEQ, [(source, source ^ mask) for source in range(lax.axis_size(SEQ))])


def split_traded(value, first, second):
    return lax.ppermute(
        value,
        SEQ,
        [(source, source ^ (2 * (second if source % 2 else first))) for source in range(lax.axis_size(SEQ))],
    )


def layer_traded(value, first, second):
    axes = ("dp", *SEQ)
    count = lax.axis_size(SEQ)
    pairs = []
    for source in range(lax.axis_size(axes)):
        layer, spot = divmod(source, count)
        pairs.append((source, (layer ^ (second if spot % 2 else first)) * count + spot))
    return lax.ppermute(value, axes, pairs)


def from_siblings(levels, top):
    arrived = {}
    for offset in range(1, 2**top):
        height = offset.bit_length()
        if offset == 1:
            arrived[1] = traded(levels[0], 1)
        elif offset % 2 == 0:
            arrived[offset] = traded(levels[height - 1], offset)
        else:
            arrived[offset] = traded(arrived[offset - 1], 1)
    grouped = []
    for height in range(1, top + 1):
        parts = [arrived[offset] for offset in range(2 ** (height - 1), 2**height)]
        if parts[0].shape[0] < 16:
            parts = [jnp.concatenate(parts, axis=0)]
        grouped.append([View(part) for part in parts])
    return grouped


def shards(queries, key_rows, value_rows, head_scale, out_weight, cotangent):
    rows, width = queries.shape[1:]
    heads = head_scale.shape[0]
    top = lax.axis_size(SEQ).bit_length() - 1
    parts = lax.axis_size("dp")
    assert width == HALF * heads and width % LANES == 0 and width <= 4 * LANES
    paired = top == 3 and parts == 4 and rows == 256
    whole = (rows, width)
    wide = width + LANES
    sizes = [rows >> height for height in range(top + 1)]
    starts = [0]
    for size in sizes:
        starts.append(starts[-1] + max(size, 16))
    if paired:
        places, messages = [(0, 0), (1, 0), (0, sizes[1])], [sizes[1] + sizes[3], sizes[2]]
    else:
        places, messages = [(height, 0) for height in range(top)], sizes[1:]
    factors, own_rows_all, *levels = call(
        functools.partial(pool_kernel, top, starts, places),
        "pool",
        [((factor_rows(heads), LANES), F32), ((starts[-1], 3 * width), BF)]
        + [((count, 2 * width), BF) for count in messages],
        [
            pltpu.with_memory_space_constraint(value, pltpu.HBM)
            for value in (queries[0], key_rows[0], value_rows[0], head_scale)
        ],
        specs=[HBM] * 4,
        scratch=[pltpu.VMEM(whole, BF)] * 3 + [pltpu.SMEM((heads,), F32), pltpu.SemaphoreType.DMA((4,))],
    )
    own = [[View(own_rows_all, starts[height], sizes[height])] for height in range(1, top + 1)]
    sums, base_weights, back = call(
        functools.partial(base_kernel, top),
        "base",
        [((rows, 2 * width), F32), ((rows, heads * rows), BF), ((rows, 2 * width), BF)],
        [factors, own_rows_all]
        + [pltpu.with_memory_space_constraint(value, pltpu.HBM) for value in (cotangent[0], out_weight)],
        specs=[VMEM, VMEM, HBM, HBM],
        scratch=[pltpu.VMEM(whole, BF), pltpu.VMEM((width, width), BF), pltpu.SemaphoreType.DMA((2,))],
        flops=100000000,
    )

    def attend_level(height, views, sums):
        return call(
            functools.partial(level_kernel, height),
            "level",
            [((sizes[height], heads * rows // 2), BF), ((rows, 2 * width), F32)],
            [factors, sums],
            views=[own[height - 1], views],
            flops=100000000//4,
        )

    if paired:
        within = traded(levels[0], 1)
        across = traded(levels[1], 2)
        (third,) = placed(
            "third_rows",
            [((2 * sizes[3], 2 * width), BF)],
            [(0, 0, [View(levels[0], sizes[1])]), (0, sizes[3], [View(within, sizes[1])])],
        )
        split = split_traded(third, 2, 3)
        level_weights = []
        if READY > 0:
            weights, sums = attend_level(1, [View(within, 0, sizes[1])], sums)
            level_weights.append(weights)
        across, sums = lax.optimization_barrier((across, sums))
        across_too = traded(across, 1)
        split_too = traded(split, 1)
        if READY > 1:
            weights, sums = attend_level(2, [View(across), View(across_too)], sums)
            level_weights.append(weights)
            split_too, sums = lax.optimization_barrier((split_too, sums))
        siblings = [[View(within, 0, sizes[1])], [View(across), View(across_too)], [View(split), View(split_too)]]
    else:
        siblings = from_siblings(levels, top)
        level_weights = []
    ready = len(level_weights)
    own_rows = width // parts
    half = own_rows // 2
    layer = lax.axis_index("dp").astype(jnp.int32)
    if paired:
        core = lax.axis_index(SEQ).astype(jnp.int32) % 2
        place = jnp.stack([layer, layer ^ (1 + 2 * core), layer ^ (3 - 2 * core), layer ^ 2, core * half])
        grad_places = [(0, 0), (1, 0), (2, 0), (1, sizes[1])]
        grad_shapes = [(rows, wide), (sizes[1] + sizes[3], wide + width), (sizes[2], wide + width)]
        pieces = [
            (0, 0, own_rows, 0, 0),
            (1, 0, own_rows, 1, 0),
            (3, lambda ref: ref[4], half, 1, own_rows),
            (2, 0, own_rows, 2, 0),
            (3, lambda ref: half - ref[4], half, 2, own_rows),
        ]
        shapes = [(own_rows, width), (own_rows + half, width), (own_rows + half, width)]
    else:
        place = (layer + jnp.arange(parts, dtype=jnp.int32)) % parts
        grad_places = [(height, 0) for height in range(top + 1)]
        pieces = [(step, 0, own_rows, step, 0) for step in range(parts)]
        grad_shapes = [(rows, wide)] + [(size, wide + width) for size in sizes[1:]]
        shapes = [(own_rows, width)] * parts
    outs = call(
        functools.partial(forward_kernel, top, ready, parts, pieces),
        "forward",
        [((size, heads * rows // 2), BF) for size in sizes[ready + 1 :]]
        + [(whole, F32), (whole, F32)]
        + [(shape, BF) for shape in shapes],
        [factors, sums, back],
        views=own[ready:] + siblings[ready:] + siblings[:ready],
        scalars=[place],
        scratch=[pltpu.VMEM((width, width), F32)],
    )
    level_weights += outs[: top - ready]
    outs = outs[top - ready :]
    (grad_rows, denom_rows), pieces = outs[:2], outs[2:]
    outs = call(
        functools.partial(grads_kernel, grad_places),
        "grads",
        [(shape, BF) for shape in grad_shapes],
        [grad_rows, denom_rows],
        views=own,
        flops=100000000,
    )

    def own_grads(arrays):
        return [
            [View(arrays[target], start, sizes[height])] for height, (target, start) in enumerate(grad_places) if height
        ]

    near_query, near_key, near_value = call(
        near_kernel,
        "near",
        [(whole, F32)] * 3,
        [factors, own_rows_all, outs[0], base_weights],
        flops=1600000000,
    )
    (query_grad,) = call(
        functools.partial(far_kernel, top),
        "far",
        [(whole, BF)],
        [factors, near_query, *level_weights],
        views=own_grads(outs) + siblings,
        flops=100000000,
    )

    def key_call(first, last, sums, sibling_grads, kind):
        return call(
            functools.partial(key_kernel, top, first, last),
            "key",
            [(whole, kind), (whole, kind)],
            [factors, *sums],
            views=own[first - 1 : last] + sibling_grads,
            flops=100000000,
        )

    if paired:
        near, far = outs[1:3]
        mine, send, theirs = pieces
        theirs_in = traded(theirs, 1)
        send_one, send_half = placed(
            "layer_rows",
            [((own_rows, width), BF), ((half, width), BF)],
            [
                (0, 0, [View(send, 0, own_rows), View(theirs_in, 0, own_rows)]),
                (1, 0, [View(send, own_rows), View(theirs_in, own_rows)]),
            ],
            flops=LARGE,
        )
        near_in = traded(near, 1)
        far_in = traded(far, 2)
        layer_one = layer_traded(send_one, 1, 3)
        layer_half = layer_traded(send_half, 2, 2)
        (third,) = placed(
            "third_grads",
            [((2 * sizes[3], wide + width), BF)],
            [(0, 0, [View(near, sizes[1])]), (0, sizes[3], [View(near_in, sizes[1])])],
        )
        third_in = split_traded(third, 2, 3)
        layer_one, layer_half, near_key = lax.optimization_barrier((layer_one, layer_half, near_key))
        (joint,) = placed(
            "layer_sum",
            [((own_rows + half, width), BF)],
            [(0, 0, [View(mine), View(layer_one)]), (0, own_rows, [View(layer_half)])],
            flops=LARGE,
        )
        joint_in = traded(joint, 1)
        far_in, near_key = lax.optimization_barrier((far_in, near_key))
        far_too = traded(far_in, 1)
        near_sums = key_call(1, 1, (near_key, near_value), [[View(near_in, 0, sizes[1])]], F32)
        joint_in, near_sums = lax.optimization_barrier((joint_in, tuple(near_sums)))
        weight, weight_half = chip_total("layer_total", core, [joint, joint_in], half, BF)
        third_in, _ = lax.optimization_barrier((third_in, weight))
        third_too = traded(third_in, 1)
        sibling_grads = [[View(far_in), View(far_too)], [View(third_in), View(third_too)]]
        plane_one = split_traded(weight, 1, 3)
        plane_half = traded(weight_half, 4)
        key_grad, value_grad = key_call(2, top, near_sums, sibling_grads, BF)
        plane_one, key_grad, query_grad = lax.optimization_barrier((plane_one, key_grad, query_grad))
        (joint,) = placed(
            "plane_rows",
            [((own_rows + half, width), BF)],
            [(0, 0, [View(plane_one)]), (0, own_rows, [View(plane_half)])],
            flops=LARGE,
        )
        joint_in = traded(joint, 1)
        query_grad, key_grad, value_grad = flush(query_grad, key_grad, value_grad)
        joint_in, key_grad = lax.optimization_barrier((joint_in, key_grad))
        (weight,) = chip_total("weight_out", core, [joint, joint_in, weight], half, F32)
    else:
        weight = pieces[0].astype(F32)
        for step in range(1, parts):
            weight = weight + lax.ppermute(
                pieces[step], "dp", [(source, (source + step) % parts) for source in range(parts)]
            ).astype(F32)
        sibling_grads = from_siblings(outs[1 : top + 1], top)
        bit = 1
        while bit < top:
            weight = weight.astype(BF)
            group = [weight] + [traded(weight, mask << bit) for mask in range(1, 2 ** min(2, top - bit))]
            weight = sum(value.astype(F32) for value in group)
            bit += 2
        weight = weight.astype(BF)
        weight = weight.astype(F32) + traded(weight, 1).astype(F32)
        key_grad, value_grad = key_call(1, top, (near_key, near_value), sibling_grads, BF)
    return query_grad[None], key_grad[None], value_grad[None], weight


def solution(mesh):
    spread = P("dp", SEQ, None)
    return jax.shard_map(
        shards,
        mesh=mesh,
        in_specs=(spread, spread, spread, P(), P(), spread),
        out_specs=(spread, spread, spread, P("dp", None)),
        check_vma=False,
    )
```

```python
import functools
import math

import jax
import jax.numpy as jnp
from jax import lax
from jax.experimental import pallas as pl
from jax.experimental.pallas import tpu as pltpu
from jax.sharding import PartitionSpec as P

BF = jnp.bfloat16
F32 = jnp.float32
SEQ = ("seqhi", "seqlo")
LANES = 128
HALF = 64
READY = 2
SMALL, BYTES, LARGE = 1, 10000, 1
LOG2E = math.log2(math.e)
NN = (((1,), (0,)), ((), ()))
NT = (((1,), (1,)), ((), ()))
TN = (((0,), (0,)), ((), ()))


def dot(left, right, dims=NN):
    return lax.dot_general(left, right, dims, preferred_element_type=F32)


def iota(shape, dim):
    return lax.broadcasted_iota(jnp.int32, shape, dim)


def order_matrix(rows, top, inverse=False):
    source = iota((rows, rows), 0 if inverse else 1)
    place = source >> top
    for bit in range(top):
        place = place + ((source >> bit) & 1) * (rows >> (bit + 1))
    return jnp.where(place == iota((rows, rows), 1 if inverse else 0), 1.0, 0.0).astype(BF)


def side_masks():
    lane = iota((1, LANES), 1)
    low = jnp.where(lane < HALF, 1.0, 0.0)
    return low.astype(BF), (1.0 - low).astype(BF)


def factor_rows(heads):
    return -(-(heads + heads // 2) // 8) * 8


def fill_factors(scale_ref, factor_ref):
    heads = scale_ref.shape[0]
    lane = iota((1, LANES), 1)
    for head in range(heads):
        factor_ref[head : head + 1, :] = jnp.full((1, LANES), scale_ref[head] * (HALF**-0.5 * LOG2E), F32)
    for pair in range(heads // 2):
        both = jnp.where(lane < HALF, scale_ref[2 * pair], scale_ref[2 * pair + 1]) * (HALF**-0.5)
        factor_ref[heads + pair : heads + pair + 1, :] = both


def exponent(factor_ref, head, columns):
    return stack([factor_ref[head : head + 1, :]] * (columns // LANES), 1)


def side_factor(factor_ref, heads, pair):
    return factor_ref[heads + pair : heads + pair + 1, :]


def stack(parts, axis):
    return parts[0] if len(parts) == 1 else jnp.concatenate(parts, axis=axis)


def doubled(value):
    return jnp.concatenate([value, value], axis=0)


def halves_sum(value):
    half = value.shape[0] // 2
    return value[:half] + value[half:]


def lane_pair(offset, pair):
    return slice(offset + LANES * pair, offset + LANES * (pair + 1))


def slot_masks(pair):
    lane = iota((1, LANES), 1)
    masks = []
    for side in (0, 1):
        slot = lane - side * HALF
        hit = (slot == 16 * pair) | (slot == 16 * pair + 8)
        masks.append(jnp.where(hit, 1.0, 0.0).astype(BF))
    return masks


def denom_lanes(denoms):
    lane = iota((1, LANES), 1)
    slot = (lane % HALF) // 8
    packed = jnp.zeros(denoms[0].shape, F32)
    for pair, value in enumerate(denoms):
        high = value.astype(BF).astype(F32)
        packed = jnp.where(slot == 2 * pair, high, packed)
        packed = jnp.where(slot == 2 * pair + 1, value - high, packed)
    return packed.astype(BF)


class View:
    def __init__(self, array, start=0, rows=None):
        self.array = array
        self.start = start
        self.rows = array.shape[0] - start if rows is None else rows


VMEM = pl.BlockSpec(memory_space=pltpu.VMEM)
SMEM = pl.BlockSpec(memory_space=pltpu.SMEM)
HBM = pl.BlockSpec(memory_space=pltpu.HBM)


def call(kernel, name, shapes, arrays, views=(), scalars=(), flops=SMALL, scratch=(), specs=None, out_specs=None):
    unique, where = [], []
    for group in views:
        places = []
        for view in group:
            spot = next((at for at, array in enumerate(unique) if array is view.array), None)
            if spot is None:
                spot = len(unique)
                unique.append(view.array)
            places.append((spot, view.start, view.rows))
        where.append(places)

    def body(*refs):
        scalar_refs, refs = refs[: len(scalars)], refs[len(scalars) :]
        array_refs, refs = refs[: len(arrays)], refs[len(arrays) :]
        view_refs, refs = refs[: len(unique)], refs[len(unique) :]

        def load(group, columns):
            return stack(
                [view_refs[spot][start : start + rows, columns] for spot, start, rows in where[group]], 0
            )

        kernel(load, *scalar_refs, *array_refs, *refs)

    return pl.pallas_call(
        body,
        out_shape=[jax.ShapeDtypeStruct(shape, kind) for shape, kind in shapes],
        in_specs=[SMEM] * len(scalars) + (specs or [VMEM] * len(arrays)) + [VMEM] * len(unique),
        out_specs=out_specs or [VMEM] * len(shapes),
        scratch_shapes=list(scratch),
        compiler_params=pltpu.CompilerParams(vmem_limit_bytes=16 * 2**20),
        cost_estimate=pl.CostEstimate(flops=flops, transcendentals=0, bytes_accessed=BYTES),
        name=name,
    )(*scalars, *arrays, *unique)


def pool_kernel(top, starts, places, load, q_hbm, k_hbm, v_hbm, scale_hbm, factor_ref, rows_ref, *refs):
    level_refs, (q_ref, k_ref, v_ref, scale_ref, sems) = refs[:-5], refs[-5:]
    copies = [
        pltpu.make_async_copy(source, target, sems.at[index])
        for index, (source, target) in enumerate(
            ((q_hbm, q_ref), (k_hbm, k_ref), (v_hbm, v_ref), (scale_hbm, scale_ref))
        )
    ]
    for which in (1, 2, 0, 3):
        copies[which].start()
    rows, width = q_ref.shape
    order = order_matrix(rows, top)
    current = {}
    for which, ref in ((1, k_ref), (2, v_ref), (0, q_ref)):
        copies[which].wait()
        current[which] = dot(order, ref[...])
    for height in range(top + 1):
        for which in (1, 2, 0):
            columns = slice(which * width, (which + 1) * width)
            if height:
                total = halves_sum(current[which])
                rounded = (total if which == 2 else 0.5 * total).astype(BF)
            else:
                rounded = current[which].astype(BF)
            rows_ref[starts[height] : starts[height] + rounded.shape[0], columns] = rounded
            if height and which:
                target, start = places[height - 1]
                span = slice(start, start + rounded.shape[0])
                level_refs[target][span, (which - 1) * width : which * width] = rounded
            current[which] = rounded.astype(F32)
    copies[3].wait()
    fill_factors(scale_ref, factor_ref)


def masked_stack(value, masks):
    return stack([value * mask for mask in masks], 0)


def both_weights(factor_ref, pair, first, second, masks):
    rows = first.shape[0]
    logits = dot(masked_stack(first, masks), second, NT)
    columns = second.shape[0]
    return [
        jnp.exp2(logits[side * rows : (side + 1) * rows] * exponent(factor_ref, 2 * pair + side, columns))
        for side in (0, 1)
    ]


def attend(factor_ref, items, masks):
    weights = [
        stack([weight.astype(BF) for weight in both_weights(factor_ref, pair, queries, keys, masks)], 1)
        for pair, queries, keys, _, _ in items
    ]
    results = []
    for joined, (_, _, _, values, amount) in zip(weights, items):
        count = jnp.full(values.shape, float(amount), BF)
        right = stack([stack([values * mask, count * mask], 1) for mask in masks], 0)
        results.append((joined, dot(joined, right)))
    return results


def block(pair, span):
    return slice(span * pair, span * (pair + 1))


def base_kernel(top, load, factor_ref, x_ref, cot_hbm, w_hbm, sums_ref, weights_ref, back_ref, cot_ref, w_ref, sems):
    copies = [
        pltpu.make_async_copy(cot_hbm, cot_ref, sems.at[0]),
        pltpu.make_async_copy(w_hbm, w_ref, sems.at[1]),
    ]
    for copy in copies:
        copy.start()
    rows, width = cot_ref.shape
    masks = side_masks()
    items = [
        (pair, *(x_ref[:rows, lane_pair(width * which, pair)] for which in range(3)), 1)
        for pair in range(width // LANES)
    ]
    for pair, (joined, both) in enumerate(attend(factor_ref, items, masks)):
        sums_ref[:, block(pair, 2 * LANES)] = both
        weights_ref[:, block(pair, 2 * rows)] = joined
    order = order_matrix(rows, top)
    copies[0].wait()
    cotan = dot(order, cot_ref[...]).astype(BF)
    copies[1].wait()
    back_ref[:, width:] = cotan
    back_ref[:, :width] = dot(cotan, w_ref[...], NT).astype(BF)


def level_kernel(height, load, factor_ref, sums_ref, weights_ref, total_ref):
    width = sums_ref.shape[1] // 2
    masks = side_masks()
    items = [
        (pair, load(0, lane_pair(0, pair)), *(load(1, lane_pair(start, pair)) for start in (0, width)), 2**height)
        for pair in range(width // LANES)
    ]
    for pair, (joined, both) in enumerate(attend(factor_ref, items, masks)):
        weights_ref[:, block(pair, joined.shape[1])] = joined
        for _ in range(height):
            both = doubled(both)
        total_ref[:, block(pair, 2 * LANES)] = sums_ref[:, block(pair, 2 * LANES)] + both


def forward_kernel(
    top, ready, parts, pieces, load, place_ref, factor_ref, sums_ref, back_ref, *refs
):
    weights_refs, refs = refs[: top - ready], refs[top - ready :]
    (grad_ref, slope_ref), out_refs, weight_ref = refs[:2], refs[2:-1], refs[-1]
    rows, width = grad_ref.shape
    masks = side_masks()
    lane = iota((LANES, LANES), 1)
    ones = jnp.where(lane // HALF == iota((LANES, LANES), 0) // HALF, 1.0, 0.0).astype(BF)
    adder = doubled(ones)
    pairs = range(width // LANES)
    spots = [(pair, at) for pair in pairs for at in range(top - ready - 1, -1, -1)]
    items = []
    for pair, at in spots:
        keys, values = (load(top - ready + at, lane_pair(start, pair)) for start in (0, width))
        items.append((pair, load(at, lane_pair(0, pair)), keys, values, 2 ** (ready + at + 1)))
    sums = {}
    for (pair, at), (joined, both) in zip(spots, attend(factor_ref, items, masks)):
        weights_refs[at][:, block(pair, joined.shape[1])] = joined
        sums[pair, at] = both
    attended, inverses, products = [], [], []
    for pair in pairs:
        total = sums[pair, top - ready - 1]
        for at in range(top - ready - 2, -1, -1):
            total = sums[pair, at] + doubled(total)
        for _ in range(ready + 1):
            total = doubled(total)
        total = total + sums_ref[:, block(pair, 2 * LANES)]
        inverse = 1.0 / total[:, LANES:]
        ratio = total[:, :LANES] * inverse
        attended.append(ratio.astype(BF))
        inverses.append(inverse)
        products.append(back_ref[:, lane_pair(0, pair)].astype(F32) * ratio)
    weight_ref[...] = dot(stack(attended, 1), back_ref[:, width:], TN)
    for pair in pairs:
        high = products[pair].astype(BF)
        low = (products[pair] - high.astype(F32)).astype(BF)
        grad_ref[:, lane_pair(0, pair)] = back_ref[:, lane_pair(0, pair)].astype(F32) * inverses[pair]
        slope_ref[:, lane_pair(0, pair)] = -dot(stack([high, low], 1), adder) * inverses[pair]
    own_rows = width // parts
    for entry, offset, count, target, start in pieces:
        shift = offset if isinstance(offset, int) else offset(place_ref)
        first = pl.multiple_of(place_ref[entry] * own_rows + shift, math.gcd(own_rows, count))
        out_refs[target][start : start + count, :] = weight_ref[pl.ds(first, count), :].astype(BF)


def grads_kernel(grad_places, load, grad_ref, slope_ref, *out_refs):
    rows, width = grad_ref.shape
    grad_rows = [grad_ref[:, lane_pair(0, pair)] for pair in range(width // LANES)]
    denom_rows = [slope_ref[:, lane_pair(0, pair)] for pair in range(width // LANES)]
    for height, (target, start) in enumerate(grad_places):
        if height:
            grad_rows = [halves_sum(value) for value in grad_rows]
            denom_rows = [halves_sum(value) for value in denom_rows]
        span = slice(start, start + (rows >> height))
        for pair, value in enumerate(grad_rows):
            out_refs[target][span, lane_pair(0, pair)] = value.astype(BF)
        out_refs[target][span, width : width + LANES] = denom_lanes(denom_rows)
        if height:
            out_refs[target][span, width + LANES :] = load(height - 1, slice(0, width))


def query_slopes(joined, grad, denom, values, pair, height, masks):
    rows, columns = grad.shape[0], values.shape[0]
    left = stack([stack([grad * mask, denom * slot], 1) for mask, slot in zip(masks, slot_masks(pair))], 0)
    right = stack([values, jnp.full((columns, LANES), float(2**height), BF)], 1)
    product = dot(left, right, NT)
    return [
        (joined[:, side * columns : (side + 1) * columns].astype(F32) * product[side * rows : (side + 1) * rows])
        .astype(BF)
        for side in (0, 1)
    ]


def near_kernel(load, factor_ref, x_ref, gh_ref, weights_ref, query_ref, key_ref, value_ref):
    rows, width = query_ref.shape
    heads = width // HALF
    masks = side_masks()
    pairs = range(width // LANES)
    slopes = []
    for pair in pairs:
        values = x_ref[:rows, lane_pair(2 * width, pair)]
        joined = weights_ref[:, block(pair, 2 * rows)]
        grad = gh_ref[:, lane_pair(0, pair)]
        slopes.append(query_slopes(joined, grad, gh_ref[:, width:], values, pair, 0, masks))
    for pair in pairs:
        factor = side_factor(factor_ref, heads, pair)
        keys = x_ref[:rows, lane_pair(width, pair)]
        query_ref[:, lane_pair(0, pair)] = dot(stack(slopes[pair], 1), masked_stack(keys, masks)) * factor
    for pair in pairs:
        joined = weights_ref[:, block(pair, 2 * rows)]
        weights = stack([joined[:, :rows], joined[:, rows:]], 0)
        grad = gh_ref[:, lane_pair(0, pair)]
        value_ref[:, lane_pair(0, pair)] = dot(weights, masked_stack(grad, masks), TN)
    for pair in pairs:
        factor = side_factor(factor_ref, heads, pair)
        queries = x_ref[:rows, lane_pair(0, pair)]
        key_ref[:, lane_pair(0, pair)] = dot(stack(slopes[pair], 0), masked_stack(queries, masks), TN) * factor


def far_kernel(top, load, factor_ref, base_ref, *refs):
    weights_refs, out_ref = refs[:top], refs[top]
    rows, width = out_ref.shape
    heads = width // HALF
    masks = side_masks()
    pairs = range(width // LANES)
    slopes = {}
    for pair in pairs:
        for height in range(top, 0, -1):
            grad = load(height - 1, lane_pair(0, pair))
            denom = load(height - 1, slice(width, width + LANES))
            values = load(top + height - 1, lane_pair(width, pair))
            joined = weights_refs[height - 1][:, block(pair, 2 * values.shape[0])]
            slopes[pair, height] = query_slopes(joined, grad, denom, values, pair, height, masks)
    pieces = {}
    for pair, height in slopes:
        keys = load(top + height - 1, lane_pair(0, pair))
        pieces[pair, height] = dot(stack(slopes[pair, height], 1), masked_stack(keys, masks))
    results = []
    for pair in pairs:
        total = pieces[pair, top]
        for height in range(top - 1, 0, -1):
            total = pieces[pair, height] + 0.5 * doubled(total)
        total = total * side_factor(factor_ref, heads, pair)
        total = base_ref[:, lane_pair(0, pair)] + 0.5 * doubled(total)
        results.append(total.astype(BF))
    out_ref[...] = dot(order_matrix(rows, top, True), stack(results, 1)).astype(BF)


def key_kernel(top, first, last, load, factor_ref, base_key_ref, base_value_ref, key_out_ref, value_out_ref):
    rows, width = key_out_ref.shape
    heads = width // HALF
    masks = side_masks()
    levels = last - first + 1
    pairs = range(width // LANES)
    spots = [(pair, at) for pair in pairs for at in range(levels - 1, -1, -1)]
    weights, slopes, key_pieces, value_pieces = {}, {}, {}, {}
    for pair, at in spots:
        keys = load(at, lane_pair(width, pair))
        queries = load(levels + at, lane_pair(width + LANES, pair))
        weights[pair, at] = both_weights(factor_ref, pair, keys, queries, masks)
    for pair, at in spots:
        values = load(at, lane_pair(2 * width, pair))
        grad = load(levels + at, lane_pair(0, pair))
        denom = load(levels + at, slice(width, width + LANES))
        count = values.shape[0]
        left = stack(
            [
                stack([values * mask, jnp.broadcast_to(slot * float(2 ** (first + at)), (count, LANES))], 1)
                for mask, slot in zip(masks, slot_masks(pair))
            ],
            0,
        )
        product = dot(left, stack([grad, denom], 1), NT)
        slopes[pair, at] = [
            (weight * product[side * count : (side + 1) * count]).astype(BF)
            for side, weight in enumerate(weights[pair, at])
        ]
    for pair, at in spots:
        grad = load(levels + at, lane_pair(0, pair))
        rounded = stack([weight.astype(BF) for weight in weights[pair, at]], 1)
        value_pieces[pair, at] = dot(rounded, masked_stack(grad, masks))
        queries = load(levels + at, lane_pair(width + LANES, pair))
        key_pieces[pair, at] = dot(stack(slopes[pair, at], 1), masked_stack(queries, masks))
    key_results, value_results = [], []
    for pair in pairs:
        key_total, value_total = key_pieces[pair, levels - 1], value_pieces[pair, levels - 1]
        for at in range(levels - 2, -1, -1):
            key_total = key_pieces[pair, at] + 0.5 * doubled(key_total)
            value_total = value_pieces[pair, at] + doubled(value_total)
        key_total = key_total * side_factor(factor_ref, heads, pair)
        for _ in range(first):
            key_total, value_total = 0.5 * doubled(key_total), doubled(value_total)
        key_results.append(base_key_ref[:, lane_pair(0, pair)] + key_total)
        value_results.append(base_value_ref[:, lane_pair(0, pair)] + value_total)
    key_total, value_total = stack(key_results, 1), stack(value_results, 1)
    if last == top:
        back = order_matrix(rows, top, True)
        key_total, value_total = dot(back, key_total.astype(BF)), dot(back, value_total.astype(BF))
    key_out_ref[...] = key_total.astype(key_out_ref.dtype)
    value_out_ref[...] = value_total.astype(value_out_ref.dtype)


def place_kernel(spots, load, *refs):
    for target, start, groups in spots:
        total = None
        for group in groups:
            value = load(group, slice(None))
            if len(groups) > 1 or refs[target].dtype == F32:
                value = value.astype(F32)
            total = value if total is None else total + value
        refs[target][start : start + total.shape[0], :] = total.astype(refs[target].dtype)


def flush_kernel(load, *refs):
    count = (len(refs) - 1) // 2
    copies = [
        pltpu.make_async_copy(refs[at], refs[count + at], refs[-1].at[at]) for at in range(count)
    ]
    for copy in copies:
        copy.start()
    for copy in copies:
        copy.wait()


def flush(*arrays):
    return call(
        flush_kernel,
        "flush",
        [(array.shape, array.dtype) for array in arrays],
        arrays,
        out_specs=[HBM] * len(arrays),
        scratch=[pltpu.SemaphoreType.DMA((len(arrays),))],
    )


def placed(name, shapes, spots, flops=SMALL):
    views, listed = [], []
    for target, start, parts in spots:
        listed.append((target, start, range(len(views), len(views) + len(parts))))
        views += [[part] for part in parts]
    return call(functools.partial(place_kernel, listed), name, shapes, [], views=views, flops=flops)


def total_kernel(load, core_ref, own_ref, partner_ref, *refs):
    half = own_ref.shape[0] // 3
    base_ref = refs[0] if refs[0].shape[0] == 2 * half and len(refs) == 3 and refs[1].dtype == F32 else None
    out_refs = refs[:-1] if base_ref is None else refs[1:-1]
    sum_ref = refs[-1]
    total = own_ref[: 2 * half, :].astype(F32) + partner_ref[: 2 * half, :].astype(F32)
    if base_ref is not None:
        total = total + base_ref[...].astype(F32)
    sum_ref[...] = total
    for ref, core in ((own_ref, core_ref[0]), (partner_ref, 1 - core_ref[0])):
        span = pl.ds(pl.multiple_of(core * half, half), half)
        sum_ref[span, :] = sum_ref[span, :] + ref[2 * half :, :].astype(F32)
    out_refs[0][...] = sum_ref[...].astype(out_refs[0].dtype)
    if len(out_refs) > 1:
        span = pl.ds(pl.multiple_of(core_ref[0] * half, half), half)
        out_refs[1][...] = sum_ref[span, :].astype(BF)


def chip_total(name, core, arrays, half, kind):
    width = arrays[0].shape[1]
    shapes = [((2 * half, width), kind)] + [((half, width), BF)] * (kind == BF)
    return call(
        total_kernel,
        name,
        shapes,
        arrays,
        scalars=[core.reshape(1)],
        flops=LARGE,
        scratch=[pltpu.VMEM((2 * half, width), F32)],
    )


def traded(value, mask):
    return lax.ppermute(value, SEQ, [(source, source ^ mask) for source in range(lax.axis_size(SEQ))])


def split_traded(value, first, second):
    return lax.ppermute(
        value,
        SEQ,
        [(source, source ^ (2 * (second if source % 2 else first))) for source in range(lax.axis_size(SEQ))],
    )


def layer_traded(value, first, second):
    axes = ("dp", *SEQ)
    count = lax.axis_size(SEQ)
    pairs = []
    for source in range(lax.axis_size(axes)):
        layer, spot = divmod(source, count)
        pairs.append((source, (layer ^ (second if spot % 2 else first)) * count + spot))
    return lax.ppermute(value, axes, pairs)


def from_siblings(levels, top):
    arrived = {}
    for offset in range(1, 2**top):
        height = offset.bit_length()
        if offset == 1:
            arrived[1] = traded(levels[0], 1)
        elif offset % 2 == 0:
            arrived[offset] = traded(levels[height - 1], offset)
        else:
            arrived[offset] = traded(arrived[offset - 1], 1)
    grouped = []
    for height in range(1, top + 1):
        parts = [arrived[offset] for offset in range(2 ** (height - 1), 2**height)]
        if parts[0].shape[0] < 16:
            parts = [jnp.concatenate(parts, axis=0)]
        grouped.append([View(part) for part in parts])
    return grouped


def shards(queries, key_rows, value_rows, head_scale, out_weight, cotangent):
    rows, width = queries.shape[1:]
    heads = head_scale.shape[0]
    top = lax.axis_size(SEQ).bit_length() - 1
    parts = lax.axis_size("dp")
    assert width == HALF * heads and width % LANES == 0 and width <= 4 * LANES
    paired = top == 3 and parts == 4 and rows == 256
    whole = (rows, width)
    wide = width + LANES
    sizes = [rows >> height for height in range(top + 1)]
    starts = [0]
    for size in sizes:
        starts.append(starts[-1] + max(size, 16))
    if paired:
        places, messages = [(0, 0), (1, 0), (0, sizes[1])], [sizes[1] + sizes[3], sizes[2]]
    else:
        places, messages = [(height, 0) for height in range(top)], sizes[1:]
    factors, own_rows_all, *levels = call(
        functools.partial(pool_kernel, top, starts, places),
        "pool",
        [((factor_rows(heads), LANES), F32), ((starts[-1], 3 * width), BF)]
        + [((count, 2 * width), BF) for count in messages],
        [
            pltpu.with_memory_space_constraint(value, pltpu.HBM)
            for value in (queries[0], key_rows[0], value_rows[0], head_scale)
        ],
        specs=[HBM] * 4,
        scratch=[pltpu.VMEM(whole, BF)] * 3 + [pltpu.SMEM((heads,), F32), pltpu.SemaphoreType.DMA((4,))],
    )
    own = [[View(own_rows_all, starts[height], sizes[height])] for height in range(1, top + 1)]
    sums, base_weights, back = call(
        functools.partial(base_kernel, top),
        "base",
        [((rows, 2 * width), F32), ((rows, heads * rows), BF), ((rows, 2 * width), BF)],
        [factors, own_rows_all]
        + [pltpu.with_memory_space_constraint(value, pltpu.HBM) for value in (cotangent[0], out_weight)],
        specs=[VMEM, VMEM, HBM, HBM],
        scratch=[pltpu.VMEM(whole, BF), pltpu.VMEM((width, width), BF), pltpu.SemaphoreType.DMA((2,))],
        flops=100000000,
    )

    def attend_level(height, views, sums):
        return call(
            functools.partial(level_kernel, height),
            "level",
            [((sizes[height], heads * rows // 2), BF), ((rows, 2 * width), F32)],
            [factors, sums],
            views=[own[height - 1], views],
            flops=100000000//4,
        )

    if paired:
        within = traded(levels[0], 1)
        across = traded(levels[1], 2)
        (third,) = placed(
            "third_rows",
            [((2 * sizes[3], 2 * width), BF)],
            [(0, 0, [View(levels[0], sizes[1])]), (0, sizes[3], [View(within, sizes[1])])],
        )
        split = split_traded(third, 2, 3)
        level_weights = []
        if READY > 0:
            weights, sums = attend_level(1, [View(within, 0, sizes[1])], sums)
            level_weights.append(weights)
        across, sums = lax.optimization_barrier((across, sums))
        across_too = traded(across, 1)
        split_too = traded(split, 1)
        if READY > 1:
            weights, sums = attend_level(2, [View(across), View(across_too)], sums)
            level_weights.append(weights)
            split_too, sums = lax.optimization_barrier((split_too, sums))
        siblings = [[View(within, 0, sizes[1])], [View(across), View(across_too)], [View(split), View(split_too)]]
    else:
        siblings = from_siblings(levels, top)
        level_weights = []
    ready = len(level_weights)
    own_rows = width // parts
    half = own_rows // 2
    layer = lax.axis_index("dp").astype(jnp.int32)
    if paired:
        core = lax.axis_index(SEQ).astype(jnp.int32) % 2
        place = jnp.stack([layer, layer ^ (1 + 2 * core), layer ^ (3 - 2 * core), layer ^ 2, core * half])
        grad_places = [(0, 0), (1, 0), (2, 0), (1, sizes[1])]
        grad_shapes = [(rows, wide), (sizes[1] + sizes[3], wide + width), (sizes[2], wide + width)]
        pieces = [
            (0, 0, own_rows, 0, 0),
            (1, 0, own_rows, 1, 0),
            (3, lambda ref: ref[4], half, 1, own_rows),
            (2, 0, own_rows, 2, 0),
            (3, lambda ref: half - ref[4], half, 2, own_rows),
        ]
        shapes = [(own_rows, width), (own_rows + half, width), (own_rows + half, width)]
    else:
        place = (layer + jnp.arange(parts, dtype=jnp.int32)) % parts
        grad_places = [(height, 0) for height in range(top + 1)]
        pieces = [(step, 0, own_rows, step, 0) for step in range(parts)]
        grad_shapes = [(rows, wide)] + [(size, wide + width) for size in sizes[1:]]
        shapes = [(own_rows, width)] * parts
    outs = call(
        functools.partial(forward_kernel, top, ready, parts, pieces),
        "forward",
        [((size, heads * rows // 2), BF) for size in sizes[ready + 1 :]]
        + [(whole, F32), (whole, F32)]
        + [(shape, BF) for shape in shapes],
        [factors, sums, back],
        views=own[ready:] + siblings[ready:] + siblings[:ready],
        scalars=[place],
        scratch=[pltpu.VMEM((width, width), F32)],
    )
    level_weights += outs[: top - ready]
    outs = outs[top - ready :]
    (grad_rows, denom_rows), pieces = outs[:2], outs[2:]
    outs = call(
        functools.partial(grads_kernel, grad_places),
        "grads",
        [(shape, BF) for shape in grad_shapes],
        [grad_rows, denom_rows],
        views=own,
        flops=100000000,
    )

    def own_grads(arrays):
        return [
            [View(arrays[target], start, sizes[height])] for height, (target, start) in enumerate(grad_places) if height
        ]

    near_query, near_key, near_value = call(
        near_kernel,
        "near",
        [(whole, F32)] * 3,
        [factors, own_rows_all, outs[0], base_weights],
        flops=1600000000,
    )
    (query_grad,) = call(
        functools.partial(far_kernel, top),
        "far",
        [(whole, BF)],
        [factors, near_query, *level_weights],
        views=own_grads(outs) + siblings,
        flops=100000000,
    )

    def key_call(first, last, sums, sibling_grads, kind):
        return call(
            functools.partial(key_kernel, top, first, last),
            "key",
            [(whole, kind), (whole, kind)],
            [factors, *sums],
            views=own[first - 1 : last] + sibling_grads,
            flops=100000000,
        )

    if paired:
        near, far = outs[1:3]
        mine, send, theirs = pieces
        theirs_in = traded(theirs, 1)
        send_one, send_half = placed(
            "layer_rows",
            [((own_rows, width), BF), ((half, width), BF)],
            [
                (0, 0, [View(send, 0, own_rows), View(theirs_in, 0, own_rows)]),
                (1, 0, [View(send, own_rows), View(theirs_in, own_rows)]),
            ],
            flops=LARGE,
        )
        near_in = traded(near, 1)
        far_in = traded(far, 2)
        layer_one = layer_traded(send_one, 1, 3)
        layer_half = layer_traded(send_half, 2, 2)
        (third,) = placed(
            "third_grads",
            [((2 * sizes[3], wide + width), BF)],
            [(0, 0, [View(near, sizes[1])]), (0, sizes[3], [View(near_in, sizes[1])])],
        )
        third_in = split_traded(third, 2, 3)
        layer_one, layer_half, near_key = lax.optimization_barrier((layer_one, layer_half, near_key))
        (joint,) = placed(
            "layer_sum",
            [((own_rows + half, width), BF)],
            [(0, 0, [View(mine), View(layer_one)]), (0, own_rows, [View(layer_half)])],
            flops=LARGE,
        )
        joint_in = traded(joint, 1)
        far_in, near_key = lax.optimization_barrier((far_in, near_key))
        far_too = traded(far_in, 1)
        near_sums = key_call(1, 1, (near_key, near_value), [[View(near_in, 0, sizes[1])]], F32)
        joint_in, near_sums = lax.optimization_barrier((joint_in, tuple(near_sums)))
        weight, weight_half = chip_total("layer_total", core, [joint, joint_in], half, BF)
        third_in, _ = lax.optimization_barrier((third_in, weight))
        third_too = traded(third_in, 1)
        sibling_grads = [[View(far_in), View(far_too)], [View(third_in), View(third_too)]]
        plane_one = split_traded(weight, 1, 3)
        plane_half = traded(weight_half, 4)
        key_grad, value_grad = key_call(2, top, near_sums, sibling_grads, BF)
        plane_one, key_grad, query_grad = lax.optimization_barrier((plane_one, key_grad, query_grad))
        (joint,) = placed(
            "plane_rows",
            [((own_rows + half, width), BF)],
            [(0, 0, [View(plane_one)]), (0, own_rows, [View(plane_half)])],
            flops=LARGE,
        )
        joint_in = traded(joint, 1)
        query_grad, key_grad, value_grad = flush(query_grad, key_grad, value_grad)
        joint_in, key_grad = lax.optimization_barrier((joint_in, key_grad))
        (weight,) = chip_total("weight_out", core, [joint, joint_in, weight], half, F32)
    else:
        weight = pieces[0].astype(F32)
        for step in range(1, parts):
            weight = weight + lax.ppermute(
                pieces[step], "dp", [(source, (source + step) % parts) for source in range(parts)]
            ).astype(F32)
        sibling_grads = from_siblings(outs[1 : top + 1], top)
        bit = 1
        while bit < top:
            weight = weight.astype(BF)
            group = [weight] + [traded(weight, mask << bit) for mask in range(1, 2 ** min(2, top - bit))]
            weight = sum(value.astype(F32) for value in group)
            bit += 2
        weight = weight.astype(BF)
        weight = weight.astype(F32) + traded(weight, 1).astype(F32)
        key_grad, value_grad = key_call(1, top, (near_key, near_value), sibling_grads, BF)
    return query_grad[None], key_grad[None], value_grad[None], weight


def solution(mesh):
    spread = P("dp", SEQ, None)
    return jax.shard_map(
        shards,
        mesh=mesh,
        in_specs=(spread, spread, spread, P(), P(), spread),
        out_specs=(spread, spread, spread, P("dp", None)),
        check_vma=False,
    )
```
